128 devices in a mesh: fsdp: 4 (over z), seq: 8 (over x, core), head: 4 (over y).
Axes of the slice: x: 4, y: 4, z: 4, core: 2. Of those that a mesh axis runs over, the one named last changes fastest.
Arguments:
- queries: bfloat16 [8192, 4096], P(('fsdp', 'seq'), 'head'), may hold values from -6 to 6
- span_k: bfloat16 [8192, 512], P(('fsdp', 'seq'), 'head'), may hold values from -6 to 6
- span_v: bfloat16 [8192, 512], P(('fsdp', 'seq'), 'head'), may hold values from -6 to 6
- cache_k: bfloat16 [2048, 128, 512], P(('fsdp', 'seq'), None, 'head'), may hold values from -6 to 6
- cache_v: bfloat16 [2048, 128, 512], P(('fsdp', 'seq'), None, 'head'), may hold values from -6 to 6
- block_slot: int32 [2048], replicated, may hold values from 0 to 2047, as said below
- pattern: int32 [64, 48], P(('fsdp', 'seq')), may hold values from 0 to 2047, as said below
- wo: bfloat16 [4096, 8192], P('head', 'fsdp'), may hold values from -6 to 6
Outputs:
- mixed: bfloat16 [8192, 8192], P(('fsdp', 'seq'))
The draws below stay inside these ranges and needn't reach their ends.
Inputs may be any that keep to these rules, and one draw needn't show every extreme that they name: `pattern`: each row lists 48 different blocks. Of the 96 entries in the rows of one index of fsdp and seq, all are different, at most 6 have a storage row block_slot between o * 64 and (o + 1) * 64 - 1 for any o, and exactly 6 do for some o. A permutation: block c is stored at row block_slot[c] of cache_k and cache_v.
All inputs are finite; a program needn't handle non-finite values.
Results may differ from the reference program's by a relative error of at most 0.0095.
Values may be sent and summed in bfloat16 or wider, within the bound.
A program may use at most 128 MiB of HBM per device.

```python
import jax
import jax.numpy as jnp
from jax import lax

D = 8192
HD = 128
KVH = 4
GROUP = 8
BLK = 128
NLIST = 48
QB_DEV = 2
CB_DEV = 64
QH = 32
SEQ_DEVS = 32
QBLOCKS = 64
TOKENS = 8192
CACHE_BLOCKS = 2048
CAP = 6
N_HEAD = 4


def draw_queries(key, part):
    shape = (TOKENS, QH * HD)
    values = jnp.clip(jax.random.normal(jax.random.fold_in(key, 1), shape), -6.0, 6.0)
    return values.astype(jnp.bfloat16)


def draw_cache_k(key, part):
    shape = (CACHE_BLOCKS, BLK, KVH * HD)
    values = jnp.clip(jax.random.normal(jax.random.fold_in(key, 4), shape), -6.0, 6.0)
    return values.astype(jnp.bfloat16)


def slot_layout(key):
    return jax.random.permutation(jax.random.fold_in(key, 11), CACHE_BLOCKS).astype(jnp.int32)


def draw_block_slot(key, part):
    return slot_layout(key)


def device_lists(device_key):
    requests = QB_DEV * NLIST
    pool = jnp.arange(SEQ_DEVS * CAP, dtype=jnp.int32) // CAP
    pool = jax.random.permutation(jax.random.fold_in(device_key, 1), pool)
    heavy = jax.random.randint(jax.random.fold_in(device_key, 2), (), 0, SEQ_DEVS).astype(jnp.int32)
    ranked = (pool == heavy).astype(jnp.int32) * (SEQ_DEVS * CAP) + jnp.arange(SEQ_DEVS * CAP, dtype=jnp.int32)
    taken = pool[jnp.argsort(ranked)][:requests - CAP]
    owners = jnp.concatenate([jnp.full((CAP,), heavy, jnp.int32), taken])
    position = jnp.arange(requests)
    earlier = (owners[None, :] == owners[:, None]) & (position[None, :] < position[:, None])
    ranking = jnp.sum(earlier.astype(jnp.int32), axis=1)
    offsets = jax.random.randint(jax.random.fold_in(device_key, 3), (SEQ_DEVS,), 0, CB_DEV).astype(jnp.int32)
    within = (offsets[owners] + ranking) % CB_DEV
    shuffle = jax.random.permutation(jax.random.fold_in(device_key, 4), requests)
    return (owners * CB_DEV + within)[shuffle]


def draw_pattern(key, part):
    base_key = jax.random.fold_in(key, 77)
    device_keys = jax.vmap(lambda device: jax.random.fold_in(base_key, device))(jnp.arange(SEQ_DEVS))
    slots = jax.vmap(device_lists)(device_keys)
    inverse = jnp.argsort(slot_layout(key)).astype(jnp.int32)
    return inverse[slots].reshape(QBLOCKS, NLIST).astype(jnp.int32)


def block_levels(stream_key, dims, split, low, largest):
    loudness, own = 1.0, jax.random.fold_in(stream_key, 6)
    for dim, blocks in split:
        steps = jnp.exp(jax.random.uniform(jax.random.fold_in(own, dim), (blocks,), jnp.float32, low / len(split), largest / len(split)))
        loudness = loudness * jnp.repeat(steps, dims[dim] // blocks).reshape([-1 if axis == dim else 1 for axis in range(len(dims))])
    return loudness


def noise(stream_key, dims, spread, reach, pieces=(), kind=jnp.bfloat16):
    values = spread * jax.random.normal(stream_key, dims, jnp.float32)
    if pieces:
        values = values * block_levels(stream_key, dims, pieces, -0.22, 0.18)
    return jnp.clip(values, -reach, reach).astype(kind)


def setup_inputs(seed: int = 0) -> dict:
    arg_keys = jax.random.split(jax.random.key(seed), 9)
    queries = draw_queries(jax.random.fold_in(arg_keys[8], 71), 0)
    span_k = noise(arg_keys[1], (TOKENS, KVH * HD), 1.0, 6.0, ((0, 32), (1, 4)))
    span_v = noise(arg_keys[2], (TOKENS, KVH * HD), 1.0, 6.0, ((0, 32), (1, 4)))
    cache_k = draw_cache_k(jax.random.fold_in(arg_keys[8], 71), 0)
    cache_v = noise(arg_keys[4], (CACHE_BLOCKS, BLK, KVH * HD), 1.0, 6.0, ((0, 32), (2, 4)))
    block_slot = draw_block_slot(jax.random.fold_in(arg_keys[8], 71), 0)
    pattern = draw_pattern(jax.random.fold_in(arg_keys[8], 71), 0)
    wo = noise(arg_keys[7], (QH * HD, D), 1.0, 6.0, ((0, 4), (1, 4)))
    return {"queries": queries, "span_k": span_k, "span_v": span_v, "cache_k": cache_k, "cache_v": cache_v, "block_slot": block_slot, "pattern": pattern, "wo": wo}


def attend_block(query_block, keys, values, present):
    length = keys.shape[0]
    block_len = query_block.shape[0]
    scores = jnp.einsum('tkgd,lkd->kgtl', query_block.astype(jnp.float32), keys.astype(jnp.float32)) / jnp.sqrt(jnp.float32(HD))
    column = jnp.arange(length)[None, :]
    row_ids = jnp.arange(block_len)[:, None]
    listed_end = length - 2 * block_len
    own_start = listed_end + block_len
    allowed = (column < listed_end) | (column >= listed_end) & (column < own_start) & present | (column >= own_start) & (column - own_start <= row_ids)
    scores = jnp.where(allowed, scores, -jnp.inf)
    top = lax.optimization_barrier(jnp.max(scores, axis=-1, keepdims=True))
    expo = jnp.exp(scores - top)
    probs_bf = (expo / lax.optimization_barrier(jnp.sum(expo, axis=-1, keepdims=True))).astype(jnp.bfloat16)
    output = jnp.einsum('kgtl,lkd->tkgd', probs_bf.astype(jnp.float32), values.astype(jnp.float32))
    return output.reshape(block_len, -1).astype(jnp.bfloat16)

def reference(queries, span_k, span_v, cache_k, cache_v, block_slot, pattern, wo):
    query_blocks = queries.reshape(QBLOCKS, BLK, KVH, GROUP, HD)
    own_k = span_k.reshape(QBLOCKS, BLK, KVH, HD)
    own_v = span_v.reshape(QBLOCKS, BLK, KVH, HD)

    def one_block(index):
        storage = block_slot[pattern[index]]
        listed_k = cache_k[storage].reshape(NLIST * BLK, KVH, HD)
        listed_v = cache_v[storage].reshape(NLIST * BLK, KVH, HD)
        before = jnp.maximum(index - 1, 0).astype(jnp.int32)
        keys = jnp.concatenate([listed_k, own_k[before], own_k[index]], axis=0)
        values = jnp.concatenate([listed_v, own_v[before], own_v[index]], axis=0)
        return attend_block(query_blocks[index], keys, values, index > 0)
    attended = lax.map(one_block, jnp.arange(QBLOCKS, dtype=jnp.int32)).reshape(TOKENS, QH * HD)
    group_cols = QH * HD // N_HEAD
    total = jnp.zeros((TOKENS, D), jnp.float32)
    for group_index in range(N_HEAD):
        lower = group_index * group_cols
        term = jnp.dot(attended[:, lower:lower + group_cols], wo[lower:lower + group_cols], preferred_element_type=jnp.float32).astype(jnp.bfloat16)
        term = lax.optimization_barrier(term)
        total = total + term.astype(jnp.float32)
    return total.astype(jnp.bfloat16)
```

```python
import functools

import jax
import jax.numpy as jnp
from jax import lax
from jax.experimental import pallas as pl
from jax.experimental.pallas import tpu as pltpu
from jax.sharding import PartitionSpec as P

HD = 128
BLK = 128
NEG = -1e30
MESH = pl.DeviceIdType.MESH
BF16 = jnp.bfloat16
F32 = jnp.float32
LOG2E = 1.4426950408889634


def position():
    z = lax.axis_index("fsdp")
    s = lax.axis_index("seq")
    y = lax.axis_index("head")
    return z, s // 2, s % 2, y


def dev(z, x, c, y):
    return ((z + 4) % 4, ((x + 4) % 4) * 2 + c, (y + 4) % 4)


def gather_kernel(q_ref, ck_ref, cv_ref, sk_ref, sv_ref, tab_ref,
                  qall_ref, pk_ref, pv_ref, prev_ref, taball_ref,
                  send_sem, recv_sem, loc_sem):
    z, x, c, y = position()
    far_z, far_x = (z, x + jnp.where(c == 0, -1, 1))
    wrap = jnp.where(c == 0, jnp.where(x == 0, -1, 0), jnp.where(x == 3, 1, 0))
    far_z = far_z + wrap

    barrier = pltpu.get_barrier_semaphore()
    for off in range(1, 16):
        pl.semaphore_signal(barrier, inc=1, device_id=dev(z + off // 4, x + off % 4, c, y), device_id_type=MESH)
    pl.semaphore_signal(barrier, inc=1, device_id=dev(z, x, 1 - c, y), device_id_type=MESH)
    pl.semaphore_signal(barrier, inc=1, device_id=dev(far_z, far_x, 1 - c, y), device_id_type=MESH)
    pl.semaphore_wait(barrier, 17)

    copies = []

    def send(src, dst, target):
        k = len(copies)
        cp = pltpu.make_async_remote_copy(
            src_ref=src, dst_ref=dst, send_sem=send_sem.at[k], recv_sem=recv_sem.at[k],
            device_id=target, device_id_type=MESH)
        cp.start()
        copies.append(cp)
        return cp

    def slot(dz, dx):
        return ((z + dz + 4) % 4) * 4 + (x + dx + 4) % 4

    here = slot(0, 0)
    tables = []
    for off in range(1, 16):
        dz, dx = off // 4, off % 4
        tables.append(send(tab_ref.at[slot(dz, dx)], taball_ref.at[here], dev(z + dz, x + dx, c, y)))
    nxt_x = x + jnp.where(c == 0, 0, 1)
    nxt_z = z + jnp.where((c == 1) & (x == 3), 1, 0)
    nxt = dev(nxt_z, nxt_x, 1 - c, y)
    send(sk_ref.at[pl.ds(BLK, BLK)], prev_ref.at[0], nxt)
    send(sv_ref.at[pl.ds(BLK, BLK)], prev_ref.at[1], nxt)

    def step(color, major, minor):
        return (minor, major) if color == 0 else (major, minor)

    def chunk(color, a, b, half=None):
        dz, dx = step(color, a, b)
        ref = qall_ref.at[slot(dz, dx), color]
        if half is None:
            return ref
        return ref.at[pl.ds(half * (BLK // 2), BLK // 2)]

    def to(color, a, b):
        dz, dx = step(color, a, b)
        return dev(z + dz, x + dx, c, y)

    ring = {}

    def own(color):
        mine, dst = q_ref.at[color], qall_ref.at[here, color]
        for d in (1, -1):
            ring[color, "a", d] = send(mine, dst, to(color, d, 0))
        for d in (1, -1):
            ring[color, "b", 0, d] = send(mine, dst, to(color, 0, d))

    own(0)
    own(1)
    partner = dev(z, x, 1 - c, y)
    send(ck_ref, pk_ref, partner)
    send(cv_ref, pv_ref, partner)
    locals_ = [pltpu.make_async_copy(q_ref, qall_ref.at[here], loc_sem.at[0]),
               pltpu.make_async_copy(tab_ref.at[here], taball_ref.at[here], loc_sem.at[1])]
    for cp in locals_:
        cp.start()

    for d in (1, -1):
        for color in (0, 1):
            ring[color, "a", d].wait_recv()
            half = 0 if d == 1 else 1
            part = chunk(color, -d, 0, half)
            ring[color, "o", d] = send(part, part, to(color, d, 0))
            whole = chunk(color, -d, 0)
            for e in (1, -1):
                ring[color, "b", -d, e] = send(whole, whole, to(color, 0, e))
    for d in (1, -1):
        for color in (0, 1):
            ring[color, "b", 0, d].wait_recv()
            part = chunk(color, 0, -d, 0 if d == 1 else 1)
            ring[color, "c", 0, d] = send(part, part, to(color, 0, d))
    for color in (0, 1):
        ring[color, "o", 1].wait_recv()
        ring[color, "o", -1].wait_recv()
        whole = chunk(color, 2, 0)
        for e in (1, -1):
            ring[color, "b", 2, e] = send(whole, whole, to(color, 0, e))
    for a in (-1, 1, 2):
        for d in (1, -1):
            for color in (0, 1):
                ring[color, "b", a, d].wait_recv()
                part = chunk(color, a, -d, 0 if d == 1 else 1)
                ring[color, "c", a, d] = send(part, part, to(color, 0, d))
    waited = {id(v) for k, v in ring.items() if k[1] != "c"}
    for cp in copies:
        if id(cp) not in waited:
            cp.wait_recv()
    for cp in copies:
        cp.wait_send()
    for cp in locals_:
        cp.wait()


N_GATHER = 15 + 2 + 8 + 2 + 4 + 8 + 4 + 4 + 12


def gather_queries(q, ck, cv, sk, sv, tab):
    anyspec = pl.BlockSpec(memory_space=pl.ANY)
    return pl.pallas_call(
        gather_kernel,
        out_shape=(
            jax.ShapeDtypeStruct((16, 2, BLK, q.shape[-1]), BF16),
            jax.ShapeDtypeStruct(ck.shape, BF16),
            jax.ShapeDtypeStruct(cv.shape, BF16),
            jax.ShapeDtypeStruct((2, BLK, HD), BF16),
            jax.ShapeDtypeStruct(tab.shape, jnp.int32),
        ),
        in_specs=[anyspec] * 6,
        out_specs=[anyspec] * 5,
        scratch_shapes=[
            pltpu.SemaphoreType.DMA((N_GATHER,)),
            pltpu.SemaphoreType.DMA((N_GATHER,)),
            pltpu.SemaphoreType.DMA((2,)),
        ],
        compiler_params=pltpu.CompilerParams(collective_id=0, has_side_effects=True),
        name="gather_queries",
    )(q, ck, cv, sk, sv, tab)


def attend_kernel(tab_ref, q_ref, ck_ref, cv_ref, pk_ref, pv_ref, sk_ref, sv_ref, prev_ref, out_ref,
                  kall, vall, span, qt, m_s, l_s, acc, sems):
    i = pl.program_id(0)
    z, x, c, y = position()
    chip = i // 2
    color = i % 2
    mine = chip == z * 4 + x

    @pl.when(i == 0)
    def _():
        loads = [
            pltpu.make_async_copy(ck_ref, kall.at[pl.ds(0, 64)], sems.at[0]),
            pltpu.make_async_copy(pk_ref, kall.at[pl.ds(64, 64)], sems.at[1]),
            pltpu.make_async_copy(cv_ref, vall.at[pl.ds(0, 64)], sems.at[2]),
            pltpu.make_async_copy(pv_ref, vall.at[pl.ds(64, 64)], sems.at[3]),
            pltpu.make_async_copy(prev_ref.at[0], span.at[0, pl.ds(0, BLK)], sems.at[4]),
            pltpu.make_async_copy(prev_ref.at[1], span.at[1, pl.ds(0, BLK)], sems.at[5]),
            pltpu.make_async_copy(sk_ref, span.at[0, pl.ds(BLK, 2 * BLK)], sems.at[6]),
            pltpu.make_async_copy(sv_ref, span.at[1, pl.ds(BLK, 2 * BLK)], sems.at[7]),
        ]
        for cp in loads:
            cp.start()
        for cp in loads:
            cp.wait()

    heads = q_ref.shape[-1] // HD
    for g in range(heads):
        qt[:, g * HD:(g + 1) * HD] = q_ref[0, 0, :, g * HD:(g + 1) * HD].T
    m_s[...] = jnp.full_like(m_s, NEG)
    l_s[...] = jnp.zeros_like(l_s)
    acc[...] = jnp.zeros_like(acc)
    scale = LOG2E / (HD ** 0.5)
    width = 256

    def pair(keys, values, bias):
        for t in range(heads * HD // width):
            cols = slice(t * width, (t + 1) * width)
            s = jnp.dot(keys, qt[:, cols], preferred_element_type=F32) * scale
            if bias is not None:
                s = s + bias
            top = jnp.maximum(m_s[:, cols], jnp.max(s, axis=0, keepdims=True))
            old = jnp.exp2(m_s[:, cols] - top)
            p = jnp.exp2(s - top)
            m_s[:, cols] = top
            l_s[:, cols] = l_s[:, cols] * old + jnp.sum(p, axis=0, keepdims=True)
            acc[:, cols] = acc[:, cols] * old + lax.dot_general(
                values, p.astype(BF16), (((0,), (0,)), ((), ())), preferred_element_type=F32)

    count = tab_ref[chip, 0, color * 16 + 15]
    base = color * 16

    def both(j, carry):
        i0 = tab_ref[chip, 0, base + 2 * j]
        i1 = tab_ref[chip, 0, base + 2 * j + 1]
        keys = jnp.concatenate([kall[i0], kall[i1]], axis=0)
        values = jnp.concatenate([vall[i0], vall[i1]], axis=0)
        pair(keys, values, None)
        return carry

    lax.fori_loop(0, count // 2, both, 0)

    @pl.when(count % 2 == 1)
    def _():
        i0 = tab_ref[chip, 0, base + count - 1]
        pair(kall[i0], vall[i0], None)

    @pl.when(mine)
    def _():
        rows = pl.ds(pl.multiple_of(color * BLK, BLK), 2 * BLK)
        key = lax.broadcasted_iota(jnp.int32, (2 * BLK, width), 0)
        tok = lax.broadcasted_iota(jnp.int32, (2 * BLK, width), 1) % BLK
        first = (z * 8 + x * 2 + c) * 2 + color == 0
        low = jnp.where(first, BLK, 0)
        allowed = (key >= low) & (key - BLK <= tok)
        pair(span[0, rows, :], span[1, rows, :], jnp.where(allowed, 0.0, 2 * NEG))

    some = l_s[...] > 0
    total = jnp.where(some, l_s[...], 1.0)
    lse = m_s[...] + jnp.log2(total)
    hi = lse.astype(BF16)
    rest = lse - hi.astype(F32)
    mid = rest.astype(BF16)
    low_ = (rest - mid.astype(F32)).astype(BF16)
    o = (acc[...] / total).astype(BF16)
    row = lax.broadcasted_iota(jnp.int32, (16, lse.shape[1]), 0)
    tail = jnp.where(row == 0, hi.astype(F32), jnp.where(row == 1, mid.astype(F32), jnp.where(row == 2, low_.astype(F32), 0.0))).astype(BF16)
    half = lse.shape[1] // 2
    for h in range(2):
        out_ref[0, 0, h, 0:HD, :] = o[:, h * half:(h + 1) * half]
        out_ref[0, 0, h, HD:HD + 16, :] = tail[:, h * half:(h + 1) * half]


def attend(tab, q_all, ck, cv, pk, pv, sk, sv, prev):
    width = q_all.shape[-1]
    anyspec = pl.BlockSpec(memory_space=pl.ANY)
    return pl.pallas_call(
        attend_kernel,
        out_shape=jax.ShapeDtypeStruct((16, 2, 2, HD + 16, width // 2), BF16),
        grid_spec=pltpu.PrefetchScalarGridSpec(
            num_scalar_prefetch=1,
            grid=(32,),
            in_specs=[pl.BlockSpec((1, 1, BLK, width), lambda i, t: (i // 2, i % 2, 0, 0))] + [anyspec] * 7,
            out_specs=pl.BlockSpec((1, 1, 2, HD + 16, width // 2), lambda i, t: (i // 2, i % 2, 0, 0, 0)),
            scratch_shapes=[
                pltpu.VMEM((128, BLK, HD), BF16),
                pltpu.VMEM((128, BLK, HD), BF16),
                pltpu.VMEM((2, 3 * BLK, HD), BF16),
                pltpu.VMEM((HD, width), BF16),
                pltpu.VMEM((1, width), F32),
                pltpu.VMEM((1, width), F32),
                pltpu.VMEM((HD, width), F32),
                pltpu.SemaphoreType.DMA((8,)),
            ],
        ),
        compiler_params=pltpu.CompilerParams(vmem_limit_bytes=40 * 2**20),
        cost_estimate=pl.CostEstimate(flops=7_000_000_000, bytes_accessed=26_000_000, transcendentals=13_000_000),
        name="attend",
    )(tab, q_all, ck, cv, pk, pv, sk, sv, prev)


def merge(dst, *srcs):
    def lse_of(ref):
        t = ref[HD:HD + 16, :].astype(F32)
        return t[0:1] + t[1:2] + t[2:3]

    lses = [lse_of(r) for r in srcs]
    top = functools.reduce(jnp.maximum, lses)
    ws = [jnp.exp2(v - top) for v in lses]
    total = functools.reduce(lambda a, b: a + b, ws)
    inv = 1.0 / total
    ws = [w * inv for w in ws]
    lse = top + jnp.log2(total)
    rows = 32

    def body(r, carry):
        sl = pl.ds(pl.multiple_of(r * rows, rows), rows)
        out = ws[0] * srcs[0][sl, :].astype(F32)
        for w, ref in zip(ws[1:], srcs[1:]):
            out = out + w * ref[sl, :].astype(F32)
        dst[sl, :] = out.astype(BF16)
        return carry

    lax.fori_loop(0, HD // rows, body, 0)
    hi = lse.astype(BF16).astype(F32)
    mid = (lse - hi).astype(BF16).astype(F32)
    low = lse - hi - mid
    row = lax.broadcasted_iota(jnp.int32, (16, lse.shape[1]), 0)
    dst[HD:HD + 16, :] = jnp.where(row == 0, hi, jnp.where(row == 1, mid, jnp.where(row == 2, low, 0.0))).astype(BF16)


def reduce_kernel(part_ref, out_ref, loc, recv, send_sem, recv_sem, load_sem):
    z, x, c, y = position()
    barrier = pltpu.get_barrier_semaphore()
    for dz, dx in ((0, 1), (0, -1), (1, 0), (-1, 0)):
        pl.semaphore_signal(barrier, inc=1, device_id=dev(z + dz, x + dx, c, y), device_id_type=MESH)

    def step(color, a, b):
        return (a, b) if color == 0 else (b, a)

    def slot(color, a, b):
        dz, dx = step(color, a, b)
        return ((z + dz + 4) % 4) * 4 + (x + dx + 4) % 4

    def to(color, a, b):
        dz, dx = step(color, a, b)
        return dev(z + dz, x + dx, c, y)

    order = [2, 1, 3, 0]
    loads = {}
    k = 0
    for a in (2, 1, 3, 0):
        for b in order:
            for color in (0, 1):
                cp = pltpu.make_async_copy(
                    part_ref.at[slot(color, a, b), color], loc.at[color, a * 4 + b], load_sem.at[k])
                cp.start()
                loads[color, a, b] = cp
                k += 1
    pl.semaphore_wait(barrier, 4)

    copies = {}

    def send(key, src, target):
        k = len(copies)
        cp = pltpu.make_async_remote_copy(
            src_ref=src, dst_ref=recv.at[k], send_sem=send_sem.at[k], recv_sem=recv_sem.at[k],
            device_id=target, device_id_type=MESH)
        cp.start()
        copies[key] = (cp, k)

    def got(key):
        cp, k = copies[key]
        cp.wait_recv()
        return recv.at[k]

    def piece(color, a, b, half):
        return loc.at[color, a * 4 + b, half]

    for b in order:
        for color in (0, 1):
            loads[color, 2, b].wait()
            send((color, 1, b, "op"), piece(color, 2, b, 0), to(color, 1, 0))
            send((color, 1, b, "om"), piece(color, 2, b, 1), to(color, -1, 0))
    for b in order:
        for color in (0, 1):
            loads[color, 1, b].wait()
            send((color, 1, b, "p1"), piece(color, 1, b, 1), to(color, 1, 0))
            loads[color, 3, b].wait()
            send((color, 1, b, "m0"), piece(color, 3, b, 0), to(color, -1, 0))
    for b in order:
        for color in (0, 1):
            r = got((color, 1, b, "op"))
            merge(piece(color, 1, b, 0), piece(color, 1, b, 0), r)
            send((color, 1, b, "p0"), piece(color, 1, b, 0), to(color, 1, 0))
            r = got((color, 1, b, "om"))
            merge(piece(color, 3, b, 1), piece(color, 3, b, 1), r)
            send((color, 1, b, "m1"), piece(color, 3, b, 1), to(color, -1, 0))
    for b in order:
        for color in (0, 1):
            loads[color, 0, b].wait()
            for half in (0, 1):
                p = got((color, 1, b, "p%d" % half))
                m = got((color, 1, b, "m%d" % half))
                merge(piece(color, 0, b, half), piece(color, 0, b, half), p, m)
            if b == 2:
                send((color, 2, "op"), piece(color, 0, 2, 0), to(color, 0, 1))
                send((color, 2, "om"), piece(color, 0, 2, 1), to(color, 0, -1))
            if b == 1:
                send((color, 2, "p1"), piece(color, 0, 1, 1), to(color, 0, 1))
            if b == 3:
                send((color, 2, "m0"), piece(color, 0, 3, 0), to(color, 0, -1))
    for color in (0, 1):
        r = got((color, 2, "op"))
        merge(piece(color, 0, 1, 0), piece(color, 0, 1, 0), r)
        send((color, 2, "p0"), piece(color, 0, 1, 0), to(color, 0, 1))
        r = got((color, 2, "om"))
        merge(piece(color, 0, 3, 1), piece(color, 0, 3, 1), r)
        send((color, 2, "m1"), piece(color, 0, 3, 1), to(color, 0, -1))
    for color in (0, 1):
        for half in (0, 1):
            p = got((color, 2, "p%d" % half))
            m = got((color, 2, "m%d" % half))
            own = piece(color, 0, 0, half)
            merge(own, own, p, m)
            lanes = own.shape[1]
            for g in range(lanes // HD):
                col = half * lanes + g * HD
                out_ref[color * BLK:(color + 1) * BLK, col:col + HD] = own[0:HD, g * HD:(g + 1) * HD].T
    for cp, _ in copies.values():
        cp.wait_send()


N_REDUCE = 60


def reduce_partials(part):
    rows, lanes = part.shape[-2:]
    return pl.pallas_call(
        reduce_kernel,
        out_shape=jax.ShapeDtypeStruct((2 * BLK, 2 * lanes), BF16),
        in_specs=[pl.BlockSpec(memory_space=pl.ANY)],
        out_specs=pl.BlockSpec(memory_space=pltpu.VMEM),
        scratch_shapes=[
            pltpu.VMEM((2, 16, 2, rows, lanes), BF16),
            pltpu.VMEM((N_REDUCE, rows, lanes), BF16),
            pltpu.SemaphoreType.DMA((N_REDUCE,)),
            pltpu.SemaphoreType.DMA((N_REDUCE,)),
            pltpu.SemaphoreType.DMA((32,)),
        ],
        compiler_params=pltpu.CompilerParams(
            collective_id=1, has_side_effects=True, vmem_limit_bytes=40 * 2**20),
        name="reduce_partials",
    )(part)


def request_table(block_slot, pattern, core, cb_local):
    slot_ids = block_slot[pattern]
    owners = slot_ids // cb_local
    chips = owners // 2
    rel = jnp.where(owners % 2 == core, 0, cb_local) + slot_ids % cb_local
    entry = jnp.arange(pattern.shape[1])
    same = (chips[:, :, None] == chips[:, None, :]) & (entry[None, :] < entry[:, None])[None]
    rank = jnp.sum(same.astype(jnp.int32), axis=2)
    lane = jnp.arange(16)
    hit = (chips[None, :, None, :] == jnp.arange(16)[:, None, None, None])
    pick = hit & (rank[None, :, None, :] == lane[None, None, :, None])
    value = jnp.where(lane[None, None, :, None] == 15, hit.astype(jnp.int32), jnp.where(pick, rel[None, :, None, :], 0))
    table = jnp.sum(value, axis=3).reshape(16, 1, 32)
    return jnp.pad(table, ((0, 0), (0, 0), (0, 96)))


def body(queries, span_k, span_v, cache_k, cache_v, block_slot, pattern, wo):
    core = lax.axis_index("seq") % 2
    tab = request_table(block_slot, pattern, core, cache_k.shape[0])
    q = queries.reshape(2, BLK, queries.shape[1])
    q_all, pk, pv, prev, tab_all = gather_queries(q, cache_k, cache_v, span_k, span_v, tab)
    part = attend(tab_all, q_all, cache_k, cache_v, pk, pv, span_k, span_v, prev)
    attended = reduce_partials(part)
    partial_terms = jnp.dot(
        attended, lax.all_gather(wo, "fsdp", axis=1, tiled=True), preferred_element_type=F32
    )
    return lax.psum(partial_terms.astype(BF16), "head")


def solution(mesh):
    return jax.shard_map(
        body,
        mesh=mesh,
        in_specs=(
            P(("fsdp", "seq"), "head"),
            P(("fsdp", "seq"), "head"),
            P(("fsdp", "seq"), "head"),
            P(("fsdp", "seq"), None, "head"),
            P(("fsdp", "seq"), None, "head"),
            P(),
            P(("fsdp", "seq"), None),
            P("head", "fsdp"),
        ),
        out_specs=P(("fsdp", "seq"), None),
        check_vma=False,
    )
```

```python
import functools

import jax
import jax.numpy as jnp
from jax import lax
from jax.experimental import pallas as pl
from jax.experimental.pallas import tpu as pltpu
from jax.sharding import PartitionSpec as P

HD = 128
BLK = 128
NEG = -1e30
VMEM = 62 * 2**20
MESH = pl.DeviceIdType.MESH
BF16 = jnp.bfloat16
F32 = jnp.float32
LOG2E = 1.4426950408889634


def position():
    z = lax.axis_index("fsdp")
    s = lax.axis_index("seq")
    y = lax.axis_index("head")
    return z, s // 2, s % 2, y


def dev(z, x, c, y):
    return ((z + 4) % 4, ((x + 4) % 4) * 2 + c, (y + 4) % 4)


def gather_kernel(q_ref, ck_ref, cv_ref, sk_ref, sv_ref, tab_ref, wo_ref,
                  qall_ref, pk_ref, pv_ref, prev_ref, taball_ref, won_ref,
                  send_sem, recv_sem, loc_sem):
    z, x, c, y = position()
    far_z, far_x = (z, x + jnp.where(c == 0, -1, 1))
    wrap = jnp.where(c == 0, jnp.where(x == 0, -1, 0), jnp.where(x == 3, 1, 0))
    far_z = far_z + wrap

    barrier = pltpu.get_barrier_semaphore()
    for off in range(1, 16):
        pl.semaphore_signal(barrier, inc=1, device_id=dev(z + off // 4, x + off % 4, c, y), device_id_type=MESH)
    pl.semaphore_signal(barrier, inc=1, device_id=dev(z, x, 1 - c, y), device_id_type=MESH)
    pl.semaphore_signal(barrier, inc=1, device_id=dev(far_z, far_x, 1 - c, y), device_id_type=MESH)
    for d in (1, -1):
        pl.semaphore_signal(barrier, inc=1, device_id=dev(z, x, c, y + d), device_id_type=MESH)
    pl.semaphore_wait(barrier, 19)

    copies = []

    def send(src, dst, target):
        k = len(copies)
        cp = pltpu.make_async_remote_copy(
            src_ref=src, dst_ref=dst, send_sem=send_sem.at[k], recv_sem=recv_sem.at[k],
            device_id=target, device_id_type=MESH)
        cp.start()
        copies.append(cp)
        return cp

    def slot(dz, dx):
        return ((z + dz + 4) % 4) * 4 + (x + dx + 4) % 4

    here = slot(0, 0)
    tables = []
    for off in range(1, 16):
        dz, dx = off // 4, off % 4
        tables.append(send(tab_ref.at[slot(dz, dx)], taball_ref.at[here], dev(z + dz, x + dx, c, y)))
    nxt_x = x + jnp.where(c == 0, 0, 1)
    nxt_z = z + jnp.where((c == 1) & (x == 3), 1, 0)
    nxt = dev(nxt_z, nxt_x, 1 - c, y)
    send(sk_ref.at[pl.ds(BLK, BLK)], prev_ref.at[0], nxt)
    send(sv_ref.at[pl.ds(BLK, BLK)], prev_ref.at[1], nxt)

    def step(color, major, minor):
        return (minor, major) if color == 0 else (major, minor)

    def chunk(color, a, b, half=None):
        dz, dx = step(color, a, b)
        ref = qall_ref.at[slot(dz, dx), color]
        if half is None:
            return ref
        return ref.at[pl.ds(half * (BLK // 2), BLK // 2)]

    def to(color, a, b):
        dz, dx = step(color, a, b)
        return dev(z + dz, x + dx, c, y)

    ring = {}

    def own(color):
        mine, dst = q_ref.at[color], qall_ref.at[here, color]
        for d in (1, -1):
            ring[color, "a", d] = send(mine, dst, to(color, d, 0))
        for d in (1, -1):
            ring[color, "b", 0, d] = send(mine, dst, to(color, 0, d))

    own(0)
    own(1)
    depth = wo_ref.shape[0] // 2
    share = pl.ds(pl.multiple_of(c * depth, depth), depth)
    wo_up = send(wo_ref.at[share], won_ref.at[0, share], dev(z, x, c, y + 1))
    wo_down = send(wo_ref.at[share], won_ref.at[1, share], dev(z, x, c, y - 1))
    partner = dev(z, x, 1 - c, y)
    send(ck_ref, pk_ref, partner)
    send(cv_ref, pv_ref, partner)
    locals_ = [pltpu.make_async_copy(q_ref, qall_ref.at[here], loc_sem.at[0]),
               pltpu.make_async_copy(tab_ref.at[here], taball_ref.at[here], loc_sem.at[1])]
    for cp in locals_:
        cp.start()

    for d in (1, -1):
        for color in (0, 1):
            ring[color, "a", d].wait_recv()
            half = 0 if d == 1 else 1
            part = chunk(color, -d, 0, half)
            ring[color, "o", d] = send(part, part, to(color, d, 0))
            whole = chunk(color, -d, 0)
            for e in (1, -1):
                ring[color, "b", -d, e] = send(whole, whole, to(color, 0, e))
    for d in (1, -1):
        for color in (0, 1):
            ring[color, "b", 0, d].wait_recv()
            part = chunk(color, 0, -d, 0 if d == 1 else 1)
            ring[color, "c", 0, d] = send(part, part, to(color, 0, d))
    for color in (0, 1):
        ring[color, "o", 1].wait_recv()
        ring[color, "o", -1].wait_recv()
        whole = chunk(color, 2, 0)
        for e in (1, -1):
            ring[color, "b", 2, e] = send(whole, whole, to(color, 0, e))
    for a in (-1, 1, 2):
        for d in (1, -1):
            for color in (0, 1):
                ring[color, "b", a, d].wait_recv()
                part = chunk(color, a, -d, 0 if d == 1 else 1)
                ring[color, "c", a, d] = send(part, part, to(color, 0, d))
    wo_up.wait_recv()
    send(won_ref.at[0, share], won_ref.at[0, share], partner)
    wo_down.wait_recv()
    send(won_ref.at[1, share], won_ref.at[1, share], partner)
    waited = {id(v) for k, v in ring.items() if k[1] != "c"} | {id(wo_up), id(wo_down)}
    for cp in copies:
        if id(cp) not in waited:
            cp.wait_recv()
    for cp in copies:
        cp.wait_send()
    for cp in locals_:
        cp.wait()


N_GATHER = 15 + 2 + 8 + 2 + 2 + 4 + 8 + 4 + 4 + 12 + 2


def gather_queries(q, ck, cv, sk, sv, tab, wo):
    anyspec = pl.BlockSpec(memory_space=pl.ANY)
    return pl.pallas_call(
        gather_kernel,
        out_shape=(
            jax.ShapeDtypeStruct((16, 2, BLK, q.shape[-1]), BF16),
            jax.ShapeDtypeStruct(ck.shape, BF16),
            jax.ShapeDtypeStruct(cv.shape, BF16),
            jax.ShapeDtypeStruct((2, BLK, HD), BF16),
            jax.ShapeDtypeStruct(tab.shape, jnp.int32),
            jax.ShapeDtypeStruct((2,) + wo.shape, BF16),
        ),
        in_specs=[anyspec] * 7,
        out_specs=[anyspec] * 6,
        scratch_shapes=[
            pltpu.SemaphoreType.DMA((N_GATHER,)),
            pltpu.SemaphoreType.DMA((N_GATHER,)),
            pltpu.SemaphoreType.DMA((2,)),
        ],
        compiler_params=pltpu.CompilerParams(collective_id=0, has_side_effects=True, vmem_limit_bytes=VMEM),
        name="gather_queries",
    )(q, ck, cv, sk, sv, tab, wo)


def attend_kernel(tab_ref, q_ref, ck_ref, cv_ref, pk_ref, pv_ref, sk_ref, sv_ref, prev_ref, out_ref,
                  kall, vall, span, sbuf, pbuf, m_s, l_s, acc, sems):
    i = pl.program_id(0)
    z, x, c, y = position()
    chip = i // 2
    color = i % 2
    mine = chip == z * 4 + x

    @pl.when(i == 0)
    def _():
        loads = [
            pltpu.make_async_copy(ck_ref, kall.at[pl.ds(0, 64)], sems.at[0]),
            pltpu.make_async_copy(pk_ref, kall.at[pl.ds(64, 64)], sems.at[1]),
            pltpu.make_async_copy(cv_ref, vall.at[pl.ds(0, 64)], sems.at[2]),
            pltpu.make_async_copy(pv_ref, vall.at[pl.ds(64, 64)], sems.at[3]),
            pltpu.make_async_copy(prev_ref.at[0], span.at[0, pl.ds(0, BLK)], sems.at[4]),
            pltpu.make_async_copy(prev_ref.at[1], span.at[1, pl.ds(0, BLK)], sems.at[5]),
            pltpu.make_async_copy(sk_ref, span.at[0, pl.ds(BLK, 2 * BLK)], sems.at[6]),
            pltpu.make_async_copy(sv_ref, span.at[1, pl.ds(BLK, 2 * BLK)], sems.at[7]),
        ]
        for cp in loads:
            cp.start()
        for cp in loads:
            cp.wait()

    heads = q_ref.shape[-1] // HD
    m_s[...] = jnp.full_like(m_s, NEG)
    l_s[...] = jnp.zeros_like(l_s)
    acc[...] = jnp.zeros_like(acc)
    scale = LOG2E / (HD ** 0.5)
    width = 256

    def pair(keys, values, bias):
        rows = keys.shape[0]
        spans = [slice(t * width, (t + 1) * width) for t in range(heads * HD // width)]
        tops = []
        for cols in spans:
            s = jnp.dot(keys, q_ref[0, 0, :, cols], preferred_element_type=F32) * scale
            if bias is not None:
                s = s + bias
            sbuf[0:rows, cols] = s
            tops.append(jnp.maximum(m_s[:, cols], jnp.max(s, axis=0, keepdims=True)))
        olds = []
        for cols, top in zip(spans, tops):
            old = jnp.exp2(m_s[:, cols] - top)
            p = jnp.exp2(sbuf[0:rows, cols] - top)
            pbuf[0:rows, cols] = p.astype(BF16)
            m_s[:, cols] = top
            l_s[:, cols] = l_s[:, cols] * old + jnp.sum(p, axis=0, keepdims=True)
            olds.append(old)
        for cols, old in zip(spans, olds):
            acc[:, cols] = acc[:, cols] * old + lax.dot_general(
                values, pbuf[0:rows, cols], (((0,), (0,)), ((), ())), preferred_element_type=F32)

    count = tab_ref[chip, 0, color * 16 + 15]
    base = color * 16

    def both(j, carry):
        i0 = tab_ref[chip, 0, base + 2 * j]
        i1 = tab_ref[chip, 0, base + 2 * j + 1]
        keys = jnp.concatenate([kall[i0], kall[i1]], axis=0)
        values = jnp.concatenate([vall[i0], vall[i1]], axis=0)
        pair(keys, values, None)
        return carry

    lax.fori_loop(0, count // 2, both, 0)

    @pl.when(count % 2 == 1)
    def _():
        i0 = tab_ref[chip, 0, base + count - 1]
        pair(kall[i0], vall[i0], None)

    @pl.when(mine)
    def _():
        rows = pl.ds(pl.multiple_of(color * BLK, BLK), 2 * BLK)
        key = lax.broadcasted_iota(jnp.int32, (2 * BLK, width), 0)
        tok = lax.broadcasted_iota(jnp.int32, (2 * BLK, width), 1) % BLK
        first = (z * 8 + x * 2 + c) * 2 + color == 0
        low = jnp.where(first, BLK, 0)
        allowed = (key >= low) & (key - BLK <= tok)
        pair(span[0, rows, :], span[1, rows, :], jnp.where(allowed, 0.0, 2 * NEG))

    some = l_s[...] > 0
    total = jnp.where(some, l_s[...], 1.0)
    lse = m_s[...] + jnp.log2(total)
    hi = lse.astype(BF16)
    rest = lse - hi.astype(F32)
    mid = rest.astype(BF16)
    low_ = (rest - mid.astype(F32)).astype(BF16)
    o = (acc[...] / total).astype(BF16)
    row = lax.broadcasted_iota(jnp.int32, (16, lse.shape[1]), 0)
    tail = jnp.where(row == 0, hi.astype(F32), jnp.where(row == 1, mid.astype(F32), jnp.where(row == 2, low_.astype(F32), 0.0))).astype(BF16)
    half = lse.shape[1] // 2
    for h in range(2):
        out_ref[0, 0, h, 0:HD, :] = o[:, h * half:(h + 1) * half]
        out_ref[0, 0, h, HD:HD + 16, :] = tail[:, h * half:(h + 1) * half]


def attend(tab, q_all, ck, cv, pk, pv, sk, sv, prev):
    width = q_all.shape[-1]
    anyspec = pl.BlockSpec(memory_space=pl.ANY)
    return pl.pallas_call(
        attend_kernel,
        out_shape=jax.ShapeDtypeStruct((16, 2, 2, HD + 16, width // 2), BF16),
        grid_spec=pltpu.PrefetchScalarGridSpec(
            num_scalar_prefetch=1,
            grid=(32,),
            in_specs=[pl.BlockSpec((1, 1, BLK, width), lambda i, t: (i // 2, i % 2, 0, 0))] + [anyspec] * 7,
            out_specs=pl.BlockSpec((1, 1, 2, HD + 16, width // 2), lambda i, t: (i // 2, i % 2, 0, 0, 0)),
            scratch_shapes=[
                pltpu.VMEM((128, BLK, HD), BF16),
                pltpu.VMEM((128, BLK, HD), BF16),
                pltpu.VMEM((2, 3 * BLK, HD), BF16),
                pltpu.VMEM((2 * BLK, width), F32),
                pltpu.VMEM((2 * BLK, width), BF16),
                pltpu.VMEM((1, width), F32),
                pltpu.VMEM((1, width), F32),
                pltpu.VMEM((HD, width), F32),
                pltpu.SemaphoreType.DMA((8,)),
            ],
        ),
        compiler_params=pltpu.CompilerParams(vmem_limit_bytes=VMEM),
        cost_estimate=pl.CostEstimate(flops=7_000_000_000, bytes_accessed=26_000_000, transcendentals=13_000_000),
        name="attend",
    )(tab, q_all, ck, cv, pk, pv, sk, sv, prev)


def merge(dst, *srcs):
    def lse_of(ref):
        t = ref[HD:HD + 16, :].astype(F32)
        return t[0:1] + t[1:2] + t[2:3]

    lses = [lse_of(r) for r in srcs]
    top = functools.reduce(jnp.maximum, lses)
    ws = [jnp.exp2(v - top) for v in lses]
    total = functools.reduce(lambda a, b: a + b, ws)
    inv = 1.0 / total
    ws = [w * inv for w in ws]
    lse = top + jnp.log2(total)
    rows = 32

    def body(r, carry):
        sl = pl.ds(pl.multiple_of(r * rows, rows), rows)
        out = ws[0] * srcs[0][sl, :].astype(F32)
        for w, ref in zip(ws[1:], srcs[1:]):
            out = out + w * ref[sl, :].astype(F32)
        dst[sl, :] = out.astype(BF16)
        return carry

    lax.fori_loop(0, HD // rows, body, 0)
    hi = lse.astype(BF16).astype(F32)
    mid = (lse - hi).astype(BF16).astype(F32)
    low = lse - hi - mid
    row = lax.broadcasted_iota(jnp.int32, (16, lse.shape[1]), 0)
    dst[HD:HD + 16, :] = jnp.where(row == 0, hi, jnp.where(row == 1, mid, jnp.where(row == 2, low, 0.0))).astype(BF16)


def reduce_kernel(part_ref, won_ref, out_ref, woo_ref, loc, recv, send_sem, recv_sem, load_sem, wo_send, wo_recv):
    z, x, c, y = position()
    barrier = pltpu.get_barrier_semaphore()
    for dz, dx in ((0, 1), (0, -1), (1, 0), (-1, 0)):
        pl.semaphore_signal(barrier, inc=1, device_id=dev(z + dz, x + dx, c, y), device_id_type=MESH)
    for d in (1, -1):
        pl.semaphore_signal(barrier, inc=1, device_id=dev(z, x, c, y + d), device_id_type=MESH)
    partner = dev(z, x, 1 - c, y)
    pl.semaphore_signal(barrier, inc=1, device_id=partner, device_id_type=MESH)

    def step(color, a, b):
        return (a, b) if color == 0 else (b, a)

    def slot(color, a, b):
        dz, dx = step(color, a, b)
        return ((z + dz + 4) % 4) * 4 + (x + dx + 4) % 4

    def to(color, a, b):
        dz, dx = step(color, a, b)
        return dev(z + dz, x + dx, c, y)

    order = [2, 1, 3, 0]
    loads = {}
    k = 0
    for a in (2, 1, 3, 0):
        for b in order:
            for color in (0, 1):
                cp = pltpu.make_async_copy(
                    part_ref.at[slot(color, a, b), color], loc.at[color, a * 4 + b], load_sem.at[k])
                cp.start()
                loads[color, a, b] = cp
                k += 1
    pl.semaphore_wait(barrier, 7)

    quarter = woo_ref.shape[0] // 4
    wo_copies = []

    def send_wo(src, k, target):
        rows = pl.ds(pl.multiple_of(c * (2 * quarter) + (k % 2) * quarter, quarter), quarter)
        cp = pltpu.make_async_remote_copy(
            src_ref=src.at[rows], dst_ref=woo_ref.at[rows], send_sem=wo_send.at[k], recv_sem=wo_recv.at[k],
            device_id=target, device_id_type=MESH)
        cp.start()
        wo_copies.append(cp)

    send_wo(won_ref.at[0], 0, dev(z, x, c, y + 1))
    send_wo(won_ref.at[1], 1, dev(z, x, c, y - 1))

    copies = {}

    def send(key, src, target):
        k = len(copies)
        cp = pltpu.make_async_remote_copy(
            src_ref=src, dst_ref=recv.at[k], send_sem=send_sem.at[k], recv_sem=recv_sem.at[k],
            device_id=target, device_id_type=MESH)
        cp.start()
        copies[key] = (cp, k)

    def got(key):
        cp, k = copies[key]
        cp.wait_recv()
        return recv.at[k]

    def piece(color, a, b, half):
        return loc.at[color, a * 4 + b, half]

    for b in order:
        for color in (0, 1):
            loads[color, 2, b].wait()
            send((color, 1, b, "op"), piece(color, 2, b, 0), to(color, 1, 0))
            send((color, 1, b, "om"), piece(color, 2, b, 1), to(color, -1, 0))
    for b in order:
        for color in (0, 1):
            loads[color, 1, b].wait()
            send((color, 1, b, "p1"), piece(color, 1, b, 1), to(color, 1, 0))
            loads[color, 3, b].wait()
            send((color, 1, b, "m0"), piece(color, 3, b, 0), to(color, -1, 0))
    for b in order:
        for color in (0, 1):
            r = got((color, 1, b, "op"))
            merge(piece(color, 1, b, 0), piece(color, 1, b, 0), r)
            send((color, 1, b, "p0"), piece(color, 1, b, 0), to(color, 1, 0))
            r = got((color, 1, b, "om"))
            merge(piece(color, 3, b, 1), piece(color, 3, b, 1), r)
            send((color, 1, b, "m1"), piece(color, 3, b, 1), to(color, -1, 0))
    for b in order:
        for color in (0, 1):
            loads[color, 0, b].wait()
            for half in (0, 1):
                p = got((color, 1, b, "p%d" % half))
                m = got((color, 1, b, "m%d" % half))
                merge(piece(color, 0, b, half), piece(color, 0, b, half), p, m)
            if b == 2:
                send((color, 2, "op"), piece(color, 0, 2, 0), to(color, 0, 1))
                send((color, 2, "om"), piece(color, 0, 2, 1), to(color, 0, -1))
            if b == 1:
                send((color, 2, "p1"), piece(color, 0, 1, 1), to(color, 0, 1))
            if b == 3:
                send((color, 2, "m0"), piece(color, 0, 3, 0), to(color, 0, -1))
    for k in (0, 1):
        wo_copies[k].wait_recv()
        send_wo(woo_ref, 2 + k, partner)
    for color in (0, 1):
        r = got((color, 2, "op"))
        merge(piece(color, 0, 1, 0), piece(color, 0, 1, 0), r)
        send((color, 2, "p0"), piece(color, 0, 1, 0), to(color, 0, 1))
        r = got((color, 2, "om"))
        merge(piece(color, 0, 3, 1), piece(color, 0, 3, 1), r)
        send((color, 2, "m1"), piece(color, 0, 3, 1), to(color, 0, -1))
    for color in (0, 1):
        for half in (0, 1):
            p = got((color, 2, "p%d" % half))
            m = got((color, 2, "m%d" % half))
            own = piece(color, 0, 0, half)
            merge(own, own, p, m)
            lanes = own.shape[1]
            for g in range(lanes // HD):
                col = half * lanes + g * HD
                out_ref[color * BLK:(color + 1) * BLK, col:col + HD] = own[0:HD, g * HD:(g + 1) * HD].T
    for cp, _ in copies.values():
        cp.wait_send()
    for k in (2, 3):
        wo_copies[k].wait_recv()
    for cp in wo_copies:
        cp.wait_send()


N_REDUCE = 60


def reduce_partials(part, won):
    rows, lanes = part.shape[-2:]
    return pl.pallas_call(
        reduce_kernel,
        out_shape=(jax.ShapeDtypeStruct((2 * BLK, 2 * lanes), BF16),
                   jax.ShapeDtypeStruct(won.shape[1:], BF16)),
        in_specs=[pl.BlockSpec(memory_space=pl.ANY)] * 2,
        out_specs=(pl.BlockSpec(memory_space=pltpu.VMEM), pl.BlockSpec(memory_space=pl.ANY)),
        scratch_shapes=[
            pltpu.VMEM((2, 16, 2, rows, lanes), BF16),
            pltpu.VMEM((N_REDUCE, rows, lanes), BF16),
            pltpu.SemaphoreType.DMA((N_REDUCE,)),
            pltpu.SemaphoreType.DMA((N_REDUCE,)),
            pltpu.SemaphoreType.DMA((32,)),
            pltpu.SemaphoreType.DMA((4,)),
            pltpu.SemaphoreType.DMA((4,)),
        ],
        compiler_params=pltpu.CompilerParams(
            collective_id=1, has_side_effects=True, vmem_limit_bytes=VMEM),
        name="reduce_partials",
    )(part, won)


NCH = 4


def project_kernel(att_ref, wo_ref, won_ref, woo_ref, out_ref,
                   attz, hb, relay, w, acc, tile, zrelay,
                   w_sem, a_send, a_recv, b_send, b_recv, s_send, s_recv, t_send, t_recv, home_sem):
    z, x, c, y = position()
    barrier = pltpu.get_barrier_semaphore()
    for d in (1, -1):
        pl.semaphore_signal(barrier, inc=1, device_id=dev(z + d, x, c, y), device_id_type=MESH)
        pl.semaphore_signal(barrier, inc=1, device_id=dev(z, x, c, y + d), device_id_type=MESH)
    loads = [
        pltpu.make_async_copy(wo_ref, w.at[0], w_sem.at[0]),
        pltpu.make_async_copy(won_ref.at[1], w.at[1], w_sem.at[1]),
        pltpu.make_async_copy(won_ref.at[0], w.at[3], w_sem.at[2]),
        pltpu.make_async_copy(woo_ref, w.at[2], w_sem.at[3]),
    ]
    for cp in loads:
        cp.start()
    pl.semaphore_wait(barrier, 4)

    tokens, depth = att_ref.shape
    half = tokens // 2
    cols = wo_ref.shape[1]
    lo, hi = pl.ds(0, half), pl.ds(half, half)

    def remote(src, dst, ssem, rsem, target):
        return pltpu.make_async_remote_copy(
            src_ref=src, dst_ref=dst, send_sem=ssem, recv_sem=rsem, device_id=target, device_id_type=MESH)

    zp, zm = dev(z + 1, x, c, y), dev(z - 1, x, c, y)
    yp, ym = dev(z, x, c, y + 1), dev(z, x, c, y - 1)

    ring = [
        remote(att_ref, attz.at[3], a_send.at[0], a_recv.at[0], zp),
        remote(att_ref, attz.at[1], a_send.at[1], a_recv.at[1], zm),
        remote(attz.at[3, lo], attz.at[2, lo], a_send.at[2], a_recv.at[2], zp),
        remote(attz.at[1, hi], attz.at[2, hi], a_send.at[3], a_recv.at[3], zm),
    ]
    ring[0].start()
    ring[1].start()

    def spread(src):
        return [
            remote(src, hb.at[3], b_send.at[0], b_recv.at[0], yp),
            remote(src, hb.at[1], b_send.at[1], b_recv.at[1], ym),
            remote(src.at[lo], relay.at[0], b_send.at[2], b_recv.at[2], yp),
            remote(src.at[hi], relay.at[1], b_send.at[3], b_recv.at[3], ym),
        ]

    for dz in (0, 3, 1, 2):
        if dz == 3:
            ring[0].wait_recv()
            ring[2].start()
        if dz == 1:
            ring[1].wait_recv()
            ring[3].start()
        if dz == 2:
            ring[2].wait_recv()
            ring[3].wait_recv()
        src = att_ref if dz == 0 else attz.at[dz]
        d = (dz - y + 4) % 4
        sends = spread(src)

        @pl.when(d == 0)
        def _():
            hb[0] = src[...]

        @pl.when(d == 1)
        def _():
            sends[0].start()

        @pl.when(d == 3)
        def _():
            sends[1].start()

        @pl.when(d == 2)
        def _():
            sends[2].start()
            sends[3].start()

    sends = spread(att_ref)
    onward = [
        remote(relay.at[0], hb.at[2, lo], b_send.at[4], b_recv.at[4], yp),
        remote(relay.at[1], hb.at[2, hi], b_send.at[5], b_recv.at[5], ym),
    ]
    step = cols // NCH

    def term(r, first):
        def one(k, carry):
            sl = pl.ds(pl.multiple_of(k * 256, 256), 256)
            v = jnp.dot(hb[r], w[r, :, sl], preferred_element_type=F32)
            acc[:, sl] = v if first else acc[:, sl] + v
            return carry
        lax.fori_loop(0, cols // 256, one, 0)

    loads[0].wait()
    term(0, True)
    for k in (0, 1):
        sends[2 + k].wait_recv()
        onward[k].start()
    sends[0].wait_recv()
    loads[2].wait()
    term(3, False)
    sends[1].wait_recv()
    loads[1].wait()
    term(1, False)
    onward[0].wait_recv()
    onward[1].wait_recv()
    loads[3].wait()

    def region(ref, f, ch, rows=None):
        sl = pl.ds(pl.multiple_of(((f + 8) % 4) * cols + ch * step, step), step)
        return ref.at[:, sl] if rows is None else ref.at[rows, sl]

    def shifts(ch):
        n = ch * 5
        src = tile.at[ch]
        return [
            remote(src, region(out_ref, z, ch), s_send.at[n], s_recv.at[n], zp),
            remote(src, region(out_ref, z, ch), s_send.at[n], s_recv.at[n], zm),
            remote(src.at[lo], zrelay.at[ch, 0], s_send.at[n + 1], s_recv.at[n + 1], zp),
            remote(src.at[hi], zrelay.at[ch, 1], s_send.at[n + 2], s_recv.at[n + 2], zm),
            remote(zrelay.at[ch, 0], region(out_ref, z - 1, ch, lo), s_send.at[n + 3], s_recv.at[n + 3], zp),
            remote(zrelay.at[ch, 1], region(out_ref, z + 1, ch, hi), s_send.at[n + 4], s_recv.at[n + 4], zm),
        ]

    def home(ch):
        return pltpu.make_async_copy(tile.at[ch], region(out_ref, z, ch), home_sem.at[ch])

    def bcast(ch):
        n = ch * 4
        mine = region(out_ref, z - y, ch)
        up = region(out_ref, z - y + 1, ch, lo)
        down = region(out_ref, z - y - 1, ch, hi)
        return [
            remote(mine, mine, t_send.at[n], t_recv.at[n], yp),
            remote(mine, mine, t_send.at[n + 1], t_recv.at[n + 1], ym),
            remote(up, up, t_send.at[n + 2], t_recv.at[n + 2], yp),
            remote(down, down, t_send.at[n + 3], t_recv.at[n + 3], ym),
        ]

    for t in range(NCH + 3):
        if t < NCH:
            for k in range(step // 256):
                sl = slice(t * step + k * 256, t * step + (k + 1) * 256)
                v = acc[:, sl] + jnp.dot(hb[2], w[2, :, sl], preferred_element_type=F32)
                tile[t, :, k * 256:(k + 1) * 256] = v.astype(BF16)
            sh = shifts(t)

            @pl.when(y == 0)
            def _():
                home(t).start()

            @pl.when(y == 1)
            def _():
                sh[0].start()

            @pl.when(y == 3)
            def _():
                sh[1].start()

            @pl.when(y == 2)
            def _():
                sh[2].start()
                sh[3].start()
        if 1 <= t < NCH + 1:
            sr = shifts(t - 1)

            @pl.when(y == 2)
            def _():
                sr[2].wait_recv()
                sr[4].start()
                sr[3].wait_recv()
                sr[5].start()
        if 2 <= t < NCH + 2:
            se = shifts(t - 2)

            @pl.when(y == 0)
            def _():
                home(t - 2).wait()

            @pl.when(y % 2 == 1)
            def _():
                se[0].wait_recv()

            @pl.when(y == 2)
            def _():
                se[4].wait_recv()
                se[5].wait_recv()

            b = bcast(t - 2)
            b[0].start()
            b[1].start()
        if 3 <= t:
            b = bcast(t - 3)
            b[0].wait_recv()
            b[2].start()
            b[1].wait_recv()
            b[3].start()
    for ch in range(NCH):
        b = bcast(ch)
        b[2].wait_recv()
        b[3].wait_recv()
        for cp in b:
            cp.wait_send()
        sw = shifts(ch)

        @pl.when(y % 2 == 1)
        def _():
            sw[0].wait_send()

        @pl.when(y == 2)
        def _():
            for cp in sw[2:]:
                cp.wait_send()
    for cp in ring + sends + onward:
        cp.wait_send()


def project(att, wo, won, woo):
    tokens, depth = att.shape
    cols = wo.shape[1]
    anyspec = pl.BlockSpec(memory_space=pl.ANY)
    sem = pltpu.SemaphoreType.DMA
    return pl.pallas_call(
        project_kernel,
        out_shape=jax.ShapeDtypeStruct((tokens, 4 * cols), BF16),
        in_specs=[pl.BlockSpec(memory_space=pltpu.VMEM)] + [anyspec] * 3,
        out_specs=anyspec,
        scratch_shapes=[
            pltpu.VMEM((4, tokens, depth), BF16),
            pltpu.VMEM((4, tokens, depth), BF16),
            pltpu.VMEM((2, tokens // 2, depth), BF16),
            pltpu.VMEM((4, depth, cols), BF16),
            pltpu.VMEM((tokens, cols), F32),
            pltpu.VMEM((NCH, tokens, cols // NCH), BF16),
            pltpu.VMEM((NCH, 2, tokens // 2, cols // NCH), BF16),
            sem((4,)), sem((4,)), sem((4,)), sem((6,)), sem((6,)),
            sem((5 * NCH,)), sem((5 * NCH,)), sem((4 * NCH,)), sem((4 * NCH,)), sem((NCH,)),
        ],
        compiler_params=pltpu.CompilerParams(
            collective_id=2, has_side_effects=True, vmem_limit_bytes=VMEM),
        name="project",
    )(att, wo, won, woo)


def turn_kernel(q_ref, out_ref):
    for color in range(2):
        for g in range(q_ref.shape[1] // HD):
            out_ref[color, :, g * BLK:(g + 1) * BLK] = q_ref[color * BLK:(color + 1) * BLK, g * HD:(g + 1) * HD].T


def turn(queries):
    return pl.pallas_call(
        turn_kernel,
        out_shape=jax.ShapeDtypeStruct((2, HD, queries.shape[1]), BF16),
        in_specs=[pl.BlockSpec(memory_space=pltpu.VMEM)],
        out_specs=pl.BlockSpec(memory_space=pltpu.VMEM),
        compiler_params=pltpu.CompilerParams(vmem_limit_bytes=VMEM),
        name="turn",
    )(queries)


def request_table(block_slot, pattern, core, cb_local):
    slot_ids = block_slot[pattern]
    owners = slot_ids // cb_local
    chips = owners // 2
    rel = jnp.where(owners % 2 == core, 0, cb_local) + slot_ids % cb_local
    entry = jnp.arange(pattern.shape[1])
    same = (chips[:, :, None] == chips[:, None, :]) & (entry[None, :] < entry[:, None])[None]
    rank = jnp.sum(same.astype(jnp.int32), axis=2)
    lane = jnp.arange(16)
    hit = (chips[None, :, None, :] == jnp.arange(16)[:, None, None, None])
    pick = hit & (rank[None, :, None, :] == lane[None, None, :, None])
    value = jnp.where(lane[None, None, :, None] == 15, hit.astype(jnp.int32), jnp.where(pick, rel[None, :, None, :], 0))
    table = jnp.sum(value, axis=3).reshape(16, 1, 32)
    return jnp.pad(table, ((0, 0), (0, 0), (0, 96)))


def body(queries, span_k, span_v, cache_k, cache_v, block_slot, pattern, wo):
    core = lax.axis_index("seq") % 2
    tab = request_table(block_slot, pattern, core, cache_k.shape[0])
    q = turn(queries)
    q_all, pk, pv, prev, tab_all, won = gather_queries(q, cache_k, cache_v, span_k, span_v, tab, wo)
    part = attend(tab_all, q_all, cache_k, cache_v, pk, pv, span_k, span_v, prev)
    attended, woo = reduce_partials(part, won)
    return project(attended, wo, won, woo)


def solution(mesh):
    return jax.shard_map(
        body,
        mesh=mesh,
        in_specs=(
            P(("fsdp", "seq"), "head"),
            P(("fsdp", "seq"), "head"),
            P(("fsdp", "seq"), "head"),
            P(("fsdp", "seq"), None, "head"),
            P(("fsdp", "seq"), None, "head"),
            P(),
            P(("fsdp", "seq"), None),
            P("head", "fsdp"),
        ),
        out_specs=P(("fsdp", "seq"), None),
        check_vma=False,
    )
```

```python
import functools

import jax
import jax.numpy as jnp
from jax import lax
from jax.experimental import pallas as pl
from jax.experimental.pallas import tpu as pltpu
from jax.sharding import PartitionSpec as P

HD = 128
BLK = 128
NEG = -1e30
VMEM = 62 * 2**20
MESH = pl.DeviceIdType.MESH
BF16 = jnp.bfloat16
F32 = jnp.float32
LOG2E = 1.4426950408889634


def position():
    z = lax.axis_index("fsdp")
    s = lax.axis_index("seq")
    y = lax.axis_index("head")
    return z, s // 2, s % 2, y


def dev(z, x, c, y):
    return ((z + 4) % 4, ((x + 4) % 4) * 2 + c, (y + 4) % 4)


def gather_kernel(q_ref, ck_ref, cv_ref, sk_ref, sv_ref, tab_ref, wo_ref,
                  qall_ref, pk_ref, pv_ref, prev_ref, taball_ref, won_ref,
                  send_sem, recv_sem, loc_sem):
    z, x, c, y = position()
    far_z, far_x = (z, x + jnp.where(c == 0, -1, 1))
    wrap = jnp.where(c == 0, jnp.where(x == 0, -1, 0), jnp.where(x == 3, 1, 0))
    far_z = far_z + wrap

    barrier = pltpu.get_barrier_semaphore()
    for off in range(1, 16):
        pl.semaphore_signal(barrier, inc=1, device_id=dev(z + off // 4, x + off % 4, c, y), device_id_type=MESH)
    pl.semaphore_signal(barrier, inc=1, device_id=dev(z, x, 1 - c, y), device_id_type=MESH)
    pl.semaphore_signal(barrier, inc=1, device_id=dev(far_z, far_x, 1 - c, y), device_id_type=MESH)
    for d in (1, -1):
        pl.semaphore_signal(barrier, inc=1, device_id=dev(z, x, c, y + d), device_id_type=MESH)
    pl.semaphore_wait(barrier, 19)

    copies = []

    def send(src, dst, target):
        k = len(copies)
        cp = pltpu.make_async_remote_copy(
            src_ref=src, dst_ref=dst, send_sem=send_sem.at[k], recv_sem=recv_sem.at[k],
            device_id=target, device_id_type=MESH)
        cp.start()
        copies.append(cp)
        return cp

    def slot(dz, dx):
        return ((z + dz + 4) % 4) * 4 + (x + dx + 4) % 4

    here = slot(0, 0)
    tables = []
    for off in range(1, 16):
        dz, dx = off // 4, off % 4
        tables.append(send(tab_ref.at[slot(dz, dx)], taball_ref.at[here], dev(z + dz, x + dx, c, y)))
    nxt_x = x + jnp.where(c == 0, 0, 1)
    nxt_z = z + jnp.where((c == 1) & (x == 3), 1, 0)
    nxt = dev(nxt_z, nxt_x, 1 - c, y)
    send(sk_ref.at[pl.ds(BLK, BLK)], prev_ref.at[0], nxt)
    send(sv_ref.at[pl.ds(BLK, BLK)], prev_ref.at[1], nxt)

    def step(color, major, minor):
        return (minor, major) if color == 0 else (major, minor)

    def chunk(color, a, b, half=None):
        dz, dx = step(color, a, b)
        ref = qall_ref.at[slot(dz, dx), color]
        if half is None:
            return ref
        return ref.at[pl.ds(half * (BLK // 2), BLK // 2)]

    def to(color, a, b):
        dz, dx = step(color, a, b)
        return dev(z + dz, x + dx, c, y)

    ring = {}

    def own(color):
        mine, dst = q_ref.at[color], qall_ref.at[here, color]
        for d in (1, -1):
            ring[color, "a", d] = send(mine, dst, to(color, d, 0))
        for d in (1, -1):
            ring[color, "b", 0, d] = send(mine, dst, to(color, 0, d))

    own(0)
    own(1)
    depth = wo_ref.shape[0] // 2
    share = pl.ds(pl.multiple_of(c * depth, depth), depth)
    wo_up = send(wo_ref.at[share], won_ref.at[0, share], dev(z, x, c, y + 1))
    wo_down = send(wo_ref.at[share], won_ref.at[1, share], dev(z, x, c, y - 1))
    partner = dev(z, x, 1 - c, y)
    send(ck_ref, pk_ref, partner)
    send(cv_ref, pv_ref, partner)
    locals_ = [pltpu.make_async_copy(q_ref, qall_ref.at[here], loc_sem.at[0]),
               pltpu.make_async_copy(tab_ref.at[here], taball_ref.at[here], loc_sem.at[1])]
    for cp in locals_:
        cp.start()

    for d in (1, -1):
        for color in (0, 1):
            ring[color, "a", d].wait_recv()
            half = 0 if d == 1 else 1
            part = chunk(color, -d, 0, half)
            ring[color, "o", d] = send(part, part, to(color, d, 0))
            whole = chunk(color, -d, 0)
            for e in (1, -1):
                ring[color, "b", -d, e] = send(whole, whole, to(color, 0, e))
    for d in (1, -1):
        for color in (0, 1):
            ring[color, "b", 0, d].wait_recv()
            part = chunk(color, 0, -d, 0 if d == 1 else 1)
            ring[color, "c", 0, d] = send(part, part, to(color, 0, d))
    for color in (0, 1):
        ring[color, "o", 1].wait_recv()
        ring[color, "o", -1].wait_recv()
        whole = chunk(color, 2, 0)
        for e in (1, -1):
            ring[color, "b", 2, e] = send(whole, whole, to(color, 0, e))
    for a in (-1, 1, 2):
        for d in (1, -1):
            for color in (0, 1):
                ring[color, "b", a, d].wait_recv()
                part = chunk(color, a, -d, 0 if d == 1 else 1)
                ring[color, "c", a, d] = send(part, part, to(color, 0, d))
    wo_up.wait_recv()
    send(won_ref.at[0, share], won_ref.at[0, share], partner)
    wo_down.wait_recv()
    send(won_ref.at[1, share], won_ref.at[1, share], partner)
    waited = {id(v) for k, v in ring.items() if k[1] != "c"} | {id(wo_up), id(wo_down)}
    for cp in copies:
        if id(cp) not in waited:
            cp.wait_recv()
    for cp in copies:
        cp.wait_send()
    for cp in locals_:
        cp.wait()


N_GATHER = 15 + 2 + 8 + 2 + 2 + 4 + 8 + 4 + 4 + 12 + 2


def gather_queries(q, ck, cv, sk, sv, tab, wo):
    anyspec = pl.BlockSpec(memory_space=pl.ANY)
    return pl.pallas_call(
        gather_kernel,
        out_shape=(
            jax.ShapeDtypeStruct((16, 2, BLK, q.shape[-1]), BF16),
            jax.ShapeDtypeStruct(ck.shape, BF16),
            jax.ShapeDtypeStruct(cv.shape, BF16),
            jax.ShapeDtypeStruct((2, BLK, HD), BF16),
            jax.ShapeDtypeStruct(tab.shape, jnp.int32),
            jax.ShapeDtypeStruct((2,) + wo.shape, BF16),
        ),
        in_specs=[anyspec] * 7,
        out_specs=[anyspec] * 6,
        scratch_shapes=[
            pltpu.SemaphoreType.DMA((N_GATHER,)),
            pltpu.SemaphoreType.DMA((N_GATHER,)),
            pltpu.SemaphoreType.DMA((2,)),
        ],
        compiler_params=pltpu.CompilerParams(collective_id=0, has_side_effects=True, vmem_limit_bytes=VMEM),
        name="gather_queries",
    )(q, ck, cv, sk, sv, tab, wo)


def attend_kernel(tab_ref, q_ref, ck_ref, cv_ref, pk_ref, pv_ref, sk_ref, sv_ref, prev_ref, out_ref,
                  kall, vall, span, sbuf, pbuf, m_s, l_s, acc, sems):
    i = pl.program_id(0)
    z, x, c, y = position()
    chip = i // 2
    color = i % 2
    mine = chip == z * 4 + x

    @pl.when(i == 0)
    def _():
        loads = [
            pltpu.make_async_copy(ck_ref, kall.at[pl.ds(0, 64)], sems.at[0]),
            pltpu.make_async_copy(pk_ref, kall.at[pl.ds(64, 64)], sems.at[1]),
            pltpu.make_async_copy(cv_ref, vall.at[pl.ds(0, 64)], sems.at[2]),
            pltpu.make_async_copy(pv_ref, vall.at[pl.ds(64, 64)], sems.at[3]),
            pltpu.make_async_copy(prev_ref.at[0], span.at[0, pl.ds(0, BLK)], sems.at[4]),
            pltpu.make_async_copy(prev_ref.at[1], span.at[1, pl.ds(0, BLK)], sems.at[5]),
            pltpu.make_async_copy(sk_ref, span.at[0, pl.ds(BLK, 2 * BLK)], sems.at[6]),
            pltpu.make_async_copy(sv_ref, span.at[1, pl.ds(BLK, 2 * BLK)], sems.at[7]),
        ]
        for cp in loads:
            cp.start()
        for cp in loads:
            cp.wait()

    heads = q_ref.shape[-1] // HD
    m_s[...] = jnp.full_like(m_s, NEG)
    l_s[...] = jnp.zeros_like(l_s)
    acc[...] = jnp.zeros_like(acc)
    scale = LOG2E / (HD ** 0.5)
    width = 256

    def pair(keys, values, bias):
        rows = keys.shape[0]
        spans = [slice(t * width, (t + 1) * width) for t in range(heads * HD // width)]
        tops = []
        for cols in spans:
            s = jnp.dot(keys, q_ref[0, 0, :, cols], preferred_element_type=F32) * scale
            if bias is not None:
                s = s + bias
            sbuf[0:rows, cols] = s
            tops.append(jnp.maximum(m_s[:, cols], jnp.max(s, axis=0, keepdims=True)))
        olds = []
        for cols, top in zip(spans, tops):
            old = jnp.exp2(m_s[:, cols] - top)
            p = jnp.exp2(sbuf[0:rows, cols] - top)
            pbuf[0:rows, cols] = p.astype(BF16)
            m_s[:, cols] = top
            l_s[:, cols] = l_s[:, cols] * old + jnp.sum(p, axis=0, keepdims=True)
            olds.append(old)
        for cols, old in zip(spans, olds):
            acc[:, cols] = acc[:, cols] * old + lax.dot_general(
                values, pbuf[0:rows, cols], (((0,), (0,)), ((), ())), preferred_element_type=F32)

    count = tab_ref[chip, 0, color * 16 + 15]
    base = color * 16

    def both(j, carry):
        i0 = tab_ref[chip, 0, base + 2 * j]
        i1 = tab_ref[chip, 0, base + 2 * j + 1]
        keys = jnp.concatenate([kall[i0], kall[i1]], axis=0)
        values = jnp.concatenate([vall[i0], vall[i1]], axis=0)
        pair(keys, values, None)
        return carry

    lax.fori_loop(0, count // 2, both, 0)

    @pl.when(count % 2 == 1)
    def _():
        i0 = tab_ref[chip, 0, base + count - 1]
        pair(kall[i0], vall[i0], None)

    @pl.when(mine)
    def _():
        rows = pl.ds(pl.multiple_of(color * BLK, BLK), 2 * BLK)
        key = lax.broadcasted_iota(jnp.int32, (2 * BLK, width), 0)
        tok = lax.broadcasted_iota(jnp.int32, (2 * BLK, width), 1) % BLK
        first = (z * 8 + x * 2 + c) * 2 + color == 0
        low = jnp.where(first, BLK, 0)
        allowed = (key >= low) & (key - BLK <= tok)
        pair(span[0, rows, :], span[1, rows, :], jnp.where(allowed, 0.0, 2 * NEG))

    some = l_s[...] > 0
    total = jnp.where(some, l_s[...], 1.0)
    lse = m_s[...] + jnp.log2(total)
    hi = lse.astype(BF16)
    rest = lse - hi.astype(F32)
    mid = rest.astype(BF16)
    low_ = (rest - mid.astype(F32)).astype(BF16)
    o = (acc[...] / total).astype(BF16)
    row = lax.broadcasted_iota(jnp.int32, (16, lse.shape[1]), 0)
    tail = jnp.where(row == 0, hi.astype(F32), jnp.where(row == 1, mid.astype(F32), jnp.where(row == 2, low_.astype(F32), 0.0))).astype(BF16)
    half = lse.shape[1] // 2
    for h in range(2):
        out_ref[0, 0, h, 0:HD, :] = o[:, h * half:(h + 1) * half]
        out_ref[0, 0, h, HD:HD + 16, :] = tail[:, h * half:(h + 1) * half]


def attend(tab, q_all, ck, cv, pk, pv, sk, sv, prev):
    width = q_all.shape[-1]
    anyspec = pl.BlockSpec(memory_space=pl.ANY)
    return pl.pallas_call(
        attend_kernel,
        out_shape=jax.ShapeDtypeStruct((16, 2, 2, HD + 16, width // 2), BF16),
        grid_spec=pltpu.PrefetchScalarGridSpec(
            num_scalar_prefetch=1,
            grid=(32,),
            in_specs=[pl.BlockSpec((1, 1, BLK, width), lambda i, t: (i // 2, i % 2, 0, 0))] + [anyspec] * 7,
            out_specs=pl.BlockSpec((1, 1, 2, HD + 16, width // 2), lambda i, t: (i // 2, i % 2, 0, 0, 0)),
            scratch_shapes=[
                pltpu.VMEM((128, BLK, HD), BF16),
                pltpu.VMEM((128, BLK, HD), BF16),
                pltpu.VMEM((2, 3 * BLK, HD), BF16),
                pltpu.VMEM((2 * BLK, width), F32),
                pltpu.VMEM((2 * BLK, width), BF16),
                pltpu.VMEM((1, width), F32),
                pltpu.VMEM((1, width), F32),
                pltpu.VMEM((HD, width), F32),
                pltpu.SemaphoreType.DMA((8,)),
            ],
        ),
        compiler_params=pltpu.CompilerParams(vmem_limit_bytes=VMEM),
        cost_estimate=pl.CostEstimate(flops=7_000_000_000, bytes_accessed=26_000_000, transcendentals=13_000_000),
        name="attend",
    )(tab, q_all, ck, cv, pk, pv, sk, sv, prev)


def merge(dst, *srcs):
    def lse_of(ref):
        t = ref[HD:HD + 16, :].astype(F32)
        return t[0:1] + t[1:2] + t[2:3]

    lses = [lse_of(r) for r in srcs]
    top = functools.reduce(jnp.maximum, lses)
    ws = [jnp.exp2(v - top) for v in lses]
    total = functools.reduce(lambda a, b: a + b, ws)
    inv = 1.0 / total
    ws = [w * inv for w in ws]
    lse = top + jnp.log2(total)
    rows = 32

    def body(r, carry):
        sl = pl.ds(pl.multiple_of(r * rows, rows), rows)
        out = ws[0] * srcs[0][sl, :].astype(F32)
        for w, ref in zip(ws[1:], srcs[1:]):
            out = out + w * ref[sl, :].astype(F32)
        dst[sl, :] = out.astype(BF16)
        return carry

    lax.fori_loop(0, HD // rows, body, 0)
    hi = lse.astype(BF16).astype(F32)
    mid = (lse - hi).astype(BF16).astype(F32)
    low = lse - hi - mid
    row = lax.broadcasted_iota(jnp.int32, (16, lse.shape[1]), 0)
    dst[HD:HD + 16, :] = jnp.where(row == 0, hi, jnp.where(row == 1, mid, jnp.where(row == 2, low, 0.0))).astype(BF16)


NCH = 4
SECOND = (2, 1, 3, 0)


def finish_kernel(part_ref, wo_ref, won_ref, out_ref,
                  loc, recv, att, attz, hb, relay, w, acc, tile, zrelay,
                  load_sem, r_send, r_recv, wo_send, wo_recv, w_sem,
                  a_send, a_recv, b_send, b_recv, s_send, s_recv, t_send, t_recv, home_sem):
    z, x, c, y = position()
    partner = dev(z, x, 1 - c, y)
    zp, zm = dev(z + 1, x, c, y), dev(z - 1, x, c, y)
    yp, ym = dev(z, x, c, y + 1), dev(z, x, c, y - 1)
    barrier = pltpu.get_barrier_semaphore()
    for target in (zp, zm, dev(z, x + 1, c, y), dev(z, x - 1, c, y), yp, ym, partner):
        pl.semaphore_signal(barrier, inc=1, device_id=target, device_id_type=MESH)

    def remote(src, dst, ssem, rsem, target):
        return pltpu.make_async_remote_copy(
            src_ref=src, dst_ref=dst, send_sem=ssem, recv_sem=rsem, device_id=target, device_id_type=MESH)

    def step(h, a, b):
        return (a, b) if h == 0 else (b, a)

    def to(h, a, b):
        dz, dx = step(h, a, b)
        return dev(z + dz, x + dx, c, y)

    loads = {}
    for k in (0, 1):
        for a in (2, 1, 3, 0):
            for b in SECOND:
                for h in (0, 1):
                    dz, dx = step(h, a, b)
                    slot = ((z + dz) % 4) * 4 + (x + dx) % 4
                    cp = pltpu.make_async_copy(part_ref.at[slot, k, h], loc.at[k * 2 + h, a * 4 + b], load_sem.at[len(loads)])
                    cp.start()
                    loads[k, h, a, b] = cp
    w_loads = [
        pltpu.make_async_copy(wo_ref, w.at[0], w_sem.at[0]),
        pltpu.make_async_copy(won_ref.at[1], w.at[1], w_sem.at[1]),
        pltpu.make_async_copy(won_ref.at[0], w.at[3], w_sem.at[2]),
    ]
    for cp in w_loads:
        cp.start()
    pl.semaphore_wait(barrier, 7)

    quarter = wo_ref.shape[0] // 4
    wo_copies = []

    def send_wo(src, n, target):
        rows = pl.ds(pl.multiple_of(c * (2 * quarter) + (n % 2) * quarter, quarter), quarter)
        cp = remote(src.at[rows], w.at[2, rows], wo_send.at[n], wo_recv.at[n], target)
        cp.start()
        wo_copies.append(cp)

    send_wo(won_ref.at[0], 0, yp)
    send_wo(won_ref.at[1], 1, ym)

    quart = loc.shape[-1] // 2
    copies = {}

    def send(key, src, target):
        n = len(copies)
        cp = remote(src, recv.at[n], r_send.at[n], r_recv.at[n], target)
        cp.start()
        copies[key] = (cp, n)

    def got(key):
        cp, n = copies[key]
        cp.wait_recv()
        return recv.at[n]

    def piece(k, h, a, b, q):
        return loc.at[k * 2 + h, a * 4 + b, :, q * quart:(q + 1) * quart]

    def first_sends(k, b):
        for h in (0, 1):
            loads[k, h, 2, b].wait()
            send((k, h, b, "op"), piece(k, h, 2, b, 0), to(h, 1, 0))
            send((k, h, b, "om"), piece(k, h, 2, b, 1), to(h, -1, 0))

    def first_raw(k, b):
        for h in (0, 1):
            loads[k, h, 1, b].wait()
            send((k, h, b, "p1"), piece(k, h, 1, b, 1), to(h, 1, 0))
            loads[k, h, 3, b].wait()
            send((k, h, b, "m0"), piece(k, h, 3, b, 0), to(h, -1, 0))

    def first_sums(k, b):
        for h in (0, 1):
            r = got((k, h, b, "op"))
            merge(piece(k, h, 1, b, 0), piece(k, h, 1, b, 0), r)
            send((k, h, b, "p0"), piece(k, h, 1, b, 0), to(h, 1, 0))
            r = got((k, h, b, "om"))
            merge(piece(k, h, 3, b, 1), piece(k, h, 3, b, 1), r)
            send((k, h, b, "m1"), piece(k, h, 3, b, 1), to(h, -1, 0))

    def second_sends(k, b):
        for h in (0, 1):
            loads[k, h, 0, b].wait()
            for q in (1, 0):
                p = got((k, h, b, "p%d" % q))
                m = got((k, h, b, "m%d" % q))
                merge(piece(k, h, 0, b, q), piece(k, h, 0, b, q), p, m)
            if b == 2:
                send((k, h, "op"), piece(k, h, 0, 2, 0), to(h, 0, 1))
                send((k, h, "om"), piece(k, h, 0, 2, 1), to(h, 0, -1))
            if b == 1:
                send((k, h, "p1"), piece(k, h, 0, 1, 1), to(h, 0, 1))
            if b == 3:
                send((k, h, "m0"), piece(k, h, 0, 3, 0), to(h, 0, -1))

    def second_sums(k):
        for h in (0, 1):
            r = got((k, h, "op"))
            merge(piece(k, h, 0, 1, 0), piece(k, h, 0, 1, 0), r)
            send((k, h, "p0"), piece(k, h, 0, 1, 0), to(h, 0, 1))
            r = got((k, h, "om"))
            merge(piece(k, h, 0, 3, 1), piece(k, h, 0, 3, 1), r)
            send((k, h, "m1"), piece(k, h, 0, 3, 1), to(h, 0, -1))

    def last_sums(k):
        for h in (0, 1):
            for q in (1, 0):
                p = got((k, h, "p%d" % q))
                m = got((k, h, "m%d" % q))
                own = piece(k, h, 0, 0, q)
                merge(own, own, p, m)
                for g in range(quart // HD):
                    col = (h * 2 + q) * quart + g * HD
                    att[k, :, col:col + HD] = own[0:HD, g * HD:(g + 1) * HD].T

    half = BLK // 2
    lo, hi = pl.ds(0, half), pl.ds(half, half)

    def ring_of(k):
        n = k * 4
        return [
            remote(att.at[k], attz.at[k, 3], a_send.at[n], a_recv.at[n], zp),
            remote(att.at[k], attz.at[k, 1], a_send.at[n + 1], a_recv.at[n + 1], zm),
            remote(attz.at[k, 3, lo], attz.at[k, 2, lo], a_send.at[n + 2], a_recv.at[n + 2], zp),
            remote(attz.at[k, 1, hi], attz.at[k, 2, hi], a_send.at[n + 3], a_recv.at[n + 3], zm),
        ]

    def spread_of(k, src):
        n = k * 6
        return [
            remote(src, hb.at[k, 3], b_send.at[n], b_recv.at[n], yp),
            remote(src, hb.at[k, 1], b_send.at[n + 1], b_recv.at[n + 1], ym),
            remote(src.at[lo], relay.at[k, 0], b_send.at[n + 2], b_recv.at[n + 2], yp),
            remote(src.at[hi], relay.at[k, 1], b_send.at[n + 3], b_recv.at[n + 3], ym),
            remote(relay.at[k, 0], hb.at[k, 2, lo], b_send.at[n + 4], b_recv.at[n + 4], yp),
            remote(relay.at[k, 1], hb.at[k, 2, hi], b_send.at[n + 5], b_recv.at[n + 5], ym),
        ]

    def spread(k, dz):
        src = att.at[k] if dz == 0 else attz.at[k, dz]
        d = (dz - y + 4) % 4

        @pl.when(d == 0)
        def _():
            hb[k, 0] = src[...]

        @pl.when(d == 1)
        def _():
            spread_of(k, src)[0].start()

        @pl.when(d == 3)
        def _():
            spread_of(k, src)[1].start()

        @pl.when(d == 2)
        def _():
            spread_of(k, src)[2].start()
            spread_of(k, src)[3].start()

    def rows_out(k):
        r = ring_of(k)
        r[0].start()
        r[1].start()
        spread(k, 0)

    def rows_next(k):
        r = ring_of(k)
        r[0].wait_recv()
        r[2].start()
        spread(k, 3)
        r[1].wait_recv()
        r[3].start()
        spread(k, 1)

    def rows_far(k):
        r = ring_of(k)
        r[2].wait_recv()
        r[3].wait_recv()
        spread(k, 2)

    def rows_relay(k):
        sp = spread_of(k, att.at[k])
        for n in (0, 1):
            sp[2 + n].wait_recv()
            sp[4 + n].start()

    cols = wo_ref.shape[1]
    width = cols // NCH

    def term(k, r, first):
        def one(n, carry):
            sl = pl.ds(pl.multiple_of(n * 256, 256), 256)
            v = jnp.dot(hb[k, r], w[r, :, sl], preferred_element_type=F32)
            acc[k, :, sl] = v if first else acc[k, :, sl] + v
            return carry
        lax.fori_loop(0, cols // 256, one, 0)

    def terms(k):
        sp = spread_of(k, att.at[k])
        if k == 0:
            w_loads[0].wait()
        term(k, 0, True)
        sp[0].wait_recv()
        if k == 0:
            w_loads[2].wait()
        term(k, 3, False)
        sp[1].wait_recv()
        if k == 0:
            w_loads[1].wait()
        term(k, 1, False)
        sp[4].wait_recv()
        sp[5].wait_recv()

    def region(k, f, ch, rows=None):
        sl = pl.ds(pl.multiple_of(((f + 8) % 4) * cols + ch * width, width), width)
        first, size = (k * BLK, BLK) if rows is None else (k * BLK + rows * half, half)
        return out_ref.at[pl.ds(first, size), sl]

    def shifts(k, ch):
        n = (k * NCH + ch) * 5
        src = tile.at[k, ch]
        return [
            remote(src, region(k, z, ch), s_send.at[n], s_recv.at[n], zp),
            remote(src, region(k, z, ch), s_send.at[n], s_recv.at[n], zm),
            remote(src.at[lo], zrelay.at[k, ch, 0], s_send.at[n + 1], s_recv.at[n + 1], zp),
            remote(src.at[hi], zrelay.at[k, ch, 1], s_send.at[n + 2], s_recv.at[n + 2], zm),
            remote(zrelay.at[k, ch, 0], region(k, z - 1, ch, 0), s_send.at[n + 3], s_recv.at[n + 3], zp),
            remote(zrelay.at[k, ch, 1], region(k, z + 1, ch, 1), s_send.at[n + 4], s_recv.at[n + 4], zm),
        ]

    def home(k, ch):
        return pltpu.make_async_copy(tile.at[k, ch], region(k, z, ch), home_sem.at[k * NCH + ch])

    def bcast(k, ch):
        n = (k * NCH + ch) * 4
        mine = region(k, z - y, ch)
        up = region(k, z - y + 1, ch, 0)
        down = region(k, z - y - 1, ch, 1)
        return [
            remote(mine, mine, t_send.at[n], t_recv.at[n], yp),
            remote(mine, mine, t_send.at[n + 1], t_recv.at[n + 1], ym),
            remote(up, up, t_send.at[n + 2], t_recv.at[n + 2], yp),
            remote(down, down, t_send.at[n + 3], t_recv.at[n + 3], ym),
        ]

    def tile_out(k, ch):
        for n in range(width // 256):
            sl = slice(ch * width + n * 256, ch * width + (n + 1) * 256)
            v = acc[k, :, sl] + jnp.dot(hb[k, 2], w[2, :, sl], preferred_element_type=F32)
            tile[k, ch, :, n * 256:(n + 1) * 256] = v.astype(BF16)

        @pl.when(y == 0)
        def _():
            home(k, ch).start()

        @pl.when(y == 1)
        def _():
            shifts(k, ch)[0].start()

        @pl.when(y == 3)
        def _():
            shifts(k, ch)[1].start()

        @pl.when(y == 2)
        def _():
            shifts(k, ch)[2].start()
            shifts(k, ch)[3].start()

    def tile_relay(k, ch):
        @pl.when(y == 2)
        def _():
            sr = shifts(k, ch)
            sr[2].wait_recv()
            sr[4].start()
            sr[3].wait_recv()
            sr[5].start()

    def tile_home(k, ch):
        @pl.when(y == 0)
        def _():
            home(k, ch).wait()

        @pl.when(y % 2 == 1)
        def _():
            shifts(k, ch)[0].wait_recv()

        @pl.when(y == 2)
        def _():
            se = shifts(k, ch)
            se[4].wait_recv()
            se[5].wait_recv()

        b = bcast(k, ch)
        b[0].start()
        b[1].start()

    def tile_onward(k, ch):
        b = bcast(k, ch)
        b[0].wait_recv()
        b[2].start()
        b[1].wait_recv()
        b[3].start()

    for b in SECOND:
        first_sends(0, b)
    for b in SECOND:
        first_raw(0, b)
    for b in SECOND:
        first_sums(0, b)
    for b in SECOND:
        first_sends(1, b)
        second_sends(0, b)
    for n in (0, 1):
        wo_copies[n].wait_recv()
        send_wo(w.at[2], 2 + n, partner)
    second_sums(0)
    for b in SECOND:
        first_raw(1, b)
    last_sums(0)
    rows_out(0)
    for b in SECOND:
        first_sums(1, b)
    rows_next(0)
    second_sends(1, 2)
    second_sends(1, 1)
    rows_far(0)
    second_sends(1, 3)
    second_sends(1, 0)
    rows_relay(0)
    second_sums(1)
    terms(0)
    last_sums(1)
    rows_out(1)
    wo_copies[2].wait_recv()
    wo_copies[3].wait_recv()
    for ch in range(NCH):
        tile_out(0, ch)
    rows_next(1)
    for ch in range(NCH):
        tile_relay(0, ch)
    tile_home(0, 0)
    tile_home(0, 1)
    rows_far(1)
    tile_home(0, 2)
    tile_home(0, 3)
    rows_relay(1)
    tile_onward(0, 0)
    terms(1)
    for ch in range(NCH):
        tile_out(1, ch)
    tile_onward(0, 1)
    tile_onward(0, 2)
    tile_onward(0, 3)
    for t in range(NCH + 2):
        if t < NCH:
            tile_relay(1, t)
        if 1 <= t < NCH + 1:
            tile_home(1, t - 1)
        if 2 <= t:
            tile_onward(1, t - 2)
    for k in (0, 1):
        for ch in range(NCH):
            b = bcast(k, ch)
            b[2].wait_recv()
            b[3].wait_recv()
            for cp in b:
                cp.wait_send()

            @pl.when(y % 2 == 1)
            def _():
                shifts(k, ch)[0].wait_send()

            @pl.when(y == 2)
            def _():
                for cp in shifts(k, ch)[2:]:
                    cp.wait_send()
        for cp in ring_of(k) + spread_of(k, att.at[k]):
            cp.wait_send()
    for cp in wo_copies:
        cp.wait_send()
    for cp, _ in copies.values():
        cp.wait_send()


N_REDUCE = 120


def finish(part, wo, won):
    rows, lanes = part.shape[-2:]
    depth, cols = wo.shape
    anyspec = pl.BlockSpec(memory_space=pl.ANY)
    sem = pltpu.SemaphoreType.DMA
    return pl.pallas_call(
        finish_kernel,
        out_shape=jax.ShapeDtypeStruct((2 * BLK, 4 * cols), BF16),
        in_specs=[anyspec] * 3,
        out_specs=anyspec,
        scratch_shapes=[
            pltpu.VMEM((4, 16, rows, lanes), BF16),
            pltpu.VMEM((N_REDUCE, rows, lanes // 2), BF16),
            pltpu.VMEM((2, BLK, depth), BF16),
            pltpu.VMEM((2, 4, BLK, depth), BF16),
            pltpu.VMEM((2, 4, BLK, depth), BF16),
            pltpu.VMEM((2, 2, BLK // 2, depth), BF16),
            pltpu.VMEM((4, depth, cols), BF16),
            pltpu.VMEM((2, BLK, cols), F32),
            pltpu.VMEM((2, NCH, BLK, cols // NCH), BF16),
            pltpu.VMEM((2, NCH, 2, BLK // 2, cols // NCH), BF16),
            sem((64,)), sem((N_REDUCE,)), sem((N_REDUCE,)), sem((4,)), sem((4,)), sem((3,)),
            sem((8,)), sem((8,)), sem((12,)), sem((12,)),
            sem((10 * NCH,)), sem((10 * NCH,)), sem((8 * NCH,)), sem((8 * NCH,)), sem((2 * NCH,)),
        ],
        compiler_params=pltpu.CompilerParams(
            collective_id=1, has_side_effects=True, vmem_limit_bytes=VMEM),
        name="finish",
    )(part, wo, won)


def turn_kernel(q_ref, out_ref):
    for color in range(2):
        for g in range(q_ref.shape[1] // HD):
            out_ref[color, :, g * BLK:(g + 1) * BLK] = q_ref[color * BLK:(color + 1) * BLK, g * HD:(g + 1) * HD].T


def turn(queries):
    return pl.pallas_call(
        turn_kernel,
        out_shape=jax.ShapeDtypeStruct((2, HD, queries.shape[1]), BF16),
        in_specs=[pl.BlockSpec(memory_space=pltpu.VMEM)],
        out_specs=pl.BlockSpec(memory_space=pltpu.VMEM),
        compiler_params=pltpu.CompilerParams(vmem_limit_bytes=VMEM),
        name="turn",
    )(queries)


def request_table(block_slot, pattern, core, cb_local):
    slot_ids = block_slot[pattern]
    owners = slot_ids // cb_local
    chips = owners // 2
    rel = jnp.where(owners % 2 == core, 0, cb_local) + slot_ids % cb_local
    entry = jnp.arange(pattern.shape[1])
    same = (chips[:, :, None] == chips[:, None, :]) & (entry[None, :] < entry[:, None])[None]
    rank = jnp.sum(same.astype(jnp.int32), axis=2)
    lane = jnp.arange(16)
    hit = (chips[None, :, None, :] == jnp.arange(16)[:, None, None, None])
    pick = hit & (rank[None, :, None, :] == lane[None, None, :, None])
    value = jnp.where(lane[None, None, :, None] == 15, hit.astype(jnp.int32), jnp.where(pick, rel[None, :, None, :], 0))
    table = jnp.sum(value, axis=3).reshape(16, 1, 32)
    return jnp.pad(table, ((0, 0), (0, 0), (0, 96)))


def body(queries, span_k, span_v, cache_k, cache_v, block_slot, pattern, wo):
    core = lax.axis_index("seq") % 2
    tab = request_table(block_slot, pattern, core, cache_k.shape[0])
    q = turn(queries)
    q_all, pk, pv, prev, tab_all, won = gather_queries(q, cache_k, cache_v, span_k, span_v, tab, wo)
    part = attend(tab_all, q_all, cache_k, cache_v, pk, pv, span_k, span_v, prev)
    return finish(part, wo, won)


def solution(mesh):
    return jax.shard_map(
        body,
        mesh=mesh,
        in_specs=(
            P(("fsdp", "seq"), "head"),
            P(("fsdp", "seq"), "head"),
            P(("fsdp", "seq"), "head"),
            P(("fsdp", "seq"), None, "head"),
            P(("fsdp", "seq"), None, "head"),
            P(),
            P(("fsdp", "seq"), None),
            P("head", "fsdp"),
        ),
        out_specs=P(("fsdp", "seq"), None),
        check_vma=False,
    )
```

```python
import functools

import jax
import jax.numpy as jnp
from jax import lax
from jax.experimental import pallas as pl
from jax.experimental.pallas import tpu as pltpu
from jax.sharding import PartitionSpec as P

HD = 128
BLK = 128
NEG = -1e30
VMEM = 62 * 2**20
MESH = pl.DeviceIdType.MESH
BF16 = jnp.bfloat16
F32 = jnp.float32
LOG2E = 1.4426950408889634


def position():
    z = lax.axis_index("fsdp")
    s = lax.axis_index("seq")
    y = lax.axis_index("head")
    return z, s // 2, s % 2, y


def dev(z, x, c, y):
    return ((z + 4) % 4, ((x + 4) % 4) * 2 + c, (y + 4) % 4)


def gather_kernel(q_ref, ck_ref, cv_ref, sk_ref, sv_ref, tab_ref, wo_ref,
                  qall_ref, pk_ref, pv_ref, prev_ref, taball_ref, won_ref,
                  send_sem, recv_sem, loc_sem):
    z, x, c, y = position()
    far_z, far_x = (z, x + jnp.where(c == 0, -1, 1))
    wrap = jnp.where(c == 0, jnp.where(x == 0, -1, 0), jnp.where(x == 3, 1, 0))
    far_z = far_z + wrap

    barrier = pltpu.get_barrier_semaphore()
    for off in range(1, 16):
        pl.semaphore_signal(barrier, inc=1, device_id=dev(z + off // 4, x + off % 4, c, y), device_id_type=MESH)
    pl.semaphore_signal(barrier, inc=1, device_id=dev(z, x, 1 - c, y), device_id_type=MESH)
    pl.semaphore_signal(barrier, inc=1, device_id=dev(far_z, far_x, 1 - c, y), device_id_type=MESH)
    for d in (1, -1):
        pl.semaphore_signal(barrier, inc=1, device_id=dev(z, x, c, y + d), device_id_type=MESH)
    pl.semaphore_wait(barrier, 19)

    copies = []

    def send(src, dst, target):
        k = len(copies)
        cp = pltpu.make_async_remote_copy(
            src_ref=src, dst_ref=dst, send_sem=send_sem.at[k], recv_sem=recv_sem.at[k],
            device_id=target, device_id_type=MESH)
        cp.start()
        copies.append(cp)
        return cp

    def slot(dz, dx):
        return ((z + dz + 4) % 4) * 4 + (x + dx + 4) % 4

    here = slot(0, 0)
    tables = []
    for off in range(1, 16):
        dz, dx = off // 4, off % 4
        tables.append(send(tab_ref.at[slot(dz, dx)], taball_ref.at[here], dev(z + dz, x + dx, c, y)))
    nxt_x = x + jnp.where(c == 0, 0, 1)
    nxt_z = z + jnp.where((c == 1) & (x == 3), 1, 0)
    nxt = dev(nxt_z, nxt_x, 1 - c, y)
    send(sk_ref.at[pl.ds(BLK, BLK)], prev_ref.at[0], nxt)
    send(sv_ref.at[pl.ds(BLK, BLK)], prev_ref.at[1], nxt)

    def step(color, major, minor):
        return (minor, major) if color == 0 else (major, minor)

    def chunk(color, a, b, half=None):
        dz, dx = step(color, a, b)
        ref = qall_ref.at[slot(dz, dx), color]
        if half is None:
            return ref
        return ref.at[pl.ds(half * (BLK // 2), BLK // 2)]

    def to(color, a, b):
        dz, dx = step(color, a, b)
        return dev(z + dz, x + dx, c, y)

    ring = {}

    def own(color):
        mine, dst = q_ref.at[color], qall_ref.at[here, color]
        for d in (1, -1):
            ring[color, "a", d] = send(mine, dst, to(color, d, 0))
        for d in (1, -1):
            ring[color, "b", 0, d] = send(mine, dst, to(color, 0, d))

    own(0)
    own(1)
    depth = wo_ref.shape[0] // (2 * WO_CHUNKS)

    def share(n):
        return pl.ds(pl.multiple_of((c * WO_CHUNKS + n) * depth, depth), depth)

    wo_in = []
    for n in range(WO_CHUNKS):
        for i, d in ((0, 1), (1, -1)):
            wo_in.append((i, n, send(wo_ref.at[share(n)], won_ref.at[i, share(n)], dev(z, x, c, y + d))))

    def hand_over(count):
        for _ in range(count):
            i, n, cp = wo_in[len(handed)]
            handed.append(cp)
            cp.wait_recv()
            send(won_ref.at[i, share(n)], won_ref.at[i, share(n)], partner)

    handed = []
    partner = dev(z, x, 1 - c, y)
    send(ck_ref, pk_ref, partner)
    send(cv_ref, pv_ref, partner)
    locals_ = [pltpu.make_async_copy(q_ref, qall_ref.at[here], loc_sem.at[0]),
               pltpu.make_async_copy(tab_ref.at[here], taball_ref.at[here], loc_sem.at[1])]
    for cp in locals_:
        cp.start()

    for d in (1, -1):
        for color in (0, 1):
            ring[color, "a", d].wait_recv()
            half = 0 if d == 1 else 1
            part = chunk(color, -d, 0, half)
            ring[color, "o", d] = send(part, part, to(color, d, 0))
            whole = chunk(color, -d, 0)
            for e in (1, -1):
                ring[color, "b", -d, e] = send(whole, whole, to(color, 0, e))
    for d in (1, -1):
        for color in (0, 1):
            ring[color, "b", 0, d].wait_recv()
            part = chunk(color, 0, -d, 0 if d == 1 else 1)
            ring[color, "c", 0, d] = send(part, part, to(color, 0, d))
    for color in (0, 1):
        ring[color, "o", 1].wait_recv()
        ring[color, "o", -1].wait_recv()
        whole = chunk(color, 2, 0)
        for e in (1, -1):
            ring[color, "b", 2, e] = send(whole, whole, to(color, 0, e))
    hand_over(2)
    for a in (-1, 1, 2):
        hand_over(2)
        for d in (1, -1):
            for color in (0, 1):
                ring[color, "b", a, d].wait_recv()
                part = chunk(color, a, -d, 0 if d == 1 else 1)
                ring[color, "c", a, d] = send(part, part, to(color, 0, d))
    hand_over(len(wo_in) - len(handed))
    waited = {id(v) for k, v in ring.items() if k[1] != "c"} | {id(cp) for cp in handed}
    for cp in copies:
        if id(cp) not in waited:
            cp.wait_recv()
    for cp in copies:
        cp.wait_send()
    for cp in locals_:
        cp.wait()


WO_CHUNKS = 4
N_GATHER = 15 + 2 + 8 + 2 + 4 + 8 + 4 + 4 + 12 + 4 * WO_CHUNKS


def gather_queries(q, ck, cv, sk, sv, tab, wo):
    anyspec = pl.BlockSpec(memory_space=pl.ANY)
    return pl.pallas_call(
        gather_kernel,
        out_shape=(
            jax.ShapeDtypeStruct((16, 2, BLK, q.shape[-1]), BF16),
            jax.ShapeDtypeStruct(ck.shape, BF16),
            jax.ShapeDtypeStruct(cv.shape, BF16),
            jax.ShapeDtypeStruct((2, BLK, HD), BF16),
            jax.ShapeDtypeStruct(tab.shape, jnp.int32),
            jax.ShapeDtypeStruct((2,) + wo.shape, BF16),
        ),
        in_specs=[anyspec] * 7,
        out_specs=[anyspec] * 6,
        scratch_shapes=[
            pltpu.SemaphoreType.DMA((N_GATHER,)),
            pltpu.SemaphoreType.DMA((N_GATHER,)),
            pltpu.SemaphoreType.DMA((2,)),
        ],
        compiler_params=pltpu.CompilerParams(collective_id=0, has_side_effects=True, vmem_limit_bytes=VMEM),
        name="gather_queries",
    )(q, ck, cv, sk, sv, tab, wo)


def attend_kernel(tab_ref, q_ref, ck_ref, cv_ref, pk_ref, pv_ref, sk_ref, sv_ref, prev_ref, out_ref,
                  kall, vall, span, sbuf, pbuf, m_s, l_s, acc, sems):
    i = pl.program_id(0)
    z, x, c, y = position()
    chip = i // 2
    color = i % 2
    mine = chip == z * 4 + x

    @pl.when(i == 0)
    def _():
        loads = [
            pltpu.make_async_copy(ck_ref, kall.at[pl.ds(0, 64)], sems.at[0]),
            pltpu.make_async_copy(pk_ref, kall.at[pl.ds(64, 64)], sems.at[1]),
            pltpu.make_async_copy(cv_ref, vall.at[pl.ds(0, 64)], sems.at[2]),
            pltpu.make_async_copy(pv_ref, vall.at[pl.ds(64, 64)], sems.at[3]),
            pltpu.make_async_copy(prev_ref.at[0], span.at[0, pl.ds(0, BLK)], sems.at[4]),
            pltpu.make_async_copy(prev_ref.at[1], span.at[1, pl.ds(0, BLK)], sems.at[5]),
            pltpu.make_async_copy(sk_ref, span.at[0, pl.ds(BLK, 2 * BLK)], sems.at[6]),
            pltpu.make_async_copy(sv_ref, span.at[1, pl.ds(BLK, 2 * BLK)], sems.at[7]),
        ]
        for cp in loads:
            cp.start()
        for cp in loads:
            cp.wait()

    heads = q_ref.shape[-1] // HD
    m_s[...] = jnp.full_like(m_s, NEG)
    l_s[...] = jnp.zeros_like(l_s)
    acc[...] = jnp.zeros_like(acc)
    scale = LOG2E / (HD ** 0.5)
    width = 256

    def pair(keys, values, bias):
        rows = keys.shape[0]
        spans = [slice(t * width, (t + 1) * width) for t in range(heads * HD // width)]
        tops = []
        for cols in spans:
            s = jnp.dot(keys, q_ref[0, 0, :, cols], preferred_element_type=F32)
            if bias is not None:
                s = s + bias
            sbuf[0:rows, cols] = s
            tops.append(jnp.maximum(m_s[:, cols], jnp.max(s, axis=0, keepdims=True)))
        olds = []
        for cols, top in zip(spans, tops):
            old = jnp.exp2((m_s[:, cols] - top) * scale)
            p = jnp.exp2((sbuf[0:rows, cols] - top) * scale)
            pbuf[0:rows, cols] = p.astype(BF16)
            m_s[:, cols] = top
            l_s[:, cols] = l_s[:, cols] * old + jnp.sum(p, axis=0, keepdims=True)
            olds.append(old)
        for cols, old in zip(spans, olds):
            acc[:, cols] = acc[:, cols] * old + lax.dot_general(
                values, pbuf[0:rows, cols], (((0,), (0,)), ((), ())), preferred_element_type=F32)

    count = tab_ref[chip, 0, color * 16 + 15]
    base = color * 16

    def both(j, carry):
        i0 = tab_ref[chip, 0, base + 2 * j]
        i1 = tab_ref[chip, 0, base + 2 * j + 1]
        keys = jnp.concatenate([kall[i0], kall[i1]], axis=0)
        values = jnp.concatenate([vall[i0], vall[i1]], axis=0)
        pair(keys, values, None)
        return carry

    lax.fori_loop(0, count // 2, both, 0)

    @pl.when(count % 2 == 1)
    def _():
        i0 = tab_ref[chip, 0, base + count - 1]
        pair(kall[i0], vall[i0], None)

    @pl.when(mine)
    def _():
        rows = pl.ds(pl.multiple_of(color * BLK, BLK), 2 * BLK)
        key = lax.broadcasted_iota(jnp.int32, (2 * BLK, width), 0)
        tok = lax.broadcasted_iota(jnp.int32, (2 * BLK, width), 1) % BLK
        first = (z * 8 + x * 2 + c) * 2 + color == 0
        low = jnp.where(first, BLK, 0)
        allowed = (key >= low) & (key - BLK <= tok)
        pair(span[0, rows, :], span[1, rows, :], jnp.where(allowed, 0.0, 2 * NEG))

    some = l_s[...] > 0
    total = jnp.where(some, l_s[...], 1.0)
    lse = m_s[...] * scale + jnp.log2(total)
    hi = lse.astype(BF16)
    rest = lse - hi.astype(F32)
    mid = rest.astype(BF16)
    low_ = (rest - mid.astype(F32)).astype(BF16)
    o = (acc[...] / total).astype(BF16)
    row = lax.broadcasted_iota(jnp.int32, (16, lse.shape[1]), 0)
    tail = jnp.where(row == 0, hi.astype(F32), jnp.where(row == 1, mid.astype(F32), jnp.where(row == 2, low_.astype(F32), 0.0))).astype(BF16)
    half = lse.shape[1] // 2
    for h in range(2):
        out_ref[0, 0, h, 0:HD, :] = o[:, h * half:(h + 1) * half]
        out_ref[0, 0, h, HD:HD + 16, :] = tail[:, h * half:(h + 1) * half]


def attend(tab, q_all, ck, cv, pk, pv, sk, sv, prev):
    width = q_all.shape[-1]
    anyspec = pl.BlockSpec(memory_space=pl.ANY)
    return pl.pallas_call(
        attend_kernel,
        out_shape=jax.ShapeDtypeStruct((16, 2, 2, HD + 16, width // 2), BF16),
        grid_spec=pltpu.PrefetchScalarGridSpec(
            num_scalar_prefetch=1,
            grid=(32,),
            in_specs=[pl.BlockSpec((1, 1, BLK, width), lambda i, t: (i // 2, i % 2, 0, 0))] + [anyspec] * 7,
            out_specs=pl.BlockSpec((1, 1, 2, HD + 16, width // 2), lambda i, t: (i // 2, i % 2, 0, 0, 0)),
            scratch_shapes=[
                pltpu.VMEM((128, BLK, HD), BF16),
                pltpu.VMEM((128, BLK, HD), BF16),
                pltpu.VMEM((2, 3 * BLK, HD), BF16),
                pltpu.VMEM((2 * BLK, width), F32),
                pltpu.VMEM((2 * BLK, width), BF16),
                pltpu.VMEM((1, width), F32),
                pltpu.VMEM((1, width), F32),
                pltpu.VMEM((HD, width), F32),
                pltpu.SemaphoreType.DMA((8,)),
            ],
        ),
        compiler_params=pltpu.CompilerParams(
            vmem_limit_bytes=VMEM),
        cost_estimate=pl.CostEstimate(flops=7_000_000_000, bytes_accessed=26_000_000, transcendentals=13_000_000),
        name="attend",
    )(tab, q_all, ck, cv, pk, pv, sk, sv, prev)


def merge(dst, *srcs):
    def lse_of(ref):
        t = ref[HD:HD + 16, :].astype(F32)
        return t[0:1] + t[1:2] + t[2:3]

    lses = [lse_of(r) for r in srcs]
    top = functools.reduce(jnp.maximum, lses)
    ws = [jnp.exp2(v - top) for v in lses]
    total = functools.reduce(lambda a, b: a + b, ws)
    inv = 1.0 / total
    ws = [w * inv for w in ws]
    lse = top + jnp.log2(total)
    rows = 32

    def body(r, carry):
        sl = pl.ds(pl.multiple_of(r * rows, rows), rows)
        out = ws[0] * srcs[0][sl, :].astype(F32)
        for w, ref in zip(ws[1:], srcs[1:]):
            out = out + w * ref[sl, :].astype(F32)
        dst[sl, :] = out.astype(BF16)
        return carry

    lax.fori_loop(0, HD // rows, body, 0)
    hi = lse.astype(BF16).astype(F32)
    mid = (lse - hi).astype(BF16).astype(F32)
    low = lse - hi - mid
    row = lax.broadcasted_iota(jnp.int32, (16, lse.shape[1]), 0)
    dst[HD:HD + 16, :] = jnp.where(row == 0, hi, jnp.where(row == 1, mid, jnp.where(row == 2, low, 0.0))).astype(BF16)


NCH = 4
SECOND = (2, 1, 3, 0)


def finish_kernel(part_ref, wo_ref, won_ref, out_ref,
                  loc, recv, att, attz, hb, relay, w, acc, tile, zrelay,
                  load_sem, r_send, r_recv, wo_send, wo_recv, w_sem,
                  a_send, a_recv, b_send, b_recv, s_send, s_recv, t_send, t_recv, home_sem):
    z, x, c, y = position()
    partner = dev(z, x, 1 - c, y)
    zp, zm = dev(z + 1, x, c, y), dev(z - 1, x, c, y)
    yp, ym = dev(z, x, c, y + 1), dev(z, x, c, y - 1)
    barrier = pltpu.get_barrier_semaphore()
    for target in (zp, zm, dev(z, x + 1, c, y), dev(z, x - 1, c, y), yp, ym, partner):
        pl.semaphore_signal(barrier, inc=1, device_id=target, device_id_type=MESH)

    def remote(src, dst, ssem, rsem, target):
        return pltpu.make_async_remote_copy(
            src_ref=src, dst_ref=dst, send_sem=ssem, recv_sem=rsem, device_id=target, device_id_type=MESH)

    def step(h, a, b):
        return (a, b) if h == 0 else (b, a)

    def to(h, a, b):
        dz, dx = step(h, a, b)
        return dev(z + dz, x + dx, c, y)

    loads = {}
    for k in (0, 1):
        for a in (2, 1, 3, 0):
            for b in SECOND:
                for h in (0, 1):
                    dz, dx = step(h, a, b)
                    slot = ((z + dz) % 4) * 4 + (x + dx) % 4
                    cp = pltpu.make_async_copy(part_ref.at[slot, k, h], loc.at[k * 2 + h, a * 4 + b], load_sem.at[len(loads)])
                    cp.start()
                    loads[k, h, a, b] = cp
    w_loads = [
        pltpu.make_async_copy(wo_ref, w.at[0], w_sem.at[0]),
        pltpu.make_async_copy(won_ref.at[1], w.at[1], w_sem.at[1]),
        pltpu.make_async_copy(won_ref.at[0], w.at[3], w_sem.at[2]),
    ]
    for cp in w_loads:
        cp.start()
    pl.semaphore_wait(barrier, 7)

    quarter = wo_ref.shape[0] // 4
    wo_copies = []

    def send_wo(src, n, target):
        rows = pl.ds(pl.multiple_of(c * (2 * quarter) + (n % 2) * quarter, quarter), quarter)
        cp = remote(src.at[rows], w.at[2, rows], wo_send.at[n], wo_recv.at[n], target)
        cp.start()
        wo_copies.append(cp)

    send_wo(won_ref.at[0], 0, yp)
    send_wo(won_ref.at[1], 1, ym)

    quart = loc.shape[-1] // 2
    copies = {}

    def send(key, src, target):
        n = len(copies)
        cp = remote(src, recv.at[n], r_send.at[n], r_recv.at[n], target)
        cp.start()
        copies[key] = (cp, n)

    def got(key):
        cp, n = copies[key]
        cp.wait_recv()
        return recv.at[n]

    def piece(k, h, a, b, q):
        return loc.at[k * 2 + h, a * 4 + b, :, q * quart:(q + 1) * quart]

    def first_sends(k, b):
        for h in (0, 1):
            loads[k, h, 2, b].wait()
            send((k, h, b, "op"), piece(k, h, 2, b, 0), to(h, 1, 0))
            send((k, h, b, "om"), piece(k, h, 2, b, 1), to(h, -1, 0))

    def first_raw(k, b):
        for h in (0, 1):
            loads[k, h, 1, b].wait()
            send((k, h, b, "p1"), piece(k, h, 1, b, 1), to(h, 1, 0))
            loads[k, h, 3, b].wait()
            send((k, h, b, "m0"), piece(k, h, 3, b, 0), to(h, -1, 0))

    def first_sums(k, b):
        for h in (0, 1):
            r = got((k, h, b, "op"))
            merge(piece(k, h, 1, b, 0), piece(k, h, 1, b, 0), r)
            send((k, h, b, "p0"), piece(k, h, 1, b, 0), to(h, 1, 0))
            r = got((k, h, b, "om"))
            merge(piece(k, h, 3, b, 1), piece(k, h, 3, b, 1), r)
            send((k, h, b, "m1"), piece(k, h, 3, b, 1), to(h, -1, 0))

    def second_sends(k, b):
        for h in (0, 1):
            loads[k, h, 0, b].wait()
            for q in (1, 0):
                p = got((k, h, b, "p%d" % q))
                m = got((k, h, b, "m%d" % q))
                merge(piece(k, h, 0, b, q), piece(k, h, 0, b, q), p, m)
            if b == 2:
                send((k, h, "op"), piece(k, h, 0, 2, 0), to(h, 0, 1))
                send((k, h, "om"), piece(k, h, 0, 2, 1), to(h, 0, -1))
            if b == 1:
                send((k, h, "p1"), piece(k, h, 0, 1, 1), to(h, 0, 1))
            if b == 3:
                send((k, h, "m0"), piece(k, h, 0, 3, 0), to(h, 0, -1))

    def second_sums(k):
        for h in (0, 1):
            r = got((k, h, "op"))
            merge(piece(k, h, 0, 1, 0), piece(k, h, 0, 1, 0), r)
            send((k, h, "p0"), piece(k, h, 0, 1, 0), to(h, 0, 1))
            r = got((k, h, "om"))
            merge(piece(k, h, 0, 3, 1), piece(k, h, 0, 3, 1), r)
            send((k, h, "m1"), piece(k, h, 0, 3, 1), to(h, 0, -1))

    def last_sums(k):
        for h in (0, 1):
            for q in (1, 0):
                p = got((k, h, "p%d" % q))
                m = got((k, h, "m%d" % q))
                own = piece(k, h, 0, 0, q)
                merge(own, own, p, m)
                for g in range(quart // HD):
                    col = (h * 2 + q) * quart + g * HD
                    att[k, :, col:col + HD] = own[0:HD, g * HD:(g + 1) * HD].T

    half = BLK // 2
    lo, hi = pl.ds(0, half), pl.ds(half, half)

    def ring_of(k):
        n = k * 4
        return [
            remote(att.at[k], attz.at[k, 3], a_send.at[n], a_recv.at[n], zp),
            remote(att.at[k], attz.at[k, 1], a_send.at[n + 1], a_recv.at[n + 1], zm),
            remote(attz.at[k, 3, lo], attz.at[k, 2, lo], a_send.at[n + 2], a_recv.at[n + 2], zp),
            remote(attz.at[k, 1, hi], attz.at[k, 2, hi], a_send.at[n + 3], a_recv.at[n + 3], zm),
        ]

    def spread_of(k, src):
        n = k * 6
        return [
            remote(src, hb.at[k, 3], b_send.at[n], b_recv.at[n], yp),
            remote(src, hb.at[k, 1], b_send.at[n + 1], b_recv.at[n + 1], ym),
            remote(src.at[lo], relay.at[k, 0], b_send.at[n + 2], b_recv.at[n + 2], yp),
            remote(src.at[hi], relay.at[k, 1], b_send.at[n + 3], b_recv.at[n + 3], ym),
            remote(relay.at[k, 0], hb.at[k, 2, lo], b_send.at[n + 4], b_recv.at[n + 4], yp),
            remote(relay.at[k, 1], hb.at[k, 2, hi], b_send.at[n + 5], b_recv.at[n + 5], ym),
        ]

    def spread(k, dz):
        src = att.at[k] if dz == 0 else attz.at[k, dz]
        d = (dz - y + 4) % 4

        @pl.when(d == 0)
        def _():
            hb[k, 0] = src[...]

        @pl.when(d == 1)
        def _():
            spread_of(k, src)[0].start()

        @pl.when(d == 3)
        def _():
            spread_of(k, src)[1].start()

        @pl.when(d == 2)
        def _():
            spread_of(k, src)[2].start()
            spread_of(k, src)[3].start()

    def rows_out(k):
        r = ring_of(k)
        r[0].start()
        r[1].start()
        spread(k, 0)

    def rows_next(k):
        r = ring_of(k)
        r[0].wait_recv()
        r[2].start()
        spread(k, 3)
        r[1].wait_recv()
        r[3].start()
        spread(k, 1)

    def rows_far(k):
        r = ring_of(k)
        r[2].wait_recv()
        r[3].wait_recv()
        spread(k, 2)

    def rows_relay(k):
        sp = spread_of(k, att.at[k])
        for n in (0, 1):
            sp[2 + n].wait_recv()
            sp[4 + n].start()

    cols = wo_ref.shape[1]
    width = cols // NCH

    def term(k, r, first):
        def one(n, carry):
            sl = pl.ds(pl.multiple_of(n * 256, 256), 256)
            v = jnp.dot(hb[k, r], w[r, :, sl], preferred_element_type=F32)
            acc[k, :, sl] = v if first else acc[k, :, sl] + v
            return carry
        lax.fori_loop(0, cols // 256, one, 0)

    def terms(k):
        sp = spread_of(k, att.at[k])
        if k == 0:
            w_loads[0].wait()
        term(k, 0, True)
        sp[0].wait_recv()
        if k == 0:
            w_loads[2].wait()
        term(k, 3, False)
        sp[1].wait_recv()
        if k == 0:
            w_loads[1].wait()
        term(k, 1, False)
        sp[4].wait_recv()
        sp[5].wait_recv()

    def region(k, f, ch, rows=None):
        sl = pl.ds(pl.multiple_of(((f + 8) % 4) * cols + ch * width, width), width)
        first, size = (k * BLK, BLK) if rows is None else (k * BLK + rows * half, half)
        return out_ref.at[pl.ds(first, size), sl]

    def shifts(k, ch):
        n = (k * NCH + ch) * 5
        src = tile.at[k, ch]
        return [
            remote(src, region(k, z, ch), s_send.at[n], s_recv.at[n], zp),
            remote(src, region(k, z, ch), s_send.at[n], s_recv.at[n], zm),
            remote(src.at[lo], zrelay.at[k, ch, 0], s_send.at[n + 1], s_recv.at[n + 1], zp),
            remote(src.at[hi], zrelay.at[k, ch, 1], s_send.at[n + 2], s_recv.at[n + 2], zm),
            remote(zrelay.at[k, ch, 0], region(k, z - 1, ch, 0), s_send.at[n + 3], s_recv.at[n + 3], zp),
            remote(zrelay.at[k, ch, 1], region(k, z + 1, ch, 1), s_send.at[n + 4], s_recv.at[n + 4], zm),
        ]

    def home(k, ch):
        return pltpu.make_async_copy(tile.at[k, ch], region(k, z, ch), home_sem.at[k * NCH + ch])

    def bcast(k, ch):
        n = (k * NCH + ch) * 4
        mine = region(k, z - y, ch)
        up = region(k, z - y + 1, ch, 0)
        down = region(k, z - y - 1, ch, 1)
        return [
            remote(mine, mine, t_send.at[n], t_recv.at[n], yp),
            remote(mine, mine, t_send.at[n + 1], t_recv.at[n + 1], ym),
            remote(up, up, t_send.at[n + 2], t_recv.at[n + 2], yp),
            remote(down, down, t_send.at[n + 3], t_recv.at[n + 3], ym),
        ]

    def tile_out(k, ch):
        for n in range(width // 256):
            sl = slice(ch * width + n * 256, ch * width + (n + 1) * 256)
            v = acc[k, :, sl] + jnp.dot(hb[k, 2], w[2, :, sl], preferred_element_type=F32)
            tile[k, ch, :, n * 256:(n + 1) * 256] = v.astype(BF16)

        @pl.when(y == 0)
        def _():
            home(k, ch).start()

        @pl.when(y == 1)
        def _():
            shifts(k, ch)[0].start()

        @pl.when(y == 3)
        def _():
            shifts(k, ch)[1].start()

        @pl.when(y == 2)
        def _():
            shifts(k, ch)[2].start()
            shifts(k, ch)[3].start()

    def tile_relay(k, ch):
        @pl.when(y == 2)
        def _():
            sr = shifts(k, ch)
            sr[2].wait_recv()
            sr[4].start()
            sr[3].wait_recv()
            sr[5].start()

    def tile_home(k, ch):
        @pl.when(y == 0)
        def _():
            home(k, ch).wait()

        @pl.when(y % 2 == 1)
        def _():
            shifts(k, ch)[0].wait_recv()

        @pl.when(y == 2)
        def _():
            se = shifts(k, ch)
            se[4].wait_recv()
            se[5].wait_recv()

        b = bcast(k, ch)
        b[0].start()
        b[1].start()

    def tile_onward(k, ch):
        b = bcast(k, ch)
        b[0].wait_recv()
        b[2].start()
        b[1].wait_recv()
        b[3].start()

    for b in SECOND:
        first_sends(0, b)
    for b in SECOND:
        first_raw(0, b)
    for b in SECOND:
        first_sums(0, b)
    for b in SECOND:
        first_sends(1, b)
        second_sends(0, b)
    for n in (0, 1):
        wo_copies[n].wait_recv()
        send_wo(w.at[2], 2 + n, partner)
    second_sums(0)
    for b in SECOND:
        first_raw(1, b)
    last_sums(0)
    rows_out(0)
    for b in SECOND:
        first_sums(1, b)
    rows_next(0)
    second_sends(1, 2)
    second_sends(1, 1)
    rows_far(0)
    second_sends(1, 3)
    second_sends(1, 0)
    rows_relay(0)
    second_sums(1)
    last_sums(1)
    rows_out(1)
    terms(0)
    wo_copies[2].wait_recv()
    wo_copies[3].wait_recv()
    for ch in range(NCH):
        tile_out(0, ch)
    rows_next(1)
    for ch in range(NCH):
        tile_relay(0, ch)
    tile_home(0, 0)
    tile_home(0, 1)
    rows_far(1)
    tile_home(0, 2)
    tile_home(0, 3)
    rows_relay(1)
    tile_onward(0, 0)
    terms(1)
    for ch in range(NCH):
        tile_out(1, ch)
    tile_onward(0, 1)
    tile_onward(0, 2)
    tile_onward(0, 3)
    for t in range(NCH + 2):
        if t < NCH:
            tile_relay(1, t)
        if 1 <= t < NCH + 1:
            tile_home(1, t - 1)
        if 2 <= t:
            tile_onward(1, t - 2)
    for k in (0, 1):
        for ch in range(NCH):
            b = bcast(k, ch)
            b[2].wait_recv()
            b[3].wait_recv()
            for cp in b:
                cp.wait_send()

            @pl.when(y % 2 == 1)
            def _():
                shifts(k, ch)[0].wait_send()

            @pl.when(y == 2)
            def _():
                for cp in shifts(k, ch)[2:]:
                    cp.wait_send()
        for cp in ring_of(k) + spread_of(k, att.at[k]):
            cp.wait_send()
    for cp in wo_copies:
        cp.wait_send()
    for cp, _ in copies.values():
        cp.wait_send()


N_REDUCE = 120


def finish(part, wo, won):
    rows, lanes = part.shape[-2:]
    depth, cols = wo.shape
    anyspec = pl.BlockSpec(memory_space=pl.ANY)
    sem = pltpu.SemaphoreType.DMA
    return pl.pallas_call(
        finish_kernel,
        out_shape=jax.ShapeDtypeStruct((2 * BLK, 4 * cols), BF16),
        in_specs=[anyspec] * 3,
        out_specs=anyspec,
        scratch_shapes=[
            pltpu.VMEM((4, 16, rows, lanes), BF16),
            pltpu.VMEM((N_REDUCE, rows, lanes // 2), BF16),
            pltpu.VMEM((2, BLK, depth), BF16),
            pltpu.VMEM((2, 4, BLK, depth), BF16),
            pltpu.VMEM((2, 4, BLK, depth), BF16),
            pltpu.VMEM((2, 2, BLK // 2, depth), BF16),
            pltpu.VMEM((4, depth, cols), BF16),
            pltpu.VMEM((2, BLK, cols), F32),
            pltpu.VMEM((2, NCH, BLK, cols // NCH), BF16),
            pltpu.VMEM((2, NCH, 2, BLK // 2, cols // NCH), BF16),
            sem((64,)), sem((N_REDUCE,)), sem((N_REDUCE,)), sem((4,)), sem((4,)), sem((3,)),
            sem((8,)), sem((8,)), sem((12,)), sem((12,)),
            sem((10 * NCH,)), sem((10 * NCH,)), sem((8 * NCH,)), sem((8 * NCH,)), sem((2 * NCH,)),
        ],
        compiler_params=pltpu.CompilerParams(
            collective_id=1, has_side_effects=True, vmem_limit_bytes=VMEM),
        name="finish",
    )(part, wo, won)


def prepare_kernel(cb_local, slot_ref, pattern_ref, q_ref, tab_ref, out_ref):
    core = position()[2]
    for chip in range(16):
        for k in range(2):
            tab_ref[chip, 0, k * 16 + 15] = 0

    def one(e, carry):
        for k in range(2):
            slot = slot_ref[pattern_ref[k, e]]
            owner = slot // cb_local
            chip = owner // 2
            here = jnp.where(owner % 2 == core, 0, cb_local) + slot % cb_local
            n = tab_ref[chip, 0, k * 16 + 15]
            tab_ref[chip, 0, k * 16 + n] = here
            tab_ref[chip, 0, k * 16 + 15] = n + 1
        return carry

    lax.fori_loop(0, pattern_ref.shape[1], one, 0)
    for color in range(2):
        for g in range(q_ref.shape[1] // HD):
            out_ref[color, :, g * BLK:(g + 1) * BLK] = q_ref[color * BLK:(color + 1) * BLK, g * HD:(g + 1) * HD].T


def prepare(block_slot, pattern, queries, cb_local):
    return pl.pallas_call(
        functools.partial(prepare_kernel, cb_local),
        out_shape=(jax.ShapeDtypeStruct((16, 1, 128), jnp.int32),
                   jax.ShapeDtypeStruct((2, HD, queries.shape[1]), BF16)),
        in_specs=[pl.BlockSpec(memory_space=pltpu.SMEM)] * 2 + [pl.BlockSpec(memory_space=pltpu.VMEM)],
        out_specs=(pl.BlockSpec(memory_space=pltpu.SMEM), pl.BlockSpec(memory_space=pltpu.VMEM)),
        compiler_params=pltpu.CompilerParams(vmem_limit_bytes=VMEM),
        name="prepare",
    )(block_slot, pattern, queries)


def body(queries, span_k, span_v, cache_k, cache_v, block_slot, pattern, wo):
    tab, q = prepare(block_slot, pattern, queries, cache_k.shape[0])
    q_all, pk, pv, prev, tab_all, won = gather_queries(q, cache_k, cache_v, span_k, span_v, tab, wo)
    part = attend(tab_all, q_all, cache_k, cache_v, pk, pv, span_k, span_v, prev)
    return finish(part, wo, won)


def solution(mesh):
    return jax.shard_map(
        body,
        mesh=mesh,
        in_specs=(
            P(("fsdp", "seq"), "head"),
            P(("fsdp", "seq"), "head"),
            P(("fsdp", "seq"), "head"),
            P(("fsdp", "seq"), None, "head"),
            P(("fsdp", "seq"), None, "head"),
            P(),
            P(("fsdp", "seq"), None),
            P("head", "fsdp"),
        ),
        out_specs=P(("fsdp", "seq"), None),
        check_vma=False,
    )
```

```python
import functools

import jax
import jax.numpy as jnp
from jax import lax
from jax.experimental import pallas as pl
from jax.experimental.pallas import tpu as pltpu
from jax.sharding import PartitionSpec as P

HD = 128
BLK = 128
EXTRA = 8
WO_CHUNKS = 4
WO_LATE = ((0, 3), (1, 0))
NEG = -1e30
VMEM = 62 * 2**20
MESH = pl.DeviceIdType.MESH
BF16 = jnp.bfloat16
F32 = jnp.float32
LOG2E = 1.4426950408889634


def position():
    z = lax.axis_index("fsdp")
    s = lax.axis_index("seq")
    y = lax.axis_index("head")
    return z, s // 2, s % 2, y


def dev(z, x, c, y):
    return ((z + 4) % 4, ((x + 4) % 4) * 2 + c, (y + 4) % 4)


def gather_kernel(q_ref, ck_ref, cv_ref, sk_ref, sv_ref, tab_ref, wo_ref,
                  qall_ref, pk_ref, pv_ref, prev_ref, taball_ref, won_ref,
                  send_sem, recv_sem, loc_sem):
    z, x, c, y = position()
    far_z, far_x = (z, x + jnp.where(c == 0, -1, 1))
    wrap = jnp.where(c == 0, jnp.where(x == 0, -1, 0), jnp.where(x == 3, 1, 0))
    far_z = far_z + wrap

    barrier = pltpu.get_barrier_semaphore()
    for off in range(1, 16):
        pl.semaphore_signal(barrier, inc=1, device_id=dev(z + off // 4, x + off % 4, c, y), device_id_type=MESH)
    pl.semaphore_signal(barrier, inc=1, device_id=dev(z, x, 1 - c, y), device_id_type=MESH)
    pl.semaphore_signal(barrier, inc=1, device_id=dev(far_z, far_x, 1 - c, y), device_id_type=MESH)
    for d in (1, -1):
        pl.semaphore_signal(barrier, inc=1, device_id=dev(z, x, c, y + d), device_id_type=MESH)
    pl.semaphore_wait(barrier, 19)

    copies = []

    def send(src, dst, target):
        k = len(copies)
        cp = pltpu.make_async_remote_copy(
            src_ref=src, dst_ref=dst, send_sem=send_sem.at[k], recv_sem=recv_sem.at[k],
            device_id=target, device_id_type=MESH)
        cp.start()
        copies.append(cp)
        return cp

    def slot(dz, dx):
        return ((z + dz + 4) % 4) * 4 + (x + dx + 4) % 4

    here = slot(0, 0)
    tables = []
    for off in range(1, 16):
        dz, dx = off // 4, off % 4
        tables.append(send(tab_ref.at[slot(dz, dx)], taball_ref.at[here], dev(z + dz, x + dx, c, y)))
    nxt_x = x + jnp.where(c == 0, 0, 1)
    nxt_z = z + jnp.where((c == 1) & (x == 3), 1, 0)
    nxt = dev(nxt_z, nxt_x, 1 - c, y)
    send(sk_ref.at[pl.ds(BLK, BLK)], prev_ref.at[0], nxt)
    send(sv_ref.at[pl.ds(BLK, BLK)], prev_ref.at[1], nxt)

    def step(color, major, minor):
        return (minor, major) if color == 0 else (major, minor)

    def chunk(color, a, b, half=None):
        dz, dx = step(color, a, b)
        ref = qall_ref.at[slot(dz, dx), color]
        if half is None:
            return ref
        return ref.at[pl.ds(half * (BLK // 2), BLK // 2)]

    def to(color, a, b):
        dz, dx = step(color, a, b)
        return dev(z + dz, x + dx, c, y)

    ring = {}

    def own(color):
        mine, dst = q_ref.at[color], qall_ref.at[here, color]
        for d in (1, -1):
            ring[color, "a", d] = send(mine, dst, to(color, d, 0))
        for d in (1, -1):
            ring[color, "b", 0, d] = send(mine, dst, to(color, 0, d))

    own(0)
    own(1)
    depth = wo_ref.shape[0] // (2 * WO_CHUNKS)

    def share(n):
        return pl.ds(pl.multiple_of((c * WO_CHUNKS + n) * depth, depth), depth)

    wo_in = []
    for n in range(WO_CHUNKS):
        for i, d in ((0, 1), (1, -1)):
            if (i, n) not in WO_LATE:
                wo_in.append((i, n, send(wo_ref.at[share(n)], won_ref.at[i, share(n)], dev(z, x, c, y + d))))

    def hand_over(count):
        for _ in range(count):
            i, n, cp = wo_in[len(handed)]
            handed.append(cp)
            cp.wait_recv()
            send(won_ref.at[i, share(n)], won_ref.at[i, share(n)], partner)

    handed = []
    partner = dev(z, x, 1 - c, y)
    send(ck_ref, pk_ref, partner)
    send(cv_ref, pv_ref, partner)
    locals_ = [pltpu.make_async_copy(q_ref, qall_ref.at[here], loc_sem.at[0]),
               pltpu.make_async_copy(tab_ref.at[here], taball_ref.at[here], loc_sem.at[1])]
    for cp in locals_:
        cp.start()

    for d in (1, -1):
        for color in (0, 1):
            ring[color, "a", d].wait_recv()
            half = 0 if d == 1 else 1
            part = chunk(color, -d, 0, half)
            ring[color, "o", d] = send(part, part, to(color, d, 0))
            whole = chunk(color, -d, 0)
            for e in (1, -1):
                ring[color, "b", -d, e] = send(whole, whole, to(color, 0, e))
    for d in (1, -1):
        for color in (0, 1):
            ring[color, "b", 0, d].wait_recv()
            part = chunk(color, 0, -d, 0 if d == 1 else 1)
            ring[color, "c", 0, d] = send(part, part, to(color, 0, d))
    for color in (0, 1):
        ring[color, "o", 1].wait_recv()
        ring[color, "o", -1].wait_recv()
        whole = chunk(color, 2, 0)
        for e in (1, -1):
            ring[color, "b", 2, e] = send(whole, whole, to(color, 0, e))
    for a in (-1, 1, 2):
        hand_over(2)
        for d in (1, -1):
            for color in (0, 1):
                ring[color, "b", a, d].wait_recv()
                part = chunk(color, a, -d, 0 if d == 1 else 1)
                ring[color, "c", a, d] = send(part, part, to(color, 0, d))
    hand_over(len(wo_in) - len(handed))
    waited = {id(v) for k, v in ring.items() if k[1] != "c"} | {id(cp) for cp in handed}
    for cp in copies:
        if id(cp) not in waited:
            cp.wait_recv()
    for cp in copies:
        cp.wait_send()
    for cp in locals_:
        cp.wait()


N_GATHER = 15 + 2 + 8 + 2 + 4 + 8 + 4 + 4 + 12 + 2 * (2 * WO_CHUNKS - len(WO_LATE))


def gather_queries(q, ck, cv, sk, sv, tab, wo):
    anyspec = pl.BlockSpec(memory_space=pl.ANY)
    return pl.pallas_call(
        gather_kernel,
        out_shape=(
            jax.ShapeDtypeStruct((16, 2, BLK, q.shape[-1]), BF16),
            jax.ShapeDtypeStruct(ck.shape, BF16),
            jax.ShapeDtypeStruct(cv.shape, BF16),
            jax.ShapeDtypeStruct((2, BLK, HD), BF16),
            jax.ShapeDtypeStruct(tab.shape, jnp.int32),
            jax.ShapeDtypeStruct((2,) + wo.shape, BF16),
        ),
        in_specs=[anyspec] * 7,
        out_specs=[anyspec] * 6,
        scratch_shapes=[
            pltpu.SemaphoreType.DMA((N_GATHER,)),
            pltpu.SemaphoreType.DMA((N_GATHER,)),
            pltpu.SemaphoreType.DMA((2,)),
        ],
        compiler_params=pltpu.CompilerParams(collective_id=0, has_side_effects=True, vmem_limit_bytes=VMEM),
        name="gather_queries",
    )(q, ck, cv, sk, sv, tab, wo)


def attend_kernel(tab_ref, q_ref, ck_ref, cv_ref, pk_ref, pv_ref, sk_ref, sv_ref, prev_ref, out_ref,
                  kall, vall, span, sbuf, pbuf, m_s, l_s, acc, sems):
    i = pl.program_id(0)
    z, x, c, y = position()
    chip = i // 2
    color = i % 2
    mine = chip == z * 4 + x

    @pl.when(i == 0)
    def _():
        loads = [
            pltpu.make_async_copy(ck_ref, kall.at[pl.ds(0, 64)], sems.at[0]),
            pltpu.make_async_copy(pk_ref, kall.at[pl.ds(64, 64)], sems.at[1]),
            pltpu.make_async_copy(cv_ref, vall.at[pl.ds(0, 64)], sems.at[2]),
            pltpu.make_async_copy(pv_ref, vall.at[pl.ds(64, 64)], sems.at[3]),
            pltpu.make_async_copy(prev_ref.at[0], span.at[0, pl.ds(0, BLK)], sems.at[4]),
            pltpu.make_async_copy(prev_ref.at[1], span.at[1, pl.ds(0, BLK)], sems.at[5]),
            pltpu.make_async_copy(sk_ref, span.at[0, pl.ds(BLK, 2 * BLK)], sems.at[6]),
            pltpu.make_async_copy(sv_ref, span.at[1, pl.ds(BLK, 2 * BLK)], sems.at[7]),
        ]
        for cp in loads:
            cp.start()
        for cp in loads:
            cp.wait()

    heads = q_ref.shape[-1] // HD
    m_s[...] = jnp.full_like(m_s, NEG)
    l_s[...] = jnp.zeros_like(l_s)
    acc[...] = jnp.zeros_like(acc)
    scale = LOG2E / (HD ** 0.5)
    width = 256

    def pair(keys, values, bias):
        rows = keys.shape[0]
        spans = [slice(t * width, (t + 1) * width) for t in range(heads * HD // width)]
        tops = []
        for cols in spans:
            s = jnp.dot(keys, q_ref[0, 0, :, cols], preferred_element_type=F32)
            if bias is not None:
                s = s + bias
            sbuf[0:rows, cols] = s
            tops.append(jnp.maximum(m_s[:, cols], jnp.max(s, axis=0, keepdims=True)))
        olds = []
        for cols, top in zip(spans, tops):
            old = jnp.exp2((m_s[:, cols] - top) * scale)
            p = jnp.exp2((sbuf[0:rows, cols] - top) * scale)
            pbuf[0:rows, cols] = p.astype(BF16)
            m_s[:, cols] = top
            l_s[:, cols] = l_s[:, cols] * old + jnp.sum(p, axis=0, keepdims=True)
            olds.append(old)
        for cols, old in zip(spans, olds):
            acc[:, cols] = acc[:, cols] * old + lax.dot_general(
                values, pbuf[0:rows, cols], (((0,), (0,)), ((), ())), preferred_element_type=F32)

    count = tab_ref[chip, 0, color * 16 + 15]
    base = color * 16

    def group(start, size):
        ids = [tab_ref[chip, 0, base + start + n] for n in range(size)]
        pair(jnp.concatenate([kall[n] for n in ids], axis=0), jnp.concatenate([vall[n] for n in ids], axis=0), None)

    def four(j, carry):
        group(4 * j, 4)
        return carry

    fours = count // 4
    lax.fori_loop(0, fours, four, 0)
    for size in (1, 2, 3):
        @pl.when(count % 4 == size)
        def _():
            group(4 * fours, size)

    @pl.when(mine)
    def _():
        rows = pl.ds(pl.multiple_of(color * BLK, BLK), 2 * BLK)
        key = lax.broadcasted_iota(jnp.int32, (2 * BLK, width), 0)
        tok = lax.broadcasted_iota(jnp.int32, (2 * BLK, width), 1) % BLK
        first = (z * 8 + x * 2 + c) * 2 + color == 0
        low = jnp.where(first, BLK, 0)
        allowed = (key >= low) & (key - BLK <= tok)
        pair(span[0, rows, :], span[1, rows, :], jnp.where(allowed, 0.0, 2 * NEG))

    some = l_s[...] > 0
    total = jnp.where(some, l_s[...], 1.0)
    lse = m_s[...] * scale + jnp.log2(total)
    hi = lse.astype(BF16)
    rest = lse - hi.astype(F32)
    mid = rest.astype(BF16)
    low_ = (rest - mid.astype(F32)).astype(BF16)
    o = (acc[...] * (1.0 / total)).astype(BF16)
    row = lax.broadcasted_iota(jnp.int32, (EXTRA, lse.shape[1]), 0)
    tail = jnp.where(row == 0, hi.astype(F32), jnp.where(row == 1, mid.astype(F32), jnp.where(row == 2, low_.astype(F32), 0.0))).astype(BF16)
    half = lse.shape[1] // 2
    for h in range(2):
        out_ref[0, 0, h, 0:HD, :] = o[:, h * half:(h + 1) * half]
        out_ref[0, 0, h, HD:HD + EXTRA, :] = tail[:, h * half:(h + 1) * half]


def attend(tab, q_all, ck, cv, pk, pv, sk, sv, prev):
    width = q_all.shape[-1]
    anyspec = pl.BlockSpec(memory_space=pl.ANY)
    return pl.pallas_call(
        attend_kernel,
        out_shape=jax.ShapeDtypeStruct((16, 2, 2, HD + EXTRA, width // 2), BF16),
        grid_spec=pltpu.PrefetchScalarGridSpec(
            num_scalar_prefetch=1,
            grid=(32,),
            in_specs=[pl.BlockSpec((1, 1, BLK, width), lambda i, t: (i // 2, i % 2, 0, 0))] + [anyspec] * 7,
            out_specs=pl.BlockSpec((1, 1, 2, HD + EXTRA, width // 2), lambda i, t: (i // 2, i % 2, 0, 0, 0)),
            scratch_shapes=[
                pltpu.VMEM((128, BLK, HD), BF16),
                pltpu.VMEM((128, BLK, HD), BF16),
                pltpu.VMEM((2, 3 * BLK, HD), BF16),
                pltpu.VMEM((4 * BLK, width), F32),
                pltpu.VMEM((4 * BLK, width), BF16),
                pltpu.VMEM((1, width), F32),
                pltpu.VMEM((1, width), F32),
                pltpu.VMEM((HD, width), F32),
                pltpu.SemaphoreType.DMA((8,)),
            ],
        ),
        compiler_params=pltpu.CompilerParams(
            vmem_limit_bytes=VMEM),
        cost_estimate=pl.CostEstimate(flops=7_000_000_000, bytes_accessed=26_000_000, transcendentals=13_000_000),
        name="attend",
    )(tab, q_all, ck, cv, pk, pv, sk, sv, prev)


def merge(dst, *srcs):
    def lse_of(ref):
        t = ref[HD:HD + EXTRA, :].astype(F32)
        return t[0:1] + t[1:2] + t[2:3]

    lses = [lse_of(r) for r in srcs]
    top = functools.reduce(jnp.maximum, lses)
    ws = [jnp.exp2(v - top) for v in lses]
    total = functools.reduce(lambda a, b: a + b, ws)
    inv = 1.0 / total
    ws = [w * inv for w in ws]
    lse = top + jnp.log2(total)
    rows = 32

    def body(r, carry):
        sl = pl.ds(pl.multiple_of(r * rows, rows), rows)
        out = ws[0] * srcs[0][sl, :].astype(F32)
        for w, ref in zip(ws[1:], srcs[1:]):
            out = out + w * ref[sl, :].astype(F32)
        dst[sl, :] = out.astype(BF16)
        return carry

    lax.fori_loop(0, HD // rows, body, 0)
    hi = lse.astype(BF16).astype(F32)
    mid = (lse - hi).astype(BF16).astype(F32)
    low = lse - hi - mid
    row = lax.broadcasted_iota(jnp.int32, (EXTRA, lse.shape[1]), 0)
    dst[HD:HD + EXTRA, :] = jnp.where(row == 0, hi, jnp.where(row == 1, mid, jnp.where(row == 2, low, 0.0))).astype(BF16)


NCH = 4
SECOND = (2, 1, 3, 0)


def finish_kernel(part_ref, wo_ref, won_ref, out_ref,
                  loc, recv, att, attz, hb, relay, w, acc, tile, zrelay,
                  load_sem, r_send, r_recv, wo_send, wo_recv, w_sem,
                  a_send, a_recv, b_send, b_recv, s_send, s_recv, t_send, t_recv, home_sem):
    z, x, c, y = position()
    partner = dev(z, x, 1 - c, y)
    zp, zm = dev(z + 1, x, c, y), dev(z - 1, x, c, y)
    yp, ym = dev(z, x, c, y + 1), dev(z, x, c, y - 1)
    barrier = pltpu.get_barrier_semaphore()
    for target in (zp, zm, dev(z, x + 1, c, y), dev(z, x - 1, c, y), yp, ym, partner):
        pl.semaphore_signal(barrier, inc=1, device_id=target, device_id_type=MESH)

    def remote(src, dst, ssem, rsem, target):
        return pltpu.make_async_remote_copy(
            src_ref=src, dst_ref=dst, send_sem=ssem, recv_sem=rsem, device_id=target, device_id_type=MESH)

    def step(h, a, b):
        return (a, b) if h == 0 else (b, a)

    def to(h, a, b):
        dz, dx = step(h, a, b)
        return dev(z + dz, x + dx, c, y)

    loads = {}
    for k in (0, 1):
        for a in (2, 1, 3, 0):
            for b in SECOND:
                for h in (0, 1):
                    dz, dx = step(h, a, b)
                    slot = ((z + dz) % 4) * 4 + (x + dx) % 4
                    cp = pltpu.make_async_copy(part_ref.at[slot, k, h], loc.at[k * 2 + h, a * 4 + b], load_sem.at[len(loads)])
                    cp.start()
                    loads[k, h, a, b] = cp
    depth = wo_ref.shape[0] // (2 * WO_CHUNKS)

    def early(i, r, core):
        first = core * WO_CHUNKS + (0 if i == 0 else 1)
        rows = pl.ds(first * depth, (WO_CHUNKS - 1) * depth)
        return pltpu.make_async_copy(won_ref.at[i, rows], w.at[r, rows], w_sem.at[1 + i * 2 + core])

    w_loads = [pltpu.make_async_copy(wo_ref, w.at[0], w_sem.at[0])]
    w_loads += [early(i, r, core) for i, r in ((1, 1), (0, 3)) for core in (0, 1)]
    for cp in w_loads:
        cp.start()
    pl.semaphore_wait(barrier, 7)

    quarter = wo_ref.shape[0] // 4
    wo_copies = []

    def send_wo(src, n, target):
        rows = pl.ds(pl.multiple_of(c * (2 * quarter) + (n % 2) * quarter, quarter), quarter)
        cp = remote(src.at[rows], w.at[2, rows], wo_send.at[n], wo_recv.at[n], target)
        cp.start()
        wo_copies.append(cp)

    send_wo(won_ref.at[0], 0, yp)
    send_wo(won_ref.at[1], 1, ym)

    def late(n, hand):
        i, chunk = WO_LATE[n]
        rows = pl.ds(pl.multiple_of((c * WO_CHUNKS + chunk) * depth, depth), depth)
        dst = w.at[3 if i == 0 else 1, rows]
        target = partner if hand else (yp if i == 0 else ym)
        return remote(dst if hand else wo_ref.at[rows], dst, wo_send.at[4 + 2 * hand + n], wo_recv.at[4 + 2 * hand + n], target)

    for n in (0, 1):
        late(n, 0).start()

    quart = loc.shape[-1] // 2
    copies = {}

    def send(key, src, target):
        n = len(copies)
        cp = remote(src, recv.at[n], r_send.at[n], r_recv.at[n], target)
        cp.start()
        copies[key] = (cp, n)

    def got(key):
        cp, n = copies[key]
        cp.wait_recv()
        return recv.at[n]

    def piece(k, h, a, b, q):
        return loc.at[k * 2 + h, a * 4 + b, :, q * quart:(q + 1) * quart]

    def first_sends(k, b):
        for h in (0, 1):
            loads[k, h, 2, b].wait()
            send((k, h, b, "op"), piece(k, h, 2, b, 0), to(h, 1, 0))
            send((k, h, b, "om"), piece(k, h, 2, b, 1), to(h, -1, 0))

    def first_raw(k, b):
        for h in (0, 1):
            loads[k, h, 1, b].wait()
            send((k, h, b, "p1"), piece(k, h, 1, b, 1), to(h, 1, 0))
            loads[k, h, 3, b].wait()
            send((k, h, b, "m0"), piece(k, h, 3, b, 0), to(h, -1, 0))

    def first_sums(k, b):
        for h in (0, 1):
            r = got((k, h, b, "op"))
            merge(piece(k, h, 1, b, 0), piece(k, h, 1, b, 0), r)
            send((k, h, b, "p0"), piece(k, h, 1, b, 0), to(h, 1, 0))
            r = got((k, h, b, "om"))
            merge(piece(k, h, 3, b, 1), piece(k, h, 3, b, 1), r)
            send((k, h, b, "m1"), piece(k, h, 3, b, 1), to(h, -1, 0))

    def second_sends(k, b):
        for h in (0, 1):
            loads[k, h, 0, b].wait()
            for q in (1, 0):
                p = got((k, h, b, "p%d" % q))
                m = got((k, h, b, "m%d" % q))
                merge(piece(k, h, 0, b, q), piece(k, h, 0, b, q), p, m)
            if b == 2:
                send((k, h, "op"), piece(k, h, 0, 2, 0), to(h, 0, 1))
                send((k, h, "om"), piece(k, h, 0, 2, 1), to(h, 0, -1))
            if b == 1:
                send((k, h, "p1"), piece(k, h, 0, 1, 1), to(h, 0, 1))
            if b == 3:
                send((k, h, "m0"), piece(k, h, 0, 3, 0), to(h, 0, -1))

    def second_sums(k):
        for h in (0, 1):
            r = got((k, h, "op"))
            merge(piece(k, h, 0, 1, 0), piece(k, h, 0, 1, 0), r)
            send((k, h, "p0"), piece(k, h, 0, 1, 0), to(h, 0, 1))
            r = got((k, h, "om"))
            merge(piece(k, h, 0, 3, 1), piece(k, h, 0, 3, 1), r)
            send((k, h, "m1"), piece(k, h, 0, 3, 1), to(h, 0, -1))

    def last_sums(k):
        for h in (0, 1):
            for q in (1, 0):
                p = got((k, h, "p%d" % q))
                m = got((k, h, "m%d" % q))
                own = piece(k, h, 0, 0, q)
                merge(own, own, p, m)
                for g in range(quart // HD):
                    col = (h * 2 + q) * quart + g * HD
                    att[k, :, col:col + HD] = own[0:HD, g * HD:(g + 1) * HD].T

    half = BLK // 2
    lo, hi = pl.ds(0, half), pl.ds(half, half)

    def ring_of(k):
        n = k * 4
        return [
            remote(att.at[k], attz.at[k, 3], a_send.at[n], a_recv.at[n], zp),
            remote(att.at[k], attz.at[k, 1], a_send.at[n + 1], a_recv.at[n + 1], zm),
            remote(attz.at[k, 3, lo], attz.at[k, 2, lo], a_send.at[n + 2], a_recv.at[n + 2], zp),
            remote(attz.at[k, 1, hi], attz.at[k, 2, hi], a_send.at[n + 3], a_recv.at[n + 3], zm),
        ]

    def spread_of(k, src):
        n = k * 6
        return [
            remote(src, hb.at[k, 3], b_send.at[n], b_recv.at[n], yp),
            remote(src, hb.at[k, 1], b_send.at[n + 1], b_recv.at[n + 1], ym),
            remote(src.at[lo], relay.at[k, 0], b_send.at[n + 2], b_recv.at[n + 2], yp),
            remote(src.at[hi], relay.at[k, 1], b_send.at[n + 3], b_recv.at[n + 3], ym),
            remote(relay.at[k, 0], hb.at[k, 2, lo], b_send.at[n + 4], b_recv.at[n + 4], yp),
            remote(relay.at[k, 1], hb.at[k, 2, hi], b_send.at[n + 5], b_recv.at[n + 5], ym),
        ]

    def spread(k, dz):
        src = att.at[k] if dz == 0 else attz.at[k, dz]
        d = (dz - y + 4) % 4

        @pl.when(d == 0)
        def _():
            hb[k, 0] = src[...]

        @pl.when(d == 1)
        def _():
            spread_of(k, src)[0].start()

        @pl.when(d == 3)
        def _():
            spread_of(k, src)[1].start()

        @pl.when(d == 2)
        def _():
            spread_of(k, src)[2].start()
            spread_of(k, src)[3].start()

    def rows_out(k):
        r = ring_of(k)
        r[0].start()
        r[1].start()
        spread(k, 0)

    def rows_next(k):
        r = ring_of(k)
        r[0].wait_recv()
        r[2].start()
        spread(k, 3)
        r[1].wait_recv()
        r[3].start()
        spread(k, 1)

    def rows_far(k):
        r = ring_of(k)
        r[2].wait_recv()
        r[3].wait_recv()
        spread(k, 2)

    def rows_relay(k):
        sp = spread_of(k, att.at[k])
        for n in (0, 1):
            sp[2 + n].wait_recv()
            sp[4 + n].start()

    cols = wo_ref.shape[1]
    width = cols // NCH

    def term(k, r, first):
        def one(n, carry):
            sl = pl.ds(pl.multiple_of(n * 256, 256), 256)
            v = jnp.dot(hb[k, r], w[r, :, sl], preferred_element_type=F32)
            acc[k, :, sl] = v if first else acc[k, :, sl] + v
            return carry
        lax.fori_loop(0, cols // 256, one, 0)

    def terms(k):
        sp = spread_of(k, att.at[k])
        if k == 0:
            for cp in w_loads:
                cp.wait()
            for n in (0, 1):
                late(n, 1).wait_recv()
        term(k, 0, True)
        sp[0].wait_recv()
        term(k, 3, False)
        sp[1].wait_recv()
        term(k, 1, False)
        sp[4].wait_recv()
        sp[5].wait_recv()

    def region(k, f, ch, rows=None):
        sl = pl.ds(pl.multiple_of(((f + 8) % 4) * cols + ch * width, width), width)
        first, size = (k * BLK, BLK) if rows is None else (k * BLK + rows * half, half)
        return out_ref.at[pl.ds(first, size), sl]

    def shifts(k, ch):
        n = (k * NCH + ch) * 5
        src = tile.at[k, ch]
        return [
            remote(src, region(k, z, ch), s_send.at[n], s_recv.at[n], zp),
            remote(src, region(k, z, ch), s_send.at[n], s_recv.at[n], zm),
            remote(src.at[lo], zrelay.at[k, ch, 0], s_send.at[n + 1], s_recv.at[n + 1], zp),
            remote(src.at[hi], zrelay.at[k, ch, 1], s_send.at[n + 2], s_recv.at[n + 2], zm),
            remote(zrelay.at[k, ch, 0], region(k, z - 1, ch, 0), s_send.at[n + 3], s_recv.at[n + 3], zp),
            remote(zrelay.at[k, ch, 1], region(k, z + 1, ch, 1), s_send.at[n + 4], s_recv.at[n + 4], zm),
        ]

    def home(k, ch):
        return pltpu.make_async_copy(tile.at[k, ch], region(k, z, ch), home_sem.at[k * NCH + ch])

    def bcast(k, ch):
        n = (k * NCH + ch) * 4
        mine = region(k, z - y, ch)
        up = region(k, z - y + 1, ch, 0)
        down = region(k, z - y - 1, ch, 1)
        return [
            remote(mine, mine, t_send.at[n], t_recv.at[n], yp),
            remote(mine, mine, t_send.at[n + 1], t_recv.at[n + 1], ym),
            remote(up, up, t_send.at[n + 2], t_recv.at[n + 2], yp),
            remote(down, down, t_send.at[n + 3], t_recv.at[n + 3], ym),
        ]

    def tile_out(k, ch):
        for n in range(width // 256):
            sl = slice(ch * width + n * 256, ch * width + (n + 1) * 256)
            v = acc[k, :, sl] + jnp.dot(hb[k, 2], w[2, :, sl], preferred_element_type=F32)
            tile[k, ch, :, n * 256:(n + 1) * 256] = v.astype(BF16)

        @pl.when(y == 0)
        def _():
            home(k, ch).start()

        @pl.when(y == 1)
        def _():
            shifts(k, ch)[0].start()

        @pl.when(y == 3)
        def _():
            shifts(k, ch)[1].start()

        @pl.when(y == 2)
        def _():
            shifts(k, ch)[2].start()
            shifts(k, ch)[3].start()

    def tile_relay(k, ch):
        @pl.when(y == 2)
        def _():
            sr = shifts(k, ch)
            sr[2].wait_recv()
            sr[4].start()
            sr[3].wait_recv()
            sr[5].start()

    def tile_home(k, ch):
        @pl.when(y == 0)
        def _():
            home(k, ch).wait()

        @pl.when(y % 2 == 1)
        def _():
            shifts(k, ch)[0].wait_recv()

        @pl.when(y == 2)
        def _():
            se = shifts(k, ch)
            se[4].wait_recv()
            se[5].wait_recv()

        b = bcast(k, ch)
        b[0].start()
        b[1].start()

    def tile_onward(k, ch):
        b = bcast(k, ch)
        b[0].wait_recv()
        b[2].start()
        b[1].wait_recv()
        b[3].start()

    for b in SECOND:
        first_sends(0, b)
    for b in SECOND:
        first_raw(0, b)
    for b in SECOND:
        first_sums(0, b)
    for b in SECOND:
        first_sends(1, b)
        second_sends(0, b)
    for n in (0, 1):
        wo_copies[n].wait_recv()
        send_wo(w.at[2], 2 + n, partner)
    second_sums(0)
    for b in SECOND:
        first_raw(1, b)
    last_sums(0)
    rows_out(0)
    for n in (0, 1):
        late(n, 0).wait_recv()
        late(n, 1).start()
    for b in SECOND:
        first_sums(1, b)
    rows_next(0)
    second_sends(1, 2)
    second_sends(1, 1)
    rows_far(0)
    second_sends(1, 3)
    second_sends(1, 0)
    rows_relay(0)
    second_sums(1)
    last_sums(1)
    rows_out(1)
    terms(0)
    wo_copies[2].wait_recv()
    wo_copies[3].wait_recv()
    for ch in range(NCH):
        tile_out(0, ch)
    rows_next(1)
    for ch in range(NCH):
        tile_relay(0, ch)
    tile_home(0, 0)
    tile_home(0, 1)
    rows_far(1)
    tile_home(0, 2)
    tile_home(0, 3)
    rows_relay(1)
    tile_onward(0, 0)
    terms(1)
    for ch in range(NCH):
        tile_out(1, ch)
    tile_onward(0, 1)
    tile_onward(0, 2)
    tile_onward(0, 3)
    for t in range(NCH + 2):
        if t < NCH:
            tile_relay(1, t)
        if 1 <= t < NCH + 1:
            tile_home(1, t - 1)
        if 2 <= t:
            tile_onward(1, t - 2)
    for k in (0, 1):
        for ch in range(NCH):
            b = bcast(k, ch)
            b[2].wait_recv()
            b[3].wait_recv()
            for cp in b:
                cp.wait_send()

            @pl.when(y % 2 == 1)
            def _():
                shifts(k, ch)[0].wait_send()

            @pl.when(y == 2)
            def _():
                for cp in shifts(k, ch)[2:]:
                    cp.wait_send()
        for cp in ring_of(k) + spread_of(k, att.at[k]):
            cp.wait_send()
    for cp in wo_copies + [late(n, hand) for n in (0, 1) for hand in (0, 1)]:
        cp.wait_send()
    for cp, _ in copies.values():
        cp.wait_send()


N_REDUCE = 120


def finish(part, wo, won):
    rows, lanes = part.shape[-2:]
    depth, cols = wo.shape
    anyspec = pl.BlockSpec(memory_space=pl.ANY)
    sem = pltpu.SemaphoreType.DMA
    return pl.pallas_call(
        finish_kernel,
        out_shape=jax.ShapeDtypeStruct((2 * BLK, 4 * cols), BF16),
        in_specs=[anyspec] * 3,
        out_specs=anyspec,
        scratch_shapes=[
            pltpu.VMEM((4, 16, rows, lanes), BF16),
            pltpu.VMEM((N_REDUCE, rows, lanes // 2), BF16),
            pltpu.VMEM((2, BLK, depth), BF16),
            pltpu.VMEM((2, 4, BLK, depth), BF16),
            pltpu.VMEM((2, 4, BLK, depth), BF16),
            pltpu.VMEM((2, 2, BLK // 2, depth), BF16),
            pltpu.VMEM((4, depth, cols), BF16),
            pltpu.VMEM((2, BLK, cols), F32),
            pltpu.VMEM((2, NCH, BLK, cols // NCH), BF16),
            pltpu.VMEM((2, NCH, 2, BLK // 2, cols // NCH), BF16),
            sem((64,)), sem((N_REDUCE,)), sem((N_REDUCE,)), sem((8,)), sem((8,)), sem((5,)),
            sem((8,)), sem((8,)), sem((12,)), sem((12,)),
            sem((10 * NCH,)), sem((10 * NCH,)), sem((8 * NCH,)), sem((8 * NCH,)), sem((2 * NCH,)),
        ],
        compiler_params=pltpu.CompilerParams(
            collective_id=1, has_side_effects=True, vmem_limit_bytes=VMEM),
        name="finish",
    )(part, wo, won)


def prepare_kernel(cb_local, slot_ref, pattern_ref, q_ref, tab_ref, out_ref):
    core = position()[2]
    for chip in range(16):
        for k in range(2):
            tab_ref[chip, 0, k * 16 + 15] = 0

    def one(e, carry):
        for k in range(2):
            slot = slot_ref[pattern_ref[k, e]]
            owner = slot // cb_local
            chip = owner // 2
            here = jnp.where(owner % 2 == core, 0, cb_local) + slot % cb_local
            n = tab_ref[chip, 0, k * 16 + 15]
            tab_ref[chip, 0, k * 16 + n] = here
            tab_ref[chip, 0, k * 16 + 15] = n + 1
        return carry

    lax.fori_loop(0, pattern_ref.shape[1], one, 0)
    for color in range(2):
        for g in range(q_ref.shape[1] // HD):
            out_ref[color, :, g * BLK:(g + 1) * BLK] = q_ref[color * BLK:(color + 1) * BLK, g * HD:(g + 1) * HD].T


def prepare(block_slot, pattern, queries, cb_local):
    return pl.pallas_call(
        functools.partial(prepare_kernel, cb_local),
        out_shape=(jax.ShapeDtypeStruct((16, 1, 128), jnp.int32),
                   jax.ShapeDtypeStruct((2, HD, queries.shape[1]), BF16)),
        in_specs=[pl.BlockSpec(memory_space=pltpu.SMEM)] * 2 + [pl.BlockSpec(memory_space=pltpu.VMEM)],
        out_specs=(pl.BlockSpec(memory_space=pltpu.SMEM), pl.BlockSpec(memory_space=pltpu.VMEM)),
        compiler_params=pltpu.CompilerParams(vmem_limit_bytes=VMEM),
        name="prepare",
    )(block_slot, pattern, queries)


def body(queries, span_k, span_v, cache_k, cache_v, block_slot, pattern, wo):
    tab, q = prepare(block_slot, pattern, queries, cache_k.shape[0])
    q_all, pk, pv, prev, tab_all, won = gather_queries(q, cache_k, cache_v, span_k, span_v, tab, wo)
    part = attend(tab_all, q_all, cache_k, cache_v, pk, pv, span_k, span_v, prev)
    return finish(part, wo, won)


def solution(mesh):
    return jax.shard_map(
        body,
        mesh=mesh,
        in_specs=(
            P(("fsdp", "seq"), "head"),
            P(("fsdp", "seq"), "head"),
            P(("fsdp", "seq"), "head"),
            P(("fsdp", "seq"), None, "head"),
            P(("fsdp", "seq"), None, "head"),
            P(),
            P(("fsdp", "seq"), None),
            P("head", "fsdp"),
        ),
        out_specs=P(("fsdp", "seq"), None),
        check_vma=False,
    )
```

```python
import functools

import jax
import jax.numpy as jnp
from jax import lax
from jax.experimental import pallas as pl
from jax.experimental.pallas import tpu as pltpu
from jax.sharding import PartitionSpec as P

HD = 128
BLK = 128
EXTRA = 8
WO_CHUNKS = 4
WO_LATE = ((0, 3), (1, 0))
NEG = -1e30
VMEM = 62 * 2**20
MESH = pl.DeviceIdType.MESH
BF16 = jnp.bfloat16
F32 = jnp.float32
LOG2E = 1.4426950408889634


def position():
    z = lax.axis_index("fsdp")
    s = lax.axis_index("seq")
    y = lax.axis_index("head")
    return z, s // 2, s % 2, y


def dev(z, x, c, y):
    return ((z + 4) % 4, ((x + 4) % 4) * 2 + c, (y + 4) % 4)


def gather_kernel(q_ref, ck_ref, cv_ref, sk_ref, sv_ref, tab_ref, wo_ref,
                  qall_ref, pk_ref, pv_ref, prev_ref, taball_ref, won_ref,
                  send_sem, recv_sem, loc_sem):
    z, x, c, y = position()
    far_z, far_x = (z, x + jnp.where(c == 0, -1, 1))
    wrap = jnp.where(c == 0, jnp.where(x == 0, -1, 0), jnp.where(x == 3, 1, 0))
    far_z = far_z + wrap

    barrier = pltpu.get_barrier_semaphore()
    for off in range(1, 16):
        pl.semaphore_signal(barrier, inc=1, device_id=dev(z + off // 4, x + off % 4, c, y), device_id_type=MESH)
    pl.semaphore_signal(barrier, inc=1, device_id=dev(z, x, 1 - c, y), device_id_type=MESH)
    pl.semaphore_signal(barrier, inc=1, device_id=dev(far_z, far_x, 1 - c, y), device_id_type=MESH)
    for d in (1, -1):
        pl.semaphore_signal(barrier, inc=1, device_id=dev(z, x, c, y + d), device_id_type=MESH)
    pl.semaphore_wait(barrier, 19)

    copies = []

    def send(src, dst, target):
        k = len(copies)
        cp = pltpu.make_async_remote_copy(
            src_ref=src, dst_ref=dst, send_sem=send_sem.at[k], recv_sem=recv_sem.at[k],
            device_id=target, device_id_type=MESH)
        cp.start()
        copies.append(cp)
        return cp

    def slot(dz, dx):
        return ((z + dz + 4) % 4) * 4 + (x + dx + 4) % 4

    here = slot(0, 0)
    tables = []
    for off in range(1, 16):
        dz, dx = off // 4, off % 4
        tables.append(send(tab_ref.at[slot(dz, dx)], taball_ref.at[here], dev(z + dz, x + dx, c, y)))
    nxt_x = x + jnp.where(c == 0, 0, 1)
    nxt_z = z + jnp.where((c == 1) & (x == 3), 1, 0)
    nxt = dev(nxt_z, nxt_x, 1 - c, y)
    send(sk_ref.at[pl.ds(BLK, BLK)], prev_ref.at[0], nxt)
    send(sv_ref.at[pl.ds(BLK, BLK)], prev_ref.at[1], nxt)

    def step(color, major, minor):
        return (minor, major) if color == 0 else (major, minor)

    def chunk(color, a, b, half=None):
        dz, dx = step(color, a, b)
        ref = qall_ref.at[slot(dz, dx), color]
        if half is None:
            return ref
        return ref.at[pl.ds(half * (BLK // 2), BLK // 2)]

    def to(color, a, b):
        dz, dx = step(color, a, b)
        return dev(z + dz, x + dx, c, y)

    ring = {}

    def own(color):
        mine, dst = q_ref.at[color], qall_ref.at[here, color]
        for d in (1, -1):
            ring[color, "a", d] = send(mine, dst, to(color, d, 0))
        for d in (1, -1):
            ring[color, "b", 0, d] = send(mine, dst, to(color, 0, d))

    own(0)
    own(1)
    depth = wo_ref.shape[0] // (2 * WO_CHUNKS)

    def share(n):
        return pl.ds(pl.multiple_of((c * WO_CHUNKS + n) * depth, depth), depth)

    wo_in = []
    for n in range(WO_CHUNKS):
        for i, d in ((0, 1), (1, -1)):
            if (i, n) not in WO_LATE:
                wo_in.append((i, n, send(wo_ref.at[share(n)], won_ref.at[i, share(n)], dev(z, x, c, y + d))))

    def hand_over(count):
        for _ in range(count):
            i, n, cp = wo_in[len(handed)]
            handed.append(cp)
            cp.wait_recv()
            send(won_ref.at[i, share(n)], won_ref.at[i, share(n)], partner)

    handed = []
    partner = dev(z, x, 1 - c, y)
    send(ck_ref, pk_ref, partner)
    send(cv_ref, pv_ref, partner)
    locals_ = [pltpu.make_async_copy(q_ref, qall_ref.at[here], loc_sem.at[0]),
               pltpu.make_async_copy(tab_ref.at[here], taball_ref.at[here], loc_sem.at[1])]
    for cp in locals_:
        cp.start()

    for d in (1, -1):
        for color in (0, 1):
            ring[color, "a", d].wait_recv()
            half = 0 if d == 1 else 1
            part = chunk(color, -d, 0, half)
            ring[color, "o", d] = send(part, part, to(color, d, 0))
            whole = chunk(color, -d, 0)
            for e in (1, -1):
                ring[color, "b", -d, e] = send(whole, whole, to(color, 0, e))
    for d in (1, -1):
        for color in (0, 1):
            ring[color, "b", 0, d].wait_recv()
            part = chunk(color, 0, -d, 0 if d == 1 else 1)
            ring[color, "c", 0, d] = send(part, part, to(color, 0, d))
    for color in (0, 1):
        ring[color, "o", 1].wait_recv()
        ring[color, "o", -1].wait_recv()
        whole = chunk(color, 2, 0)
        for e in (1, -1):
            ring[color, "b", 2, e] = send(whole, whole, to(color, 0, e))
    for a in (-1, 1, 2):
        hand_over(2)
        for d in (1, -1):
            for color in (0, 1):
                ring[color, "b", a, d].wait_recv()
                part = chunk(color, a, -d, 0 if d == 1 else 1)
                ring[color, "c", a, d] = send(part, part, to(color, 0, d))
    hand_over(len(wo_in) - len(handed))
    waited = {id(v) for k, v in ring.items() if k[1] != "c"} | {id(cp) for cp in handed}
    for cp in copies:
        if id(cp) not in waited:
            cp.wait_recv()
    for cp in copies:
        cp.wait_send()
    for cp in locals_:
        cp.wait()


N_GATHER = 15 + 2 + 8 + 2 + 4 + 8 + 4 + 4 + 12 + 2 * (2 * WO_CHUNKS - len(WO_LATE))


def gather_queries(q, ck, cv, sk, sv, tab, wo):
    anyspec = pl.BlockSpec(memory_space=pl.ANY)
    return pl.pallas_call(
        gather_kernel,
        out_shape=(
            jax.ShapeDtypeStruct((16, 2, BLK, q.shape[-1]), BF16),
            jax.ShapeDtypeStruct(ck.shape, BF16),
            jax.ShapeDtypeStruct(cv.shape, BF16),
            jax.ShapeDtypeStruct((2, BLK, HD), BF16),
            jax.ShapeDtypeStruct(tab.shape, jnp.int32),
            jax.ShapeDtypeStruct((2,) + wo.shape, BF16),
        ),
        in_specs=[anyspec] * 7,
        out_specs=[anyspec] * 6,
        scratch_shapes=[
            pltpu.SemaphoreType.DMA((N_GATHER,)),
            pltpu.SemaphoreType.DMA((N_GATHER,)),
            pltpu.SemaphoreType.DMA((2,)),
        ],
        compiler_params=pltpu.CompilerParams(collective_id=0, has_side_effects=True, vmem_limit_bytes=VMEM),
        name="gather_queries",
    )(q, ck, cv, sk, sv, tab, wo)


def attend_kernel(tab_ref, q_ref, ck_ref, cv_ref, pk_ref, pv_ref, sk_ref, sv_ref, prev_ref, out_ref,
                  kall, vall, span, sbuf, pbuf, m_s, l_s, acc, sems):
    i = pl.program_id(0)
    z, x, c, y = position()
    chip = i // 2
    color = i % 2
    mine = chip == z * 4 + x

    @pl.when(i == 0)
    def _():
        loads = [
            pltpu.make_async_copy(ck_ref, kall.at[pl.ds(0, 64)], sems.at[0]),
            pltpu.make_async_copy(pk_ref, kall.at[pl.ds(64, 64)], sems.at[1]),
            pltpu.make_async_copy(cv_ref, vall.at[pl.ds(0, 64)], sems.at[2]),
            pltpu.make_async_copy(pv_ref, vall.at[pl.ds(64, 64)], sems.at[3]),
            pltpu.make_async_copy(prev_ref.at[0], span.at[0, pl.ds(0, BLK)], sems.at[4]),
            pltpu.make_async_copy(prev_ref.at[1], span.at[1, pl.ds(0, BLK)], sems.at[5]),
            pltpu.make_async_copy(sk_ref, span.at[0, pl.ds(BLK, 2 * BLK)], sems.at[6]),
            pltpu.make_async_copy(sv_ref, span.at[1, pl.ds(BLK, 2 * BLK)], sems.at[7]),
        ]
        for cp in loads:
            cp.start()
        for cp in loads:
            cp.wait()

    heads = q_ref.shape[-1] // HD
    m_s[...] = jnp.full_like(m_s, NEG)
    l_s[...] = jnp.zeros_like(l_s)
    acc[...] = jnp.zeros_like(acc)
    scale = LOG2E / (HD ** 0.5)
    width = 256

    def pair(keys, values, bias):
        rows = keys.shape[0]
        spans = [slice(t * width, (t + 1) * width) for t in range(heads * HD // width)]
        tops = []
        for cols in spans:
            s = jnp.dot(keys, q_ref[0, 0, :, cols], preferred_element_type=F32)
            if bias is not None:
                s = s + bias
            sbuf[0:rows, cols] = s
            tops.append(jnp.maximum(m_s[:, cols], jnp.max(s, axis=0, keepdims=True)))
        olds = []
        for cols, top in zip(spans, tops):
            old = jnp.exp2((m_s[:, cols] - top) * scale)
            p = jnp.exp2((sbuf[0:rows, cols] - top) * scale)
            pbuf[0:rows, cols] = p.astype(BF16)
            m_s[:, cols] = top
            l_s[:, cols] = l_s[:, cols] * old + jnp.sum(p, axis=0, keepdims=True)
            olds.append(old)
        for cols, old in zip(spans, olds):
            acc[:, cols] = acc[:, cols] * old + lax.dot_general(
                values, pbuf[0:rows, cols], (((0,), (0,)), ((), ())), preferred_element_type=F32)

    count = tab_ref[chip, 0, color * 16 + 15]
    base = color * 16

    def group(start, size):
        ids = [tab_ref[chip, 0, base + start + n] for n in range(size)]
        pair(jnp.concatenate([kall[n] for n in ids], axis=0), jnp.concatenate([vall[n] for n in ids], axis=0), None)

    def four(j, carry):
        group(4 * j, 4)
        return carry

    fours = count // 4
    lax.fori_loop(0, fours, four, 0)
    for size in (1, 2, 3):
        @pl.when(count % 4 == size)
        def _():
            group(4 * fours, size)

    @pl.when(mine)
    def _():
        rows = pl.ds(pl.multiple_of(color * BLK, BLK), 2 * BLK)
        key = lax.broadcasted_iota(jnp.int32, (2 * BLK, width), 0)
        tok = lax.broadcasted_iota(jnp.int32, (2 * BLK, width), 1) % BLK
        first = (z * 8 + x * 2 + c) * 2 + color == 0
        low = jnp.where(first, BLK, 0)
        allowed = (key >= low) & (key - BLK <= tok)
        pair(span[0, rows, :], span[1, rows, :], jnp.where(allowed, 0.0, 2 * NEG))

    some = l_s[...] > 0
    total = jnp.where(some, l_s[...], 1.0)
    lse = m_s[...] * scale + jnp.log2(total)
    hi = lse.astype(BF16)
    rest = lse - hi.astype(F32)
    mid = rest.astype(BF16)
    low_ = (rest - mid.astype(F32)).astype(BF16)
    o = (acc[...] * (1.0 / total)).astype(BF16)
    row = lax.broadcasted_iota(jnp.int32, (EXTRA, lse.shape[1]), 0)
    tail = jnp.where(row == 0, hi.astype(F32), jnp.where(row == 1, mid.astype(F32), jnp.where(row == 2, low_.astype(F32), 0.0))).astype(BF16)
    half = lse.shape[1] // 2
    for h in range(2):
        out_ref[0, 0, h, 0:HD, :] = o[:, h * half:(h + 1) * half]
        out_ref[0, 0, h, HD:HD + EXTRA, :] = tail[:, h * half:(h + 1) * half]


def attend(tab, q_all, ck, cv, pk, pv, sk, sv, prev):
    width = q_all.shape[-1]
    anyspec = pl.BlockSpec(memory_space=pl.ANY)
    return pl.pallas_call(
        attend_kernel,
        out_shape=jax.ShapeDtypeStruct((16, 2, 2, HD + EXTRA, width // 2), BF16),
        grid_spec=pltpu.PrefetchScalarGridSpec(
            num_scalar_prefetch=1,
            grid=(32,),
            in_specs=[pl.BlockSpec((1, 1, BLK, width), lambda i, t: (i // 2, i % 2, 0, 0))] + [anyspec] * 7,
            out_specs=pl.BlockSpec((1, 1, 2, HD + EXTRA, width // 2), lambda i, t: (i // 2, i % 2, 0, 0, 0)),
            scratch_shapes=[
                pltpu.VMEM((128, BLK, HD), BF16),
                pltpu.VMEM((128, BLK, HD), BF16),
                pltpu.VMEM((2, 3 * BLK, HD), BF16),
                pltpu.VMEM((4 * BLK, width), F32),
                pltpu.VMEM((4 * BLK, width), BF16),
                pltpu.VMEM((1, width), F32),
                pltpu.VMEM((1, width), F32),
                pltpu.VMEM((HD, width), F32),
                pltpu.SemaphoreType.DMA((8,)),
            ],
        ),
        compiler_params=pltpu.CompilerParams(
            vmem_limit_bytes=VMEM),
        cost_estimate=pl.CostEstimate(flops=7_000_000_000, bytes_accessed=26_000_000, transcendentals=13_000_000),
        name="attend",
    )(tab, q_all, ck, cv, pk, pv, sk, sv, prev)


def merge(dst, *srcs):
    def lse_of(ref):
        t = ref[HD:HD + EXTRA, :].astype(F32)
        return t[0:1] + t[1:2] + t[2:3]

    lses = [lse_of(r) for r in srcs]
    top = functools.reduce(jnp.maximum, lses)
    ws = [jnp.exp2(v - top) for v in lses]
    total = functools.reduce(lambda a, b: a + b, ws)
    inv = 1.0 / total
    ws = [w * inv for w in ws]
    lse = top + jnp.log2(total)
    rows = 32

    def body(r, carry):
        sl = pl.ds(pl.multiple_of(r * rows, rows), rows)
        out = ws[0] * srcs[0][sl, :].astype(F32)
        for w, ref in zip(ws[1:], srcs[1:]):
            out = out + w * ref[sl, :].astype(F32)
        dst[sl, :] = out.astype(BF16)
        return carry

    lax.fori_loop(0, HD // rows, body, 0)
    hi = lse.astype(BF16).astype(F32)
    mid = (lse - hi).astype(BF16).astype(F32)
    low = lse - hi - mid
    row = lax.broadcasted_iota(jnp.int32, (EXTRA, lse.shape[1]), 0)
    dst[HD:HD + EXTRA, :] = jnp.where(row == 0, hi, jnp.where(row == 1, mid, jnp.where(row == 2, low, 0.0))).astype(BF16)


NCH = 4
SECOND = (2, 1, 3, 0)


def finish_kernel(part_ref, wo_ref, won_ref, out_ref,
                  loc, recv, att, attz, hb, relay, w, acc, tile, zrelay,
                  load_sem, r_send, r_recv, wo_send, wo_recv, w_sem,
                  a_send, a_recv, b_send, b_recv, s_send, s_recv, t_send, t_recv, home_sem):
    z, x, c, y = position()
    partner = dev(z, x, 1 - c, y)
    zp, zm = dev(z + 1, x, c, y), dev(z - 1, x, c, y)
    yp, ym = dev(z, x, c, y + 1), dev(z, x, c, y - 1)
    barrier = pltpu.get_barrier_semaphore()
    for target in (zp, zm, dev(z, x + 1, c, y), dev(z, x - 1, c, y), yp, ym, partner):
        pl.semaphore_signal(barrier, inc=1, device_id=target, device_id_type=MESH)

    def remote(src, dst, ssem, rsem, target):
        return pltpu.make_async_remote_copy(
            src_ref=src, dst_ref=dst, send_sem=ssem, recv_sem=rsem, device_id=target, device_id_type=MESH)

    def step(h, a, b):
        return (a, b) if h == 0 else (b, a)

    def to(h, a, b):
        dz, dx = step(h, a, b)
        return dev(z + dz, x + dx, c, y)

    loads = {}
    for k in (0, 1):
        for a in (2, 1, 3, 0):
            for b in SECOND:
                for h in (0, 1):
                    dz, dx = step(h, a, b)
                    slot = ((z + dz) % 4) * 4 + (x + dx) % 4
                    cp = pltpu.make_async_copy(part_ref.at[slot, k, h], loc.at[k * 2 + h, a * 4 + b], load_sem.at[len(loads)])
                    cp.start()
                    loads[k, h, a, b] = cp
    depth = wo_ref.shape[0] // (2 * WO_CHUNKS)

    def early(i, r, core):
        first = core * WO_CHUNKS + (0 if i == 0 else 1)
        rows = pl.ds(first * depth, (WO_CHUNKS - 1) * depth)
        return pltpu.make_async_copy(won_ref.at[i, rows], w.at[r, rows], w_sem.at[1 + i * 2 + core])

    w_loads = [pltpu.make_async_copy(wo_ref, w.at[0], w_sem.at[0])]
    w_loads += [early(i, r, core) for i, r in ((1, 1), (0, 3)) for core in (0, 1)]
    for cp in w_loads:
        cp.start()
    pl.semaphore_wait(barrier, 7)

    quarter = wo_ref.shape[0] // 4
    wo_copies = []

    def send_wo(src, n, target):
        rows = pl.ds(pl.multiple_of(c * (2 * quarter) + (n % 2) * quarter, quarter), quarter)
        cp = remote(src.at[rows], w.at[2, rows], wo_send.at[n], wo_recv.at[n], target)
        cp.start()
        wo_copies.append(cp)

    send_wo(won_ref.at[0], 0, yp)
    send_wo(won_ref.at[1], 1, ym)

    def late(n, hand):
        i, chunk = WO_LATE[n]
        rows = pl.ds(pl.multiple_of((c * WO_CHUNKS + chunk) * depth, depth), depth)
        dst = w.at[3 if i == 0 else 1, rows]
        target = partner if hand else (yp if i == 0 else ym)
        return remote(dst if hand else wo_ref.at[rows], dst, wo_send.at[4 + 2 * hand + n], wo_recv.at[4 + 2 * hand + n], target)

    for n in (0, 1):
        late(n, 0).start()

    quart = loc.shape[-1] // 2
    copies = {}

    def send(key, src, target):
        n = len(copies)
        cp = remote(src, recv.at[n], r_send.at[n], r_recv.at[n], target)
        cp.start()
        copies[key] = (cp, n)

    def got(key):
        cp, n = copies[key]
        cp.wait_recv()
        return recv.at[n]

    def piece(k, h, a, b, q):
        return loc.at[k * 2 + h, a * 4 + b, :, q * quart:(q + 1) * quart]

    def first_sends(k, b):
        for h in (0, 1):
            loads[k, h, 2, b].wait()
            send((k, h, b, "op"), piece(k, h, 2, b, 0), to(h, 1, 0))
            send((k, h, b, "om"), piece(k, h, 2, b, 1), to(h, -1, 0))

    def first_raw(k, b):
        for h in (0, 1):
            loads[k, h, 1, b].wait()
            send((k, h, b, "p1"), piece(k, h, 1, b, 1), to(h, 1, 0))
            loads[k, h, 3, b].wait()
            send((k, h, b, "m0"), piece(k, h, 3, b, 0), to(h, -1, 0))

    def first_sums(k, b):
        for h in (0, 1):
            r = got((k, h, b, "op"))
            merge(piece(k, h, 1, b, 0), piece(k, h, 1, b, 0), r)
            send((k, h, b, "p0"), piece(k, h, 1, b, 0), to(h, 1, 0))
            r = got((k, h, b, "om"))
            merge(piece(k, h, 3, b, 1), piece(k, h, 3, b, 1), r)
            send((k, h, b, "m1"), piece(k, h, 3, b, 1), to(h, -1, 0))

    def second_sends(k, b):
        for h in (0, 1):
            loads[k, h, 0, b].wait()
            for q in (1, 0):
                p = got((k, h, b, "p%d" % q))
                m = got((k, h, b, "m%d" % q))
                merge(piece(k, h, 0, b, q), piece(k, h, 0, b, q), p, m)
            if b == 2:
                send((k, h, "op"), piece(k, h, 0, 2, 0), to(h, 0, 1))
                send((k, h, "om"), piece(k, h, 0, 2, 1), to(h, 0, -1))
            if b == 1:
                send((k, h, "p1"), piece(k, h, 0, 1, 1), to(h, 0, 1))
            if b == 3:
                send((k, h, "m0"), piece(k, h, 0, 3, 0), to(h, 0, -1))

    def second_sums(k):
        for h in (0, 1):
            r = got((k, h, "op"))
            merge(piece(k, h, 0, 1, 0), piece(k, h, 0, 1, 0), r)
            send((k, h, "p0"), piece(k, h, 0, 1, 0), to(h, 0, 1))
            r = got((k, h, "om"))
            merge(piece(k, h, 0, 3, 1), piece(k, h, 0, 3, 1), r)
            send((k, h, "m1"), piece(k, h, 0, 3, 1), to(h, 0, -1))

    def last_sums(k):
        for h in (0, 1):
            for q in (1, 0):
                p = got((k, h, "p%d" % q))
                m = got((k, h, "m%d" % q))
                own = piece(k, h, 0, 0, q)
                merge(own, own, p, m)
                for g in range(quart // HD):
                    col = (h * 2 + q) * quart + g * HD
                    att[k, :, col:col + HD] = own[0:HD, g * HD:(g + 1) * HD].T

    half = BLK // 2
    lo, hi = pl.ds(0, half), pl.ds(half, half)

    def ring_of(k):
        n = k * 4
        return [
            remote(att.at[k], attz.at[k, 3], a_send.at[n], a_recv.at[n], zp),
            remote(att.at[k], attz.at[k, 1], a_send.at[n + 1], a_recv.at[n + 1], zm),
            remote(attz.at[k, 3, lo], attz.at[k, 2, lo], a_send.at[n + 2], a_recv.at[n + 2], zp),
            remote(attz.at[k, 1, hi], attz.at[k, 2, hi], a_send.at[n + 3], a_recv.at[n + 3], zm),
        ]

    def spread_of(k, src):
        n = k * 6
        return [
            remote(src, hb.at[k, 3], b_send.at[n], b_recv.at[n], yp),
            remote(src, hb.at[k, 1], b_send.at[n + 1], b_recv.at[n + 1], ym),
            remote(src.at[lo], relay.at[k, 0], b_send.at[n + 2], b_recv.at[n + 2], yp),
            remote(src.at[hi], relay.at[k, 1], b_send.at[n + 3], b_recv.at[n + 3], ym),
            remote(relay.at[k, 0], hb.at[k, 2, lo], b_send.at[n + 4], b_recv.at[n + 4], yp),
            remote(relay.at[k, 1], hb.at[k, 2, hi], b_send.at[n + 5], b_recv.at[n + 5], ym),
        ]

    def spread(k, dz):
        src = att.at[k] if dz == 0 else attz.at[k, dz]
        d = (dz - y + 4) % 4

        @pl.when(d == 0)
        def _():
            hb[k, 0] = src[...]

        @pl.when(d == 1)
        def _():
            spread_of(k, src)[0].start()

        @pl.when(d == 3)
        def _():
            spread_of(k, src)[1].start()

        @pl.when(d == 2)
        def _():
            spread_of(k, src)[2].start()
            spread_of(k, src)[3].start()

    def rows_out(k):
        r = ring_of(k)
        r[0].start()
        r[1].start()
        spread(k, 0)

    def rows_next(k):
        r = ring_of(k)
        r[0].wait_recv()
        r[2].start()
        spread(k, 3)
        r[1].wait_recv()
        r[3].start()
        spread(k, 1)

    def rows_far(k):
        r = ring_of(k)
        r[2].wait_recv()
        r[3].wait_recv()
        spread(k, 2)

    def rows_relay(k):
        sp = spread_of(k, att.at[k])
        for n in (0, 1):
            sp[2 + n].wait_recv()
            sp[4 + n].start()

    cols = wo_ref.shape[1]
    width = cols // NCH

    def term(k, r, first):
        def one(n, carry):
            sl = pl.ds(pl.multiple_of(n * 256, 256), 256)
            v = jnp.dot(hb[k, r], w[r, :, sl], preferred_element_type=F32)
            acc[k, :, sl] = v if first else acc[k, :, sl] + v
            return carry
        lax.fori_loop(0, cols // 256, one, 0)

    def terms_own(k):
        if k == 0:
            for cp in w_loads:
                cp.wait()
            for n in (0, 1):
                late(n, 1).wait_recv()
        term(k, 0, True)

    def terms_near(k, n):
        spread_of(k, att.at[k])[n].wait_recv()
        term(k, (3, 1)[n], False)

    def terms_far(k):
        sp = spread_of(k, att.at[k])
        sp[4].wait_recv()
        sp[5].wait_recv()

    def region(k, f, ch, rows=None):
        sl = pl.ds(pl.multiple_of(((f + 8) % 4) * cols + ch * width, width), width)
        first, size = (k * BLK, BLK) if rows is None else (k * BLK + rows * half, half)
        return out_ref.at[pl.ds(first, size), sl]

    def shifts(k, ch):
        n = (k * NCH + ch) * 5
        src = tile.at[k, ch]
        return [
            remote(src, region(k, z, ch), s_send.at[n], s_recv.at[n], zp),
            remote(src, region(k, z, ch), s_send.at[n], s_recv.at[n], zm),
            remote(src.at[lo], zrelay.at[k, ch, 0], s_send.at[n + 1], s_recv.at[n + 1], zp),
            remote(src.at[hi], zrelay.at[k, ch, 1], s_send.at[n + 2], s_recv.at[n + 2], zm),
            remote(zrelay.at[k, ch, 0], region(k, z - 1, ch, 0), s_send.at[n + 3], s_recv.at[n + 3], zp),
            remote(zrelay.at[k, ch, 1], region(k, z + 1, ch, 1), s_send.at[n + 4], s_recv.at[n + 4], zm),
        ]

    def home(k, ch):
        return pltpu.make_async_copy(tile.at[k, ch], region(k, z, ch), home_sem.at[k * NCH + ch])

    def bcast(k, ch):
        n = (k * NCH + ch) * 4
        mine = region(k, z - y, ch)
        up = region(k, z - y + 1, ch, 0)
        down = region(k, z - y - 1, ch, 1)
        return [
            remote(mine, mine, t_send.at[n], t_recv.at[n], yp),
            remote(mine, mine, t_send.at[n + 1], t_recv.at[n + 1], ym),
            remote(up, up, t_send.at[n + 2], t_recv.at[n + 2], yp),
            remote(down, down, t_send.at[n + 3], t_recv.at[n + 3], ym),
        ]

    def tile_fill(k, ch):
        for n in range(width // 256):
            sl = slice(ch * width + n * 256, ch * width + (n + 1) * 256)
            v = acc[k, :, sl] + jnp.dot(hb[k, 2], w[2, :, sl], preferred_element_type=F32)
            tile[k, ch, :, n * 256:(n + 1) * 256] = v.astype(BF16)

    def tile_start(k, ch):
        @pl.when(y == 0)
        def _():
            home(k, ch).start()

        @pl.when(y == 1)
        def _():
            shifts(k, ch)[0].start()

        @pl.when(y == 3)
        def _():
            shifts(k, ch)[1].start()

        @pl.when(y == 2)
        def _():
            shifts(k, ch)[2].start()
            shifts(k, ch)[3].start()

    def tile_relay(k, ch):
        @pl.when(y == 2)
        def _():
            sr = shifts(k, ch)
            sr[2].wait_recv()
            sr[4].start()
            sr[3].wait_recv()
            sr[5].start()

    def tile_home(k, ch):
        @pl.when(y == 0)
        def _():
            home(k, ch).wait()

        @pl.when(y % 2 == 1)
        def _():
            shifts(k, ch)[0].wait_recv()

        @pl.when(y == 2)
        def _():
            se = shifts(k, ch)
            se[4].wait_recv()
            se[5].wait_recv()

        b = bcast(k, ch)
        b[0].start()
        b[1].start()

    def tile_onward(k, ch):
        b = bcast(k, ch)
        b[0].wait_recv()
        b[2].start()
        b[1].wait_recv()
        b[3].start()

    for b in SECOND:
        first_sends(0, b)
    for b in SECOND:
        first_raw(0, b)
    for b in SECOND:
        first_sums(0, b)
    for b in SECOND:
        first_sends(1, b)
        second_sends(0, b)
    for n in (0, 1):
        wo_copies[n].wait_recv()
        send_wo(w.at[2], 2 + n, partner)
    second_sums(0)
    for b in SECOND:
        first_raw(1, b)
    last_sums(0)
    rows_out(0)
    for n in (0, 1):
        late(n, 0).wait_recv()
        late(n, 1).start()
    first_sums(1, 2)
    first_sums(1, 1)
    rows_next(0)
    first_sums(1, 3)
    first_sums(1, 0)
    rows_far(0)
    second_sends(1, 2)
    second_sends(1, 1)
    rows_relay(0)
    second_sends(1, 3)
    second_sends(1, 0)
    second_sums(1)
    last_sums(1)
    rows_out(1)
    terms_own(0)
    terms_near(0, 0)
    terms_near(0, 1)
    terms_far(0)
    wo_copies[2].wait_recv()
    wo_copies[3].wait_recv()
    rows_next(1)
    tile_fill(0, 0)
    tile_start(0, 0)
    tile_fill(0, 1)
    tile_start(0, 1)
    tile_fill(0, 2)
    tile_start(0, 2)
    tile_fill(0, 3)
    tile_start(0, 3)
    rows_far(1)
    tile_relay(0, 0)
    tile_home(0, 0)
    tile_relay(0, 1)
    tile_home(0, 1)
    rows_relay(1)
    tile_relay(0, 2)
    tile_home(0, 2)
    tile_relay(0, 3)
    tile_home(0, 3)
    terms_own(1)
    tile_onward(0, 0)
    terms_near(1, 0)
    tile_onward(0, 1)
    terms_near(1, 1)
    tile_onward(0, 2)
    tile_onward(0, 3)
    terms_far(1)
    tile_fill(1, 0)
    tile_start(1, 0)
    tile_fill(1, 1)
    tile_start(1, 1)
    tile_fill(1, 2)
    tile_start(1, 2)
    tile_fill(1, 3)
    tile_start(1, 3)
    tile_relay(1, 0)
    tile_relay(1, 1)
    tile_home(1, 0)
    tile_relay(1, 2)
    tile_home(1, 1)
    tile_relay(1, 3)
    tile_home(1, 2)
    tile_home(1, 3)
    tile_onward(1, 0)
    tile_onward(1, 1)
    tile_onward(1, 2)
    tile_onward(1, 3)
    for k in (0, 1):
        for ch in range(NCH):
            b = bcast(k, ch)
            b[2].wait_recv()
            b[3].wait_recv()
            for cp in b:
                cp.wait_send()

            @pl.when(y % 2 == 1)
            def _():
                shifts(k, ch)[0].wait_send()

            @pl.when(y == 2)
            def _():
                for cp in shifts(k, ch)[2:]:
                    cp.wait_send()
        for cp in ring_of(k) + spread_of(k, att.at[k]):
            cp.wait_send()
    for cp in wo_copies + [late(n, hand) for n in (0, 1) for hand in (0, 1)]:
        cp.wait_send()
    for cp, _ in copies.values():
        cp.wait_send()


N_REDUCE = 120


def finish(part, wo, won):
    rows, lanes = part.shape[-2:]
    depth, cols = wo.shape
    anyspec = pl.BlockSpec(memory_space=pl.ANY)
    sem = pltpu.SemaphoreType.DMA
    return pl.pallas_call(
        finish_kernel,
        out_shape=jax.ShapeDtypeStruct((2 * BLK, 4 * cols), BF16),
        in_specs=[anyspec] * 3,
        out_specs=anyspec,
        scratch_shapes=[
            pltpu.VMEM((4, 16, rows, lanes), BF16),
            pltpu.VMEM((N_REDUCE, rows, lanes // 2), BF16),
            pltpu.VMEM((2, BLK, depth), BF16),
            pltpu.VMEM((2, 4, BLK, depth), BF16),
            pltpu.VMEM((2, 4, BLK, depth), BF16),
            pltpu.VMEM((2, 2, BLK // 2, depth), BF16),
            pltpu.VMEM((4, depth, cols), BF16),
            pltpu.VMEM((2, BLK, cols), F32),
            pltpu.VMEM((2, NCH, BLK, cols // NCH), BF16),
            pltpu.VMEM((2, NCH, 2, BLK // 2, cols // NCH), BF16),
            sem((64,)), sem((N_REDUCE,)), sem((N_REDUCE,)), sem((8,)), sem((8,)), sem((5,)),
            sem((8,)), sem((8,)), sem((12,)), sem((12,)),
            sem((10 * NCH,)), sem((10 * NCH,)), sem((8 * NCH,)), sem((8 * NCH,)), sem((2 * NCH,)),
        ],
        compiler_params=pltpu.CompilerParams(
            collective_id=1, has_side_effects=True, vmem_limit_bytes=VMEM),
        name="finish",
    )(part, wo, won)


def emit_kernel(in_ref, out_ref):
    out_ref[...] = in_ref[...]


def emit(mixed):
    rows, cols = mixed.shape
    spec = pl.BlockSpec((64, cols), lambda i: (i, 0))
    return pl.pallas_call(
        emit_kernel,
        out_shape=jax.ShapeDtypeStruct(mixed.shape, mixed.dtype),
        grid=(rows // 64,),
        in_specs=[spec],
        out_specs=spec,
        compiler_params=pltpu.CompilerParams(vmem_limit_bytes=VMEM),
        name="emit",
    )(mixed)


def prepare_kernel(cb_local, slot_ref, pattern_ref, q_ref, tab_ref, out_ref):
    core = position()[2]
    for chip in range(16):
        for k in range(2):
            tab_ref[chip, 0, k * 16 + 15] = 0

    def one(e, carry):
        for k in range(2):
            slot = slot_ref[pattern_ref[k, e]]
            owner = slot // cb_local
            chip = owner // 2
            here = jnp.where(owner % 2 == core, 0, cb_local) + slot % cb_local
            n = tab_ref[chip, 0, k * 16 + 15]
            tab_ref[chip, 0, k * 16 + n] = here
            tab_ref[chip, 0, k * 16 + 15] = n + 1
        return carry

    lax.fori_loop(0, pattern_ref.shape[1], one, 0)
    for color in range(2):
        for g in range(q_ref.shape[1] // HD):
            out_ref[color, :, g * BLK:(g + 1) * BLK] = q_ref[color * BLK:(color + 1) * BLK, g * HD:(g + 1) * HD].T


def prepare(block_slot, pattern, queries, cb_local):
    return pl.pallas_call(
        functools.partial(prepare_kernel, cb_local),
        out_shape=(jax.ShapeDtypeStruct((16, 1, 128), jnp.int32),
                   jax.ShapeDtypeStruct((2, HD, queries.shape[1]), BF16)),
        in_specs=[pl.BlockSpec(memory_space=pltpu.SMEM)] * 2 + [pl.BlockSpec(memory_space=pltpu.VMEM)],
        out_specs=(pl.BlockSpec(memory_space=pltpu.SMEM), pl.BlockSpec(memory_space=pltpu.VMEM)),
        compiler_params=pltpu.CompilerParams(vmem_limit_bytes=VMEM),
        name="prepare",
    )(block_slot, pattern, queries)


def body(queries, span_k, span_v, cache_k, cache_v, block_slot, pattern, wo):
    tab, q = prepare(block_slot, pattern, queries, cache_k.shape[0])
    q_all, pk, pv, prev, tab_all, won = gather_queries(q, cache_k, cache_v, span_k, span_v, tab, wo)
    part = attend(tab_all, q_all, cache_k, cache_v, pk, pv, span_k, span_v, prev)
    return emit(finish(part, wo, won))


def solution(mesh):
    return jax.shard_map(
        body,
        mesh=mesh,
        in_specs=(
            P(("fsdp", "seq"), "head"),
            P(("fsdp", "seq"), "head"),
            P(("fsdp", "seq"), "head"),
            P(("fsdp", "seq"), None, "head"),
            P(("fsdp", "seq"), None, "head"),
            P(),
            P(("fsdp", "seq"), None),
            P("head", "fsdp"),
        ),
        out_specs=P(("fsdp", "seq"), None),
        check_vma=False,
    )
```

```python
import functools

import jax
import jax.numpy as jnp
from jax import lax
from jax.experimental import pallas as pl
from jax.experimental.pallas import tpu as pltpu
from jax.sharding import PartitionSpec as P

HD = 128
BLK = 128
EXTRA = 8
WO_CHUNKS = 4
WO_LATE = ((0, 3), (1, 0))
NEG = -1e30
VMEM = 62 * 2**20
MESH = pl.DeviceIdType.MESH
BF16 = jnp.bfloat16
F32 = jnp.float32
LOG2E = 1.4426950408889634


def position():
    z = lax.axis_index("fsdp")
    s = lax.axis_index("seq")
    y = lax.axis_index("head")
    return z, s // 2, s % 2, y


def dev(z, x, c, y):
    return ((z + 4) % 4, ((x + 4) % 4) * 2 + c, (y + 4) % 4)


def gather_kernel(q_ref, ck_ref, cv_ref, sk_ref, sv_ref, tab_ref, wo_ref,
                  qall_ref, pk_ref, pv_ref, prev_ref, taball_ref, won_ref,
                  send_sem, recv_sem, loc_sem):
    z, x, c, y = position()
    far_z, far_x = (z, x + jnp.where(c == 0, -1, 1))
    wrap = jnp.where(c == 0, jnp.where(x == 0, -1, 0), jnp.where(x == 3, 1, 0))
    far_z = far_z + wrap

    barrier = pltpu.get_barrier_semaphore()
    for off in range(1, 16):
        pl.semaphore_signal(barrier, inc=1, device_id=dev(z + off // 4, x + off % 4, c, y), device_id_type=MESH)
    pl.semaphore_signal(barrier, inc=1, device_id=dev(z, x, 1 - c, y), device_id_type=MESH)
    pl.semaphore_signal(barrier, inc=1, device_id=dev(far_z, far_x, 1 - c, y), device_id_type=MESH)
    for d in (1, -1):
        pl.semaphore_signal(barrier, inc=1, device_id=dev(z, x, c, y + d), device_id_type=MESH)
    pl.semaphore_wait(barrier, 19)

    copies = []

    def send(src, dst, target):
        k = len(copies)
        cp = pltpu.make_async_remote_copy(
            src_ref=src, dst_ref=dst, send_sem=send_sem.at[k], recv_sem=recv_sem.at[k],
            device_id=target, device_id_type=MESH)
        cp.start()
        copies.append(cp)
        return cp

    def slot(dz, dx):
        return ((z + dz + 4) % 4) * 4 + (x + dx + 4) % 4

    here = slot(0, 0)
    tables = []
    for off in range(1, 16):
        dz, dx = off // 4, off % 4
        tables.append(send(tab_ref.at[slot(dz, dx)], taball_ref.at[here], dev(z + dz, x + dx, c, y)))
    nxt_x = x + jnp.where(c == 0, 0, 1)
    nxt_z = z + jnp.where((c == 1) & (x == 3), 1, 0)
    nxt = dev(nxt_z, nxt_x, 1 - c, y)
    send(sk_ref.at[pl.ds(BLK, BLK)], prev_ref.at[0], nxt)
    send(sv_ref.at[pl.ds(BLK, BLK)], prev_ref.at[1], nxt)

    def step(color, major, minor):
        return (minor, major) if color == 0 else (major, minor)

    def chunk(color, a, b, half=None):
        dz, dx = step(color, a, b)
        ref = qall_ref.at[slot(dz, dx), color]
        if half is None:
            return ref
        return ref.at[pl.ds(half * (BLK // 2), BLK // 2)]

    def to(color, a, b):
        dz, dx = step(color, a, b)
        return dev(z + dz, x + dx, c, y)

    ring = {}

    def own(color):
        mine, dst = q_ref.at[color], qall_ref.at[here, color]
        for d in (1, -1):
            ring[color, "a", d] = send(mine, dst, to(color, d, 0))
        for d in (1, -1):
            ring[color, "b", 0, d] = send(mine, dst, to(color, 0, d))

    own(0)
    own(1)
    depth = wo_ref.shape[0] // (2 * WO_CHUNKS)

    def share(n):
        return pl.ds(pl.multiple_of((c * WO_CHUNKS + n) * depth, depth), depth)

    wo_in = []
    for n in range(WO_CHUNKS):
        for i, d in ((0, 1), (1, -1)):
            if (i, n) not in WO_LATE:
                wo_in.append((i, n, send(wo_ref.at[share(n)], won_ref.at[i, share(n)], dev(z, x, c, y + d))))

    def hand_over(count):
        for _ in range(count):
            i, n, cp = wo_in[len(handed)]
            handed.append(cp)
            cp.wait_recv()
            send(won_ref.at[i, share(n)], won_ref.at[i, share(n)], partner)

    handed = []
    partner = dev(z, x, 1 - c, y)
    send(ck_ref, pk_ref, partner)
    send(cv_ref, pv_ref, partner)
    locals_ = [pltpu.make_async_copy(q_ref, qall_ref.at[here], loc_sem.at[0]),
               pltpu.make_async_copy(tab_ref.at[here], taball_ref.at[here], loc_sem.at[1])]
    for cp in locals_:
        cp.start()

    for d in (1, -1):
        for color in (0, 1):
            ring[color, "a", d].wait_recv()
            half = 0 if d == 1 else 1
            part = chunk(color, -d, 0, half)
            ring[color, "o", d] = send(part, part, to(color, d, 0))
            whole = chunk(color, -d, 0)
            for e in (1, -1):
                ring[color, "b", -d, e] = send(whole, whole, to(color, 0, e))
    for d in (1, -1):
        for color in (0, 1):
            ring[color, "b", 0, d].wait_recv()
            part = chunk(color, 0, -d, 0 if d == 1 else 1)
            ring[color, "c", 0, d] = send(part, part, to(color, 0, d))
    for color in (0, 1):
        ring[color, "o", 1].wait_recv()
        ring[color, "o", -1].wait_recv()
        whole = chunk(color, 2, 0)
        for e in (1, -1):
            ring[color, "b", 2, e] = send(whole, whole, to(color, 0, e))
    for a in (-1, 1, 2):
        hand_over(2)
        for d in (1, -1):
            for color in (0, 1):
                ring[color, "b", a, d].wait_recv()
                part = chunk(color, a, -d, 0 if d == 1 else 1)
                ring[color, "c", a, d] = send(part, part, to(color, 0, d))
    hand_over(len(wo_in) - len(handed))
    waited = {id(v) for k, v in ring.items() if k[1] != "c"} | {id(cp) for cp in handed}
    for cp in copies:
        if id(cp) not in waited:
            cp.wait_recv()
    for cp in copies:
        cp.wait_send()
    for cp in locals_:
        cp.wait()


N_GATHER = 15 + 2 + 8 + 2 + 4 + 8 + 4 + 4 + 12 + 2 * (2 * WO_CHUNKS - len(WO_LATE))


def gather_queries(q, ck, cv, sk, sv, tab, wo):
    anyspec = pl.BlockSpec(memory_space=pl.ANY)
    return pl.pallas_call(
        gather_kernel,
        out_shape=(
            jax.ShapeDtypeStruct((16, 2, BLK, q.shape[-1]), BF16),
            jax.ShapeDtypeStruct(ck.shape, BF16),
            jax.ShapeDtypeStruct(cv.shape, BF16),
            jax.ShapeDtypeStruct((2, BLK, HD), BF16),
            jax.ShapeDtypeStruct(tab.shape, jnp.int32),
            jax.ShapeDtypeStruct((2,) + wo.shape, BF16),
        ),
        in_specs=[anyspec] * 7,
        out_specs=[anyspec] * 6,
        scratch_shapes=[
            pltpu.SemaphoreType.DMA((N_GATHER,)),
            pltpu.SemaphoreType.DMA((N_GATHER,)),
            pltpu.SemaphoreType.DMA((2,)),
        ],
        compiler_params=pltpu.CompilerParams(collective_id=0, has_side_effects=True, vmem_limit_bytes=VMEM),
        name="gather_queries",
    )(q, ck, cv, sk, sv, tab, wo)


def attend_kernel(tab_ref, q_ref, ck_ref, cv_ref, pk_ref, pv_ref, sk_ref, sv_ref, prev_ref, out_ref,
                  kall, vall, span, sbuf, pbuf, m_s, l_s, acc, sems):
    i = pl.program_id(0)
    z, x, c, y = position()
    chip = i // 2
    color = i % 2
    mine = chip == z * 4 + x

    @pl.when(i == 0)
    def _():
        loads = [
            pltpu.make_async_copy(ck_ref, kall.at[pl.ds(0, 64)], sems.at[0]),
            pltpu.make_async_copy(pk_ref, kall.at[pl.ds(64, 64)], sems.at[1]),
            pltpu.make_async_copy(cv_ref, vall.at[pl.ds(0, 64)], sems.at[2]),
            pltpu.make_async_copy(pv_ref, vall.at[pl.ds(64, 64)], sems.at[3]),
            pltpu.make_async_copy(prev_ref.at[0], span.at[0, pl.ds(0, BLK)], sems.at[4]),
            pltpu.make_async_copy(prev_ref.at[1], span.at[1, pl.ds(0, BLK)], sems.at[5]),
            pltpu.make_async_copy(sk_ref, span.at[0, pl.ds(BLK, 2 * BLK)], sems.at[6]),
            pltpu.make_async_copy(sv_ref, span.at[1, pl.ds(BLK, 2 * BLK)], sems.at[7]),
        ]
        for cp in loads:
            cp.start()
        for cp in loads:
            cp.wait()

    heads = q_ref.shape[-1] // HD
    m_s[...] = jnp.full_like(m_s, NEG)
    l_s[...] = jnp.zeros_like(l_s)
    acc[...] = jnp.zeros_like(acc)
    scale = LOG2E / (HD ** 0.5)
    width = 256

    def pair(keys, values, bias):
        rows = keys.shape[0]
        spans = [slice(t * width, (t + 1) * width) for t in range(heads * HD // width)]
        tops = []
        for cols in spans:
            s = jnp.dot(keys, q_ref[0, 0, :, cols], preferred_element_type=F32)
            if bias is not None:
                s = s + bias
            sbuf[0:rows, cols] = s
            tops.append(jnp.maximum(m_s[:, cols], jnp.max(s, axis=0, keepdims=True)))
        olds = []
        for cols, top in zip(spans, tops):
            old = jnp.exp2((m_s[:, cols] - top) * scale)
            p = jnp.exp2((sbuf[0:rows, cols] - top) * scale)
            pbuf[0:rows, cols] = p.astype(BF16)
            m_s[:, cols] = top
            l_s[:, cols] = l_s[:, cols] * old + jnp.sum(p, axis=0, keepdims=True)
            olds.append(old)
        for cols, old in zip(spans, olds):
            acc[:, cols] = acc[:, cols] * old + lax.dot_general(
                values, pbuf[0:rows, cols], (((0,), (0,)), ((), ())), preferred_element_type=F32)

    count = tab_ref[chip, 0, color * 16 + 15]
    base = color * 16

    def group(start, size):
        ids = [tab_ref[chip, 0, base + start + n] for n in range(size)]
        pair(jnp.concatenate([kall[n] for n in ids], axis=0), jnp.concatenate([vall[n] for n in ids], axis=0), None)

    def four(j, carry):
        group(4 * j, 4)
        return carry

    fours = count // 4
    lax.fori_loop(0, fours, four, 0)
    for size in (1, 2, 3):
        @pl.when(count % 4 == size)
        def _():
            group(4 * fours, size)

    @pl.when(mine)
    def _():
        rows = pl.ds(pl.multiple_of(color * BLK, BLK), 2 * BLK)
        key = lax.broadcasted_iota(jnp.int32, (2 * BLK, width), 0)
        tok = lax.broadcasted_iota(jnp.int32, (2 * BLK, width), 1) % BLK
        first = (z * 8 + x * 2 + c) * 2 + color == 0
        low = jnp.where(first, BLK, 0)
        allowed = (key >= low) & (key - BLK <= tok)
        pair(span[0, rows, :], span[1, rows, :], jnp.where(allowed, 0.0, 2 * NEG))

    some = l_s[...] > 0
    total = jnp.where(some, l_s[...], 1.0)
    lse = m_s[...] * scale + jnp.log2(total)
    hi = lse.astype(BF16)
    rest = lse - hi.astype(F32)
    mid = rest.astype(BF16)
    low_ = (rest - mid.astype(F32)).astype(BF16)
    o = (acc[...] * (1.0 / total)).astype(BF16)
    row = lax.broadcasted_iota(jnp.int32, (EXTRA, lse.shape[1]), 0)
    tail = jnp.where(row == 0, hi.astype(F32), jnp.where(row == 1, mid.astype(F32), jnp.where(row == 2, low_.astype(F32), 0.0))).astype(BF16)
    half = lse.shape[1] // 2
    for h in range(2):
        out_ref[0, 0, h, 0:HD, :] = o[:, h * half:(h + 1) * half]
        out_ref[0, 0, h, HD:HD + EXTRA, :] = tail[:, h * half:(h + 1) * half]


def attend(tab, q_all, ck, cv, pk, pv, sk, sv, prev):
    width = q_all.shape[-1]
    anyspec = pl.BlockSpec(memory_space=pl.ANY)
    return pl.pallas_call(
        attend_kernel,
        out_shape=jax.ShapeDtypeStruct((16, 2, 2, HD + EXTRA, width // 2), BF16),
        grid_spec=pltpu.PrefetchScalarGridSpec(
            num_scalar_prefetch=1,
            grid=(32,),
            in_specs=[pl.BlockSpec((1, 1, BLK, width), lambda i, t: (i // 2, i % 2, 0, 0))] + [anyspec] * 7,
            out_specs=pl.BlockSpec((1, 1, 2, HD + EXTRA, width // 2), lambda i, t: (i // 2, i % 2, 0, 0, 0)),
            scratch_shapes=[
                pltpu.VMEM((128, BLK, HD), BF16),
                pltpu.VMEM((128, BLK, HD), BF16),
                pltpu.VMEM((2, 3 * BLK, HD), BF16),
                pltpu.VMEM((4 * BLK, width), F32),
                pltpu.VMEM((4 * BLK, width), BF16),
                pltpu.VMEM((1, width), F32),
                pltpu.VMEM((1, width), F32),
                pltpu.VMEM((HD, width), F32),
                pltpu.SemaphoreType.DMA((8,)),
            ],
        ),
        compiler_params=pltpu.CompilerParams(
            vmem_limit_bytes=VMEM),
        cost_estimate=pl.CostEstimate(flops=7_000_000_000, bytes_accessed=26_000_000, transcendentals=13_000_000),
        name="attend",
    )(tab, q_all, ck, cv, pk, pv, sk, sv, prev)


def merge(dst, *srcs):
    def lse_of(ref):
        t = ref[HD:HD + EXTRA, :].astype(F32)
        return t[0:1] + t[1:2] + t[2:3]

    lses = [lse_of(r) for r in srcs]
    top = functools.reduce(jnp.maximum, lses)
    ws = [jnp.exp2(v - top) for v in lses]
    total = functools.reduce(lambda a, b: a + b, ws)
    inv = 1.0 / total
    ws = [w * inv for w in ws]
    lse = top + jnp.log2(total)
    rows = 32

    def body(r, carry):
        sl = pl.ds(pl.multiple_of(r * rows, rows), rows)
        out = ws[0] * srcs[0][sl, :].astype(F32)
        for w, ref in zip(ws[1:], srcs[1:]):
            out = out + w * ref[sl, :].astype(F32)
        dst[sl, :] = out.astype(BF16)
        return carry

    lax.fori_loop(0, HD // rows, body, 0)
    hi = lse.astype(BF16).astype(F32)
    mid = (lse - hi).astype(BF16).astype(F32)
    low = lse - hi - mid
    row = lax.broadcasted_iota(jnp.int32, (EXTRA, lse.shape[1]), 0)
    dst[HD:HD + EXTRA, :] = jnp.where(row == 0, hi, jnp.where(row == 1, mid, jnp.where(row == 2, low, 0.0))).astype(BF16)


NCH = 4
SECOND = (2, 1, 3, 0)


def finish_kernel(part_ref, wo_ref, won_ref, out_ref,
                  loc, recv, att, attz, hb, relay, w, acc, tile, zrelay,
                  load_sem, r_send, r_recv, wo_send, wo_recv, w_sem,
                  a_send, a_recv, b_send, b_recv, s_send, s_recv, t_send, t_recv, home_sem):
    z, x, c, y = position()
    partner = dev(z, x, 1 - c, y)
    zp, zm = dev(z + 1, x, c, y), dev(z - 1, x, c, y)
    yp, ym = dev(z, x, c, y + 1), dev(z, x, c, y - 1)
    barrier = pltpu.get_barrier_semaphore()
    for target in (zp, zm, dev(z, x + 1, c, y), dev(z, x - 1, c, y), yp, ym, partner):
        pl.semaphore_signal(barrier, inc=1, device_id=target, device_id_type=MESH)

    def remote(src, dst, ssem, rsem, target):
        return pltpu.make_async_remote_copy(
            src_ref=src, dst_ref=dst, send_sem=ssem, recv_sem=rsem, device_id=target, device_id_type=MESH)

    def step(h, a, b):
        return (a, b) if h == 0 else (b, a)

    def to(h, a, b):
        dz, dx = step(h, a, b)
        return dev(z + dz, x + dx, c, y)

    loads = {}
    for k in (0, 1):
        for a in (2, 1, 3, 0):
            for b in SECOND:
                for h in (0, 1):
                    dz, dx = step(h, a, b)
                    slot = ((z + dz) % 4) * 4 + (x + dx) % 4
                    cp = pltpu.make_async_copy(part_ref.at[slot, k, h], loc.at[k * 2 + h, a * 4 + b], load_sem.at[len(loads)])
                    cp.start()
                    loads[k, h, a, b] = cp
    depth = wo_ref.shape[0] // (2 * WO_CHUNKS)

    def early(i, r, core):
        first = core * WO_CHUNKS + (0 if i == 0 else 1)
        rows = pl.ds(first * depth, (WO_CHUNKS - 1) * depth)
        return pltpu.make_async_copy(won_ref.at[i, rows], w.at[r, rows], w_sem.at[1 + i * 2 + core])

    w_loads = [pltpu.make_async_copy(wo_ref, w.at[0], w_sem.at[0])]
    w_loads += [early(i, r, core) for i, r in ((1, 1), (0, 3)) for core in (0, 1)]
    for cp in w_loads:
        cp.start()
    pl.semaphore_wait(barrier, 7)

    quarter = wo_ref.shape[0] // 4
    wo_copies = []

    def send_wo(src, n, target):
        rows = pl.ds(pl.multiple_of(c * (2 * quarter) + (n % 2) * quarter, quarter), quarter)
        cp = remote(src.at[rows], w.at[2, rows], wo_send.at[n], wo_recv.at[n], target)
        cp.start()
        wo_copies.append(cp)

    send_wo(won_ref.at[0], 0, yp)
    send_wo(won_ref.at[1], 1, ym)

    def late(n, hand):
        i, chunk = WO_LATE[n]
        rows = pl.ds(pl.multiple_of((c * WO_CHUNKS + chunk) * depth, depth), depth)
        dst = w.at[3 if i == 0 else 1, rows]
        target = partner if hand else (yp if i == 0 else ym)
        return remote(dst if hand else wo_ref.at[rows], dst, wo_send.at[4 + 2 * hand + n], wo_recv.at[4 + 2 * hand + n], target)

    for n in (0, 1):
        late(n, 0).start()

    quart = loc.shape[-1] // 2
    copies = {}

    def send(key, src, target):
        n = len(copies)
        cp = remote(src, recv.at[n], r_send.at[n], r_recv.at[n], target)
        cp.start()
        copies[key] = (cp, n)

    def got(key):
        cp, n = copies[key]
        cp.wait_recv()
        return recv.at[n]

    def piece(k, h, a, b, q):
        return loc.at[k * 2 + h, a * 4 + b, :, q * quart:(q + 1) * quart]

    def first_sends(k, b):
        for h in (0, 1):
            loads[k, h, 2, b].wait()
            send((k, h, b, "op"), piece(k, h, 2, b, 0), to(h, 1, 0))
            send((k, h, b, "om"), piece(k, h, 2, b, 1), to(h, -1, 0))

    def first_raw(k, b):
        for h in (0, 1):
            loads[k, h, 1, b].wait()
            send((k, h, b, "p1"), piece(k, h, 1, b, 1), to(h, 1, 0))
            loads[k, h, 3, b].wait()
            send((k, h, b, "m0"), piece(k, h, 3, b, 0), to(h, -1, 0))

    def first_sums(k, b):
        for h in (0, 1):
            r = got((k, h, b, "op"))
            merge(piece(k, h, 1, b, 0), piece(k, h, 1, b, 0), r)
            send((k, h, b, "p0"), piece(k, h, 1, b, 0), to(h, 1, 0))
            r = got((k, h, b, "om"))
            merge(piece(k, h, 3, b, 1), piece(k, h, 3, b, 1), r)
            send((k, h, b, "m1"), piece(k, h, 3, b, 1), to(h, -1, 0))

    def second_sends(k, b):
        for h in (0, 1):
            loads[k, h, 0, b].wait()
            for q in (1, 0):
                p = got((k, h, b, "p%d" % q))
                m = got((k, h, b, "m%d" % q))
                merge(piece(k, h, 0, b, q), piece(k, h, 0, b, q), p, m)
            if b == 2:
                send((k, h, "op"), piece(k, h, 0, 2, 0), to(h, 0, 1))
                send((k, h, "om"), piece(k, h, 0, 2, 1), to(h, 0, -1))
            if b == 1:
                send((k, h, "p1"), piece(k, h, 0, 1, 1), to(h, 0, 1))
            if b == 3:
                send((k, h, "m0"), piece(k, h, 0, 3, 0), to(h, 0, -1))

    def second_sums(k):
        for h in (0, 1):
            r = got((k, h, "op"))
            merge(piece(k, h, 0, 1, 0), piece(k, h, 0, 1, 0), r)
            send((k, h, "p0"), piece(k, h, 0, 1, 0), to(h, 0, 1))
            r = got((k, h, "om"))
            merge(piece(k, h, 0, 3, 1), piece(k, h, 0, 3, 1), r)
            send((k, h, "m1"), piece(k, h, 0, 3, 1), to(h, 0, -1))

    def last_sums(k):
        for h in (0, 1):
            for q in (1, 0):
                p = got((k, h, "p%d" % q))
                m = got((k, h, "m%d" % q))
                own = piece(k, h, 0, 0, q)
                merge(own, own, p, m)
                for g in range(quart // HD):
                    col = (h * 2 + q) * quart + g * HD
                    att[k, :, col:col + HD] = own[0:HD, g * HD:(g + 1) * HD].T

    half = BLK // 2
    lo, hi = pl.ds(0, half), pl.ds(half, half)

    def ring_of(k):
        n = k * 4
        return [
            remote(att.at[k], attz.at[k, 3], a_send.at[n], a_recv.at[n], zp),
            remote(att.at[k], attz.at[k, 1], a_send.at[n + 1], a_recv.at[n + 1], zm),
            remote(attz.at[k, 3, lo], attz.at[k, 2, lo], a_send.at[n + 2], a_recv.at[n + 2], zp),
            remote(attz.at[k, 1, hi], attz.at[k, 2, hi], a_send.at[n + 3], a_recv.at[n + 3], zm),
        ]

    def spread_of(k, src):
        n = k * 6
        return [
            remote(src, hb.at[k, 3], b_send.at[n], b_recv.at[n], yp),
            remote(src, hb.at[k, 1], b_send.at[n + 1], b_recv.at[n + 1], ym),
            remote(src.at[lo], relay.at[k, 0], b_send.at[n + 2], b_recv.at[n + 2], yp),
            remote(src.at[hi], relay.at[k, 1], b_send.at[n + 3], b_recv.at[n + 3], ym),
            remote(relay.at[k, 0], hb.at[k, 2, lo], b_send.at[n + 4], b_recv.at[n + 4], yp),
            remote(relay.at[k, 1], hb.at[k, 2, hi], b_send.at[n + 5], b_recv.at[n + 5], ym),
        ]

    def spread(k, dz):
        src = att.at[k] if dz == 0 else attz.at[k, dz]
        d = (dz - y + 4) % 4

        @pl.when(d == 0)
        def _():
            hb[k, 0] = src[...]

        @pl.when(d == 1)
        def _():
            spread_of(k, src)[0].start()

        @pl.when(d == 3)
        def _():
            spread_of(k, src)[1].start()

        @pl.when(d == 2)
        def _():
            spread_of(k, src)[2].start()
            spread_of(k, src)[3].start()

    def rows_out(k):
        r = ring_of(k)
        r[0].start()
        r[1].start()
        spread(k, 0)

    def rows_next(k):
        r = ring_of(k)
        r[0].wait_recv()
        r[2].start()
        spread(k, 3)
        r[1].wait_recv()
        r[3].start()
        spread(k, 1)

    def rows_far(k):
        r = ring_of(k)
        r[2].wait_recv()
        r[3].wait_recv()
        spread(k, 2)

    def rows_relay(k):
        sp = spread_of(k, att.at[k])
        for n in (0, 1):
            sp[2 + n].wait_recv()
            sp[4 + n].start()

    cols = wo_ref.shape[1]
    width = cols // NCH

    def term(k, r, first):
        def one(n, carry):
            sl = pl.ds(pl.multiple_of(n * 256, 256), 256)
            v = jnp.dot(hb[k, r], w[r, :, sl], preferred_element_type=F32)
            acc[k, :, sl] = v if first else acc[k, :, sl] + v
            return carry
        lax.fori_loop(0, cols // 256, one, 0)

    def terms_own(k):
        if k == 0:
            for cp in w_loads:
                cp.wait()
            for n in (0, 1):
                late(n, 1).wait_recv()
        term(k, 0, True)

    def terms_near(k, n):
        spread_of(k, att.at[k])[n].wait_recv()
        term(k, (3, 1)[n], False)

    def terms_far(k):
        sp = spread_of(k, att.at[k])
        sp[4].wait_recv()
        sp[5].wait_recv()

    def region(k, f, ch, rows=None):
        sl = pl.ds(pl.multiple_of(((f + 8) % 4) * cols + ch * width, width), width)
        first, size = (k * BLK, BLK) if rows is None else (k * BLK + rows * half, half)
        return out_ref.at[pl.ds(first, size), sl]

    def shifts(k, ch):
        n = (k * NCH + ch) * 5
        src = tile.at[k, ch]
        return [
            remote(src, region(k, z, ch), s_send.at[n], s_recv.at[n], zp),
            remote(src, region(k, z, ch), s_send.at[n], s_recv.at[n], zm),
            remote(src.at[lo], zrelay.at[k, ch, 0], s_send.at[n + 1], s_recv.at[n + 1], zp),
            remote(src.at[hi], zrelay.at[k, ch, 1], s_send.at[n + 2], s_recv.at[n + 2], zm),
            remote(zrelay.at[k, ch, 0], region(k, z - 1, ch, 0), s_send.at[n + 3], s_recv.at[n + 3], zp),
            remote(zrelay.at[k, ch, 1], region(k, z + 1, ch, 1), s_send.at[n + 4], s_recv.at[n + 4], zm),
        ]

    def home(k, ch):
        return pltpu.make_async_copy(tile.at[k, ch], region(k, z, ch), home_sem.at[k * NCH + ch])

    def bcast(k, ch):
        n = (k * NCH + ch) * 4
        mine = region(k, z - y, ch)
        up = region(k, z - y + 1, ch, 0)
        down = region(k, z - y - 1, ch, 1)
        return [
            remote(mine, mine, t_send.at[n], t_recv.at[n], yp),
            remote(mine, mine, t_send.at[n + 1], t_recv.at[n + 1], ym),
            remote(up, up, t_send.at[n + 2], t_recv.at[n + 2], yp),
            remote(down, down, t_send.at[n + 3], t_recv.at[n + 3], ym),
        ]

    def tile_fill(k, ch):
        for n in range(width // 256):
            sl = slice(ch * width + n * 256, ch * width + (n + 1) * 256)
            v = acc[k, :, sl] + jnp.dot(hb[k, 2], w[2, :, sl], preferred_element_type=F32)
            tile[k, ch, :, n * 256:(n + 1) * 256] = v.astype(BF16)

    def tile_start(k, ch):
        @pl.when(y == 0)
        def _():
            home(k, ch).start()

        @pl.when(y == 1)
        def _():
            shifts(k, ch)[0].start()

        @pl.when(y == 3)
        def _():
            shifts(k, ch)[1].start()

        @pl.when(y == 2)
        def _():
            shifts(k, ch)[2].start()
            shifts(k, ch)[3].start()

    def tile_relay(k, ch):
        @pl.when(y == 2)
        def _():
            sr = shifts(k, ch)
            sr[2].wait_recv()
            sr[4].start()
            sr[3].wait_recv()
            sr[5].start()

    def tile_home(k, ch):
        @pl.when(y == 0)
        def _():
            home(k, ch).wait()

        @pl.when(y % 2 == 1)
        def _():
            shifts(k, ch)[0].wait_recv()

        @pl.when(y == 2)
        def _():
            se = shifts(k, ch)
            se[4].wait_recv()
            se[5].wait_recv()

        b = bcast(k, ch)
        b[0].start()
        b[1].start()

    def tile_onward(k, ch):
        b = bcast(k, ch)
        b[0].wait_recv()
        b[2].start()
        b[1].wait_recv()
        b[3].start()

    for b in SECOND:
        first_sends(0, b)
    for b in SECOND:
        first_raw(0, b)
    for b in SECOND:
        first_sums(0, b)
    for b in SECOND:
        first_sends(1, b)
        second_sends(0, b)
    second_sums(0)
    for b in SECOND:
        first_raw(1, b)
    last_sums(0)
    rows_out(0)
    for n in (0, 1):
        wo_copies[n].wait_recv()
        send_wo(w.at[2], 2 + n, partner)
    first_sums(1, 2)
    first_sums(1, 1)
    rows_next(0)
    first_sums(1, 3)
    first_sums(1, 0)
    rows_far(0)
    for n in (0, 1):
        late(n, 0).wait_recv()
        late(n, 1).start()
    second_sends(1, 2)
    second_sends(1, 1)
    rows_relay(0)
    second_sends(1, 3)
    second_sends(1, 0)
    second_sums(1)
    last_sums(1)
    rows_out(1)
    terms_own(0)
    terms_near(0, 0)
    terms_near(0, 1)
    terms_far(0)
    wo_copies[2].wait_recv()
    wo_copies[3].wait_recv()
    rows_next(1)
    tile_fill(0, 0)
    tile_start(0, 0)
    tile_fill(0, 1)
    tile_start(0, 1)
    tile_fill(0, 2)
    tile_start(0, 2)
    tile_fill(0, 3)
    tile_start(0, 3)
    rows_far(1)
    tile_relay(0, 0)
    tile_home(0, 0)
    tile_relay(0, 1)
    tile_home(0, 1)
    rows_relay(1)
    tile_relay(0, 2)
    tile_home(0, 2)
    tile_relay(0, 3)
    tile_home(0, 3)
    terms_own(1)
    tile_onward(0, 0)
    terms_near(1, 0)
    tile_onward(0, 1)
    terms_near(1, 1)
    tile_onward(0, 2)
    tile_onward(0, 3)
    terms_far(1)
    tile_fill(1, 0)
    tile_start(1, 0)
    tile_fill(1, 1)
    tile_start(1, 1)
    tile_fill(1, 2)
    tile_start(1, 2)
    tile_fill(1, 3)
    tile_start(1, 3)
    tile_relay(1, 0)
    tile_relay(1, 1)
    tile_home(1, 0)
    tile_relay(1, 2)
    tile_home(1, 1)
    tile_relay(1, 3)
    tile_home(1, 2)
    tile_home(1, 3)
    tile_onward(1, 0)
    tile_onward(1, 1)
    tile_onward(1, 2)
    tile_onward(1, 3)
    for k in (0, 1):
        for ch in range(NCH):
            b = bcast(k, ch)
            b[2].wait_recv()
            b[3].wait_recv()
            for cp in b:
                cp.wait_send()

            @pl.when(y % 2 == 1)
            def _():
                shifts(k, ch)[0].wait_send()

            @pl.when(y == 2)
            def _():
                for cp in shifts(k, ch)[2:]:
                    cp.wait_send()
        for cp in ring_of(k) + spread_of(k, att.at[k]):
            cp.wait_send()
    for cp in wo_copies + [late(n, hand) for n in (0, 1) for hand in (0, 1)]:
        cp.wait_send()
    for cp, _ in copies.values():
        cp.wait_send()


N_REDUCE = 120


def finish(part, wo, won):
    rows, lanes = part.shape[-2:]
    depth, cols = wo.shape
    anyspec = pl.BlockSpec(memory_space=pl.ANY)
    sem = pltpu.SemaphoreType.DMA
    return pl.pallas_call(
        finish_kernel,
        out_shape=jax.ShapeDtypeStruct((2 * BLK, 4 * cols), BF16),
        in_specs=[anyspec] * 3,
        out_specs=anyspec,
        scratch_shapes=[
            pltpu.VMEM((4, 16, rows, lanes), BF16),
            pltpu.VMEM((N_REDUCE, rows, lanes // 2), BF16),
            pltpu.VMEM((2, BLK, depth), BF16),
            pltpu.VMEM((2, 4, BLK, depth), BF16),
            pltpu.VMEM((2, 4, BLK, depth), BF16),
            pltpu.VMEM((2, 2, BLK // 2, depth), BF16),
            pltpu.VMEM((4, depth, cols), BF16),
            pltpu.VMEM((2, BLK, cols), F32),
            pltpu.VMEM((2, NCH, BLK, cols // NCH), BF16),
            pltpu.VMEM((2, NCH, 2, BLK // 2, cols // NCH), BF16),
            sem((64,)), sem((N_REDUCE,)), sem((N_REDUCE,)), sem((8,)), sem((8,)), sem((5,)),
            sem((8,)), sem((8,)), sem((12,)), sem((12,)),
            sem((10 * NCH,)), sem((10 * NCH,)), sem((8 * NCH,)), sem((8 * NCH,)), sem((2 * NCH,)),
        ],
        compiler_params=pltpu.CompilerParams(
            collective_id=1, has_side_effects=True, vmem_limit_bytes=VMEM),
        name="finish",
    )(part, wo, won)


def prepare_kernel(cb_local, slot_ref, pattern_ref, q_ref, tab_ref, out_ref):
    core = position()[2]
    for chip in range(16):
        for k in range(2):
            tab_ref[chip, 0, k * 16 + 15] = 0

    def one(e, carry):
        for k in range(2):
            slot = slot_ref[pattern_ref[k, e]]
            owner = slot // cb_local
            chip = owner // 2
            here = jnp.where(owner % 2 == core, 0, cb_local) + slot % cb_local
            n = tab_ref[chip, 0, k * 16 + 15]
            tab_ref[chip, 0, k * 16 + n] = here
            tab_ref[chip, 0, k * 16 + 15] = n + 1
        return carry

    lax.fori_loop(0, pattern_ref.shape[1], one, 0, unroll=True)
    for color in range(2):
        for g in range(q_ref.shape[1] // HD):
            out_ref[color, :, g * BLK:(g + 1) * BLK] = q_ref[color * BLK:(color + 1) * BLK, g * HD:(g + 1) * HD].T


def prepare(block_slot, pattern, queries, cb_local):
    return pl.pallas_call(
        functools.partial(prepare_kernel, cb_local),
        out_shape=(jax.ShapeDtypeStruct((16, 1, 128), jnp.int32),
                   jax.ShapeDtypeStruct((2, HD, queries.shape[1]), BF16)),
        in_specs=[pl.BlockSpec(memory_space=pltpu.SMEM)] * 2 + [pl.BlockSpec(memory_space=pltpu.VMEM)],
        out_specs=(pl.BlockSpec(memory_space=pltpu.SMEM), pl.BlockSpec(memory_space=pltpu.VMEM)),
        compiler_params=pltpu.CompilerParams(vmem_limit_bytes=VMEM),
        name="prepare",
    )(block_slot, pattern, queries)


def body(queries, span_k, span_v, cache_k, cache_v, block_slot, pattern, wo):
    tab, q = prepare(block_slot, pattern, queries, cache_k.shape[0])
    q_all, pk, pv, prev, tab_all, won = gather_queries(q, cache_k, cache_v, span_k, span_v, tab, wo)
    part = attend(tab_all, q_all, cache_k, cache_v, pk, pv, span_k, span_v, prev)
    return finish(part, wo, won)


def solution(mesh):
    return jax.shard_map(
        body,
        mesh=mesh,
        in_specs=(
            P(("fsdp", "seq"), "head"),
            P(("fsdp", "seq"), "head"),
            P(("fsdp", "seq"), "head"),
            P(("fsdp", "seq"), None, "head"),
            P(("fsdp", "seq"), None, "head"),
            P(),
            P(("fsdp", "seq"), None),
            P("head", "fsdp"),
        ),
        out_specs=P(("fsdp", "seq"), None),
        check_vma=False,
    )
```
